32 devices in a mesh: rep: 4 (over y, x), fsdp: 8 (over z, core).
Axes of the slice: x: 2, y: 2, z: 4, core: 2. Of those that a mesh axis runs over, the one named last changes fastest.
Arguments:
- tokens: bfloat16 [4, 1024, 2048], P('rep', 'fsdp'), may hold values from -6 to 6
- lengths: int32 [4], P('rep'), may hold values from 1024 to 1024, as said below
- cotangent: bfloat16 [4, 1024, 2048], P('rep', 'fsdp'), may hold values from -6 to 6
- w_qkv: bfloat16 [2048, 6144], P('fsdp'), may hold values from -0.125 to 0.125
- w_out: bfloat16 [2048, 2048], P('fsdp'), may hold values from -2 to 2
- w_in: bfloat16 [2048, 16384], P('fsdp'), may hold values from -0.125 to 0.125
- w_down: bfloat16 [8192, 2048], P('fsdp'), may hold values from -0.0625 to 0.0625
Outputs:
- output: bfloat16 [4, 1024, 2048], P('rep', 'fsdp')
- grad_tokens: bfloat16 [4, 1024, 2048], P('rep', 'fsdp')
- grad_qkv: float32 [2048, 6144], P('fsdp')
- grad_out: float32 [2048, 2048], P('fsdp')
- grad_in: float32 [2048, 16384], P('fsdp')
- grad_down: float32 [8192, 2048], P('fsdp')
The draws below stay inside these ranges and needn't reach their ends.
Inputs may be any that keep to these rules, and one draw needn't show every extreme that they name: Slot s holds one sequence in its first lengths[s] rows. In every draw one slot is full (1024) and another holds exactly 1024.
All inputs are finite; a program needn't handle non-finite values.
Results may differ from the reference program's by a relative error of at most 0.018.
Values may be sent and summed in bfloat16 or wider, within the bound.
A program may use at most 384 MiB of HBM per device.

```python
import jax
import jax.numpy as jnp
from jax import lax

D = 2048
HEADS = 16
HEAD_DIM = 128
FF = 8192
SLOTS = 4
SLOT = 1024
LEN_LO = 1024


def draw_lengths(key, part):
    first, second, third = jax.random.split(jax.random.fold_in(key, 17), 3)
    drawn = jax.random.randint(first, (SLOTS,), LEN_LO, SLOT + 1, dtype=jnp.int32)
    full_slot = jax.random.randint(second, (), 0, SLOTS, dtype=jnp.int32)
    short_slot = (full_slot + jax.random.randint(third, (), 1, SLOTS, dtype=jnp.int32)) % SLOTS
    index = jnp.arange(SLOTS, dtype=jnp.int32)
    drawn = jnp.where(index == full_slot, SLOT, drawn)
    drawn = jnp.where(index == short_slot, LEN_LO, drawn)
    return drawn.astype(jnp.int32)


def block_scale(own_key, shape, cuts, low, high):
    loudness = 1.0
    for axis_at, shards_of in cuts:
        heights = jax.random.uniform(jax.random.fold_in(jax.random.fold_in(own_key, 6), axis_at), (shards_of,), jnp.float32, low / len(cuts), high / len(cuts))
        loudness = loudness * jnp.repeat(jnp.exp(heights), shape[axis_at] // shards_of).reshape((-1,) + (1,) * (len(shape) - 1 - axis_at))
    return loudness


def gaussian(stream_key, shape, deviation, reach, pieces=(), kind=jnp.bfloat16):
    values = deviation * jax.random.normal(stream_key, shape, jnp.float32)
    if pieces:
        values = values * block_scale(stream_key, shape, pieces, -0.22, 0.18)
    return jnp.clip(values, -reach, reach).astype(kind)


def setup_inputs(seed: int = 0) -> dict:
    key_of = jax.random.split(jax.random.key(seed), 8)
    return {
        "tokens": gaussian(key_of[0], (SLOTS, SLOT, D), 1.0, 6.0, ((0, 4), (1, 8))),
        "lengths": draw_lengths(jax.random.fold_in(key_of[7], 71), 0),
        "cotangent": gaussian(key_of[2], (SLOTS, SLOT, D), 1.0, 6.0, ((0, 4), (1, 8))),
        "w_qkv": gaussian(key_of[3], (D, 3 * D), D ** -0.5, 0.125, ((0, 8),)),
        "w_out": gaussian(key_of[4], (D, D), (max(1, 4 * D // SLOT)) ** -0.5, 2.0, ((0, 8),)),
        "w_in": gaussian(key_of[5], (D, 2 * FF), D ** -0.5, 0.125, ((0, 8),)),
        "w_down": gaussian(key_of[6], (FF, D), FF ** -0.5, 0.0625, ((0, 8),)),
    }


@jax.custom_vjp
def low(v):
    return lax.optimization_barrier(v.astype(jnp.bfloat16)).astype(jnp.float32)

@jax.custom_vjp
def low_back(v):
    return v

def low_keep(v):
    return (low(v), None)

def low_pass(kept, grad):
    return (grad,)

def back_keep(v):
    return (v, None)

def back_low(kept, grad):
    return (low(grad),)
low.defvjp(low_keep, low_pass)
low_back.defvjp(back_keep, back_low)
eps = 1e-05
neg_big = -1e+30
highest = lax.Precision.HIGHEST

def normalize(rows):
    centred = rows - lax.optimization_barrier(jnp.mean(rows, axis=-1, keepdims=True))
    return centred * lax.rsqrt(lax.optimization_barrier(jnp.mean(centred * centred, axis=-1, keepdims=True)) + eps)

def rotary_tables(positions, head_dim):
    half = head_dim // 2
    freqs = 10000.0 ** (-jnp.arange(half, dtype=jnp.float32) * 2.0 / head_dim)
    angles = positions.astype(jnp.float32)[:, None] * freqs[None, :]
    return (jnp.cos(angles), jnp.sin(angles))

def rotate(values, cosine, sine):
    half = values.shape[-1] // 2
    first = values[..., :half]
    second = values[..., half:]
    cosine = cosine[:, None, :]
    sine = sine[:, None, :]
    return jnp.concatenate([first * cosine - second * sine, second * cosine + first * sine], axis=-1)

def layer_forward(rows_in, w_qkv, w_out, w_in, w_down, length):
    slot_len = rows_in.shape[0]
    width = rows_in.shape[1]
    positions = jnp.arange(slot_len, dtype=jnp.int32)
    valid = (positions < length).astype(jnp.float32)[:, None]
    cosine, sine = rotary_tables(positions, HEAD_DIM)
    normed1 = low(normalize(rows_in))
    qkv = low_back(jnp.dot(normed1, w_qkv, precision=highest))
    query = low(rotate(qkv[:, :width].reshape(slot_len, HEADS, HEAD_DIM), cosine, sine))
    keys = low(rotate(qkv[:, width:2 * width].reshape(slot_len, HEADS, HEAD_DIM), cosine, sine))
    values = low(qkv[:, 2 * width:].reshape(slot_len, HEADS, HEAD_DIM))
    block = min(512, slot_len)
    scale = HEAD_DIM ** (-0.5)

    def attend(start):
        q_block = lax.dynamic_slice_in_dim(query, start, block, 0)
        q_pos = start + jnp.arange(block, dtype=jnp.int32)
        raw = jnp.einsum('qhd,khd->hqk', q_block, keys, precision=highest) * scale
        allowed = (positions[None, :] <= q_pos[:, None]) & (positions[None, :] < length)
        scores = jnp.where(allowed[None], low_back(raw), neg_big)
        top = lax.optimization_barrier(jnp.max(scores, axis=-1, keepdims=True))
        total = top + jnp.log(lax.optimization_barrier(jnp.sum(jnp.exp(scores - top), axis=-1, keepdims=True)))
        probs = low(jnp.exp(scores - total))
        return jnp.einsum('hqk,khd->qhd', probs, values, precision=highest)
    starts = jnp.arange(slot_len // block, dtype=jnp.int32) * block
    attended = lax.map(jax.checkpoint(attend), starts).reshape(slot_len, width)
    attended = low_back(low(attended))
    hidden_in = rows_in + low_back(jnp.dot(attended, w_out, precision=highest))
    normed2 = low(normalize(hidden_in))
    gate_up = low_back(jnp.dot(normed2, w_in, precision=highest))
    units = gate_up.shape[1] // 2
    activ = low(jax.nn.silu(gate_up[:, :units]) * gate_up[:, units:])
    branch = low_back(jnp.dot(activ, w_down, precision=highest))
    return valid * (hidden_in + branch)

def reference(tokens, lengths, cotangent, w_qkv, w_out, w_in, w_down):
    weight_list = (w_qkv.astype(jnp.float32), w_out.astype(jnp.float32), w_in.astype(jnp.float32), w_down.astype(jnp.float32))

    def per_slot(sums, inputs):
        slot_rows, slot_grad, length = inputs

        def forward(rows_in, mat_qkv, mat_out, mat_in, mat_down):
            return layer_forward(rows_in, mat_qkv, mat_out, mat_in, mat_down, length)
        result, pullback = jax.vjp(forward, slot_rows.astype(jnp.float32), *weight_list)
        grads = pullback(slot_grad.astype(jnp.float32))
        new_sums = tuple((acc + part for acc, part in zip(sums, grads[1:])))
        return (new_sums, (result.astype(jnp.bfloat16), grads[0].astype(jnp.bfloat16)))
    zero_sums = tuple((jnp.zeros(mat.shape, jnp.float32) for mat in weight_list))
    sums, (outputs, input_grads) = lax.scan(per_slot, zero_sums, (tokens, cotangent, lengths))
    return (outputs, input_grads, sums[0], sums[1], sums[2], sums[3])
```

```python
import jax
import jax.numpy as jnp
from jax import lax
from jax.sharding import PartitionSpec as P

HEAD_DIM = 128

eps = 1e-05
neg_big = -1e30
F32 = jnp.float32
BF16 = jnp.bfloat16


def normalize(rows):
    centred = rows - jnp.mean(rows, axis=-1, keepdims=True)
    inv_std = lax.rsqrt(jnp.mean(centred * centred, axis=-1, keepdims=True) + eps)
    return (centred * inv_std, inv_std)


def norm_back(normed, inv_std, grad):
    return inv_std * (
        grad
        - jnp.mean(grad, axis=-1, keepdims=True)
        - normed * jnp.mean(grad * normed, axis=-1, keepdims=True)
    )


def rotary_tables(positions, head_dim):
    half = head_dim // 2
    freqs = 10000.0 ** (-jnp.arange(half, dtype=F32) * 2.0 / head_dim)
    angles = positions.astype(F32)[:, None] * freqs[None, :]
    return (jnp.cos(angles), jnp.sin(angles))


def rotate(values, cosine, sine):
    half = values.shape[-1] // 2
    first = values[..., :half]
    second = values[..., half:]
    cosine = cosine[:, None, :]
    sine = sine[:, None, :]
    return jnp.concatenate(
        [first * cosine - second * sine, second * cosine + first * sine], axis=-1
    )


def rotate_back(grads, cosine, sine):
    return rotate(grads, cosine, -sine)


def times_transpose(left, weight):
    return lax.dot_general(
        left, weight, (((1,), (1,)), ((), ())), preferred_element_type=F32
    )


def over_rows(left, right):
    return lax.dot_general(
        left, right, (((0,), (0,)), ((), ())), preferred_element_type=F32
    )


def dot(left, right):
    return jnp.dot(left, right, preferred_element_type=F32)


def gather_rows(block):
    return lax.all_gather(block, "fsdp", axis=0, tiled=True)


def scatter_rows(partial):
    return lax.psum_scatter(
        partial.astype(BF16), "fsdp", scatter_dimension=0, tiled=True
    ).astype(F32)


def to_columns(weight, groups):
    n = lax.axis_size("fsdp")
    reps = lax.axis_size("rep")
    depth, width = weight.shape
    part = depth // reps
    own = lax.dynamic_slice_in_dim(weight, lax.axis_index("rep") * part, part, 0)
    own = own.reshape(part, groups, n, width // (groups * n))
    sent = lax.all_to_all(own, "fsdp", split_axis=2, concat_axis=0, tiled=True)
    sent = sent.reshape(n, part, width // n)
    full = lax.all_gather(sent, "rep", axis=1, tiled=True)
    return full.reshape(n * depth, width // n)


def to_rows(grad, groups):
    n = lax.axis_size("fsdp")
    reps = lax.axis_size("rep")
    depth, width = grad.shape
    part = depth // (n * reps)
    split = grad.astype(BF16).reshape(n, reps, part, width)
    summed = lax.psum_scatter(split, "rep", scatter_dimension=1, tiled=True)
    summed = summed.reshape(n, part, groups, width // groups)
    moved = lax.all_to_all(summed, "fsdp", split_axis=0, concat_axis=0, tiled=True)
    moved = moved.transpose(1, 2, 0, 3).reshape(part, n * width)
    return lax.all_gather(moved, "rep", axis=0, tiled=True).astype(F32)


def on_device(tokens, lengths, cotangent, w_qkv, w_out, w_in, w_down):
    rows = tokens.shape[1]
    width = tokens.shape[2]
    n = lax.axis_size("fsdp")
    slot_len = rows * n
    head_dim = HEAD_DIM
    own_width = width // n
    heads = own_width // head_dim
    scale = head_dim ** (-0.5)
    length = lengths[0]
    own_positions = lax.axis_index("fsdp") * rows + jnp.arange(rows, dtype=jnp.int32)
    valid = (own_positions < length).astype(F32)[:, None]
    positions = jnp.arange(slot_len, dtype=jnp.int32)
    cosine, sine = rotary_tables(positions, head_dim)

    x_rows = tokens[0].astype(F32)
    normed1, inv1 = normalize(x_rows)
    n1_full = gather_rows(normed1.astype(BF16))
    qkv_cols = to_columns(w_qkv, 3)
    in_cols = to_columns(w_in, 2)
    dy_rows = valid * cotangent[0].astype(F32)
    dy_full = gather_rows(dy_rows.astype(BF16))

    qkv = dot(n1_full, qkv_cols)
    query = rotate(
        qkv[:, :own_width].reshape(slot_len, heads, head_dim), cosine, sine
    ).astype(BF16)
    keys = rotate(
        qkv[:, own_width : 2 * own_width].reshape(slot_len, heads, head_dim), cosine, sine
    ).astype(BF16)
    values = qkv[:, 2 * own_width :].reshape(slot_len, heads, head_dim).astype(BF16)
    allowed = (positions[None, :] <= positions[:, None]) & (positions[None, :] < length)

    raw = jnp.einsum("qhd,khd->hqk", query, keys, preferred_element_type=F32) * scale
    scores = jnp.where(allowed[None], raw, neg_big)
    top = jnp.max(scores, axis=-1, keepdims=True)
    log_total = top + jnp.log(jnp.sum(jnp.exp(scores - top), axis=-1, keepdims=True))
    probs = jnp.exp(scores - log_total)
    probs_low = probs.astype(BF16)
    attended = jnp.einsum("hqk,khd->qhd", probs_low, values, preferred_element_type=F32)
    att_low = attended.reshape(slot_len, own_width).astype(BF16)

    hidden_in = x_rows + scatter_rows(dot(att_low, w_out))
    normed2, inv2 = normalize(hidden_in)
    n2_full = gather_rows(normed2.astype(BF16))
    gate_up = dot(n2_full, in_cols)
    units = gate_up.shape[1] // 2
    gate = gate_up[:, :units]
    upper = gate_up[:, units:]
    sigma = jax.nn.sigmoid(gate)
    silu_gate = gate * sigma
    act_low = (silu_gate * upper).astype(BF16)
    d_hidden = times_transpose(dy_full, w_down)
    d_gate = d_hidden * upper * sigma * (1.0 + gate * (1.0 - sigma))
    d_up = d_hidden * silu_gate
    dgu_low = jnp.concatenate([d_gate, d_up], axis=1).astype(BF16)
    d_norm2 = scatter_rows(times_transpose(dgu_low, in_cols))
    branch = scatter_rows(dot(act_low, w_down))
    output = (valid * (hidden_in + branch)).astype(BF16)
    d_resid = dy_rows + norm_back(normed2, inv2, d_norm2)
    dres_full = gather_rows(d_resid.astype(BF16))

    grad_down = over_rows(act_low, dy_full)
    grad_in = over_rows(n2_full, dgu_low)
    grad_out = over_rows(att_low, dres_full)

    datt = times_transpose(dres_full, w_out)
    datt_low = datt.astype(BF16).reshape(slot_len, heads, head_dim)
    delta = jnp.sum(datt_low.astype(F32) * attended, axis=-1).T
    d_probs = jnp.einsum("qhd,khd->hqk", datt_low, values, preferred_element_type=F32)
    d_scores = (probs * (d_probs - delta[..., None])).astype(BF16)
    dq = jnp.einsum("hqk,khd->qhd", d_scores, keys, preferred_element_type=F32) * scale
    dk = jnp.einsum("hqk,qhd->khd", d_scores, query, preferred_element_type=F32) * scale
    dv = jnp.einsum("hqk,qhd->khd", probs_low, datt_low, preferred_element_type=F32)
    dqkv_low = jnp.concatenate(
        [
            rotate_back(dq, cosine, sine).reshape(slot_len, own_width),
            rotate_back(dk, cosine, sine).reshape(slot_len, own_width),
            dv.reshape(slot_len, own_width),
        ],
        axis=1,
    ).astype(BF16)
    d_norm1 = scatter_rows(times_transpose(dqkv_low, qkv_cols))
    grad_tokens = (d_resid + norm_back(normed1, inv1, d_norm1)).astype(BF16)
    grad_qkv = over_rows(n1_full, dqkv_low)

    return (
        output[None],
        grad_tokens[None],
        to_rows(grad_qkv, 3),
        lax.psum(grad_out.astype(BF16), "rep").astype(F32),
        to_rows(grad_in, 2),
        lax.psum(grad_down.astype(BF16), "rep").astype(F32),
    )


def solution(mesh):
    in_specs = (
        P("rep", "fsdp", None),
        P("rep"),
        P("rep", "fsdp", None),
        P("fsdp", None),
        P("fsdp", None),
        P("fsdp", None),
        P("fsdp", None),
    )
    out_specs = (
        P("rep", "fsdp", None),
        P("rep", "fsdp", None),
        P("fsdp", None),
        P("fsdp", None),
        P("fsdp", None),
        P("fsdp", None),
    )
    return jax.shard_map(
        on_device, mesh=mesh, in_specs=in_specs, out_specs=out_specs, check_vma=False
    )
```

```python
import functools

import jax
import jax.numpy as jnp
from jax import lax
from jax.experimental import pallas as pl
from jax.experimental.pallas import tpu as pltpu
from jax.sharding import PartitionSpec as P

HEAD_DIM = 128

eps = 1e-05
neg_big = -1e30
F32 = jnp.float32
BF16 = jnp.bfloat16


def normalize(rows):
    centred = rows - jnp.mean(rows, axis=-1, keepdims=True)
    inv_std = lax.rsqrt(jnp.mean(centred * centred, axis=-1, keepdims=True) + eps)
    return (centred * inv_std, inv_std)


def norm_back(normed, inv_std, grad):
    return inv_std * (
        grad
        - jnp.mean(grad, axis=-1, keepdims=True)
        - normed * jnp.mean(grad * normed, axis=-1, keepdims=True)
    )


def rotary_tables(positions, head_dim):
    half = head_dim // 2
    freqs = 10000.0 ** (-jnp.arange(half, dtype=F32) * 2.0 / head_dim)
    angles = positions.astype(F32)[:, None] * freqs[None, :]
    return (jnp.cos(angles), jnp.sin(angles))


def rotate(values, cosine, sine):
    half = values.shape[-1] // 2
    first = values[..., :half]
    second = values[..., half:]
    cosine = cosine[:, None, :]
    sine = sine[:, None, :]
    return jnp.concatenate(
        [first * cosine - second * sine, second * cosine + first * sine], axis=-1
    )


def rotate_back(grads, cosine, sine):
    return rotate(grads, cosine, -sine)


def times_transpose(left, weight):
    return lax.dot_general(
        left, weight, (((1,), (1,)), ((), ())), preferred_element_type=F32
    )


def over_rows(left, right):
    return lax.dot_general(
        left, right, (((0,), (0,)), ((), ())), preferred_element_type=F32
    )


def dot(left, right):
    return jnp.dot(left, right, preferred_element_type=F32)


MESH = pl.DeviceIdType.MESH
LIMIT = 60 * 1024 * 1024


class Kit:
    def __init__(self, sems, sizes):
        self.sems = sems
        self.used = 0
        self.n, self.reps = sizes
        self.chips = self.n // 2
        self.me = lax.axis_index("fsdp")
        self.rep = lax.axis_index("rep")
        self.chip = self.me // 2
        self.core = self.me % 2
        self.bits = self.reps.bit_length() - 1

    def sem(self):
        self.used += 1
        return self.sems.at[self.used - 1]

    def barrier(self, fsdp=True, rep=True):
        wall = pltpu.get_barrier_semaphore()
        count = 0
        if fsdp:
            for k in range(1, self.n):
                pl.semaphore_signal(wall, inc=1, device_id={"fsdp": self.me ^ k}, device_id_type=MESH)
                count += 1
        if rep:
            for b in range(self.bits):
                pl.semaphore_signal(wall, inc=1, device_id={"rep": self.rep ^ (1 << b)}, device_id_type=MESH)
                count += 1
        pl.semaphore_wait(wall, count)

    def copy(self, src, dst, sems, fsdp=None, rep=None):
        where = {"fsdp": fsdp} if rep is None else {"rep": rep}
        return pltpu.make_async_remote_copy(
            src_ref=src, dst_ref=dst, send_sem=sems[0], recv_sem=sems[1],
            device_id=where, device_id_type=MESH,
        )

    def pair(self):
        return (self.sem(), self.sem())

    def bit(self, index):
        return (self.rep >> index) & 1

    def gather_line(self, src, dst, rows):
        C, z, c = self.chips, self.chip, self.core

        def blk(chip, core):
            return dst.at[pl.ds(pl.multiple_of((2 * chip + core) * rows, rows), rows)]

        local = pltpu.make_async_copy(src, blk(z, c), self.sem())
        local.start()
        partner = self.me ^ 1
        own_sems = self.pair()
        own_pair = self.copy(src, blk(z, c), own_sems, fsdp=partner)
        other_own = blk(z, 1 - c)
        ways = []
        for sign in (1, -1):
            sends = [self.pair() for _ in range(C - 1)]
            forwards = [self.pair() for _ in range(C - 1)]
            ways.append((sign, sends, forwards))

        def inside(chip):
            return (chip >= 0) & (chip < C)

        def hop(sign, sends, k):
            shard = z - sign * k
            ref = src if k == 0 else blk(shard, c)
            return self.copy(ref, blk(shard, c), sends[k], fsdp=2 * (z + sign) + c)

        def across(sign, forwards, k):
            shard = z - sign * k
            return self.copy(blk(shard, c), blk(shard, c), forwards[k - 1], fsdp=partner)

        for sign, sends, forwards in ways:
            @pl.when(inside(z + sign))
            def _():
                hop(sign, sends, 0).start()
        own_pair.start()
        for k in range(1, C):
            yield
            for sign, sends, forwards in ways:
                @pl.when(inside(z - sign * k))
                def _():
                    shard = z - sign * k
                    self.copy(blk(shard, c), blk(shard, c), sends[k - 1], fsdp=partner).wait_recv()
                    if k < C - 1:
                        @pl.when(inside(z + sign))
                        def _():
                            hop(sign, sends, k).start()
                    across(sign, forwards, k).start()
        yield
        local.wait()
        own_pair.wait_send()
        self.copy(src, other_own, own_sems, fsdp=partner).wait_recv()
        for k in range(0, C - 1):
            for sign, sends, forwards in ways:
                @pl.when(inside(z + sign) & inside(z - sign * k))
                def _():
                    hop(sign, sends, k).wait_send()
        for k in range(1, C):
            for sign, sends, forwards in ways:
                @pl.when(inside(z - sign * k))
                def _():
                    across(sign, forwards, k).wait_send()
                    shard = z - sign * k
                    self.copy(blk(shard, c), blk(shard, 1 - c), forwards[k - 1], fsdp=partner).wait_recv()

    def scatter_line(self, partial, total, rows, near, mine, left, right):
        C, z, c = self.chips, self.chip, self.core
        partner = self.me ^ 1

        def blk(chip, core):
            return partial.at[pl.ds(pl.multiple_of((2 * chip + core) * rows, rows), rows)]

        order = []
        for j in range(C):
            for d in (C - 1 - j, j):
                if d not in order:
                    order.append(d)
        near_sems = [self.pair() for _ in range(C)]
        right_sems = [self.pair() for _ in range(C)]
        left_sems = [self.pair() for _ in range(C)]

        def swap(d):
            return self.copy(blk(d, 1 - c), near.at[d], near_sems[d], fsdp=partner)

        def to_right(d):
            return self.copy(mine.at[d], right.at[d], right_sems[d], fsdp=2 * (z + 1) + c)

        def to_left(d):
            return self.copy(mine.at[d], left.at[d], left_sems[d], fsdp=2 * (z - 1) + c)

        for d in order:
            swap(d).start()
        yield
        for d in order:
            swap(d).wait_recv()
            add_into(mine.at[d], blk(d, c), near.at[d])
            @pl.when((z == 0) & (d > 0))
            def _():
                to_right(d).start()
            @pl.when((z == C - 1) & (d < C - 1))
            def _():
                to_left(d).start()
        for j in range(C - 1):
            yield
            d = C - 1 - j
            @pl.when((z > 0) & (z < d))
            def _():
                to_right(d).wait_recv()
                add_into(mine.at[d], mine.at[d], right.at[d])
                to_right(d).start()
            e = j
            @pl.when((z < C - 1) & (z > e))
            def _():
                to_left(e).wait_recv()
                add_into(mine.at[e], mine.at[e], left.at[e])
                to_left(e).start()
        yield
        keep(total, mine.at[z])
        for d in range(C):
            if d > 0:
                @pl.when(z == d)
                def _():
                    to_right(d).wait_recv()
                    accumulate(total, right.at[d])
            if d < C - 1:
                @pl.when(z == d)
                def _():
                    to_left(d).wait_recv()
                    accumulate(total, left.at[d])
        yield
        for d in range(C):
            swap(d).wait_send()
            @pl.when(z < d)
            def _():
                to_right(d).wait_send()
            @pl.when(z > d)
            def _():
                to_left(d).wait_send()

    def exchange(self, pieces, arrivals):
        sems = {}
        for k in range(1, self.n):
            for i, (src, dst) in enumerate(pieces(self.me ^ k)):
                sems[k, i] = self.pair()
                self.copy(src, dst, sems[k, i], fsdp=self.me ^ k).start()
        yield
        for k in range(1, self.n):
            for i, (src, dst) in enumerate(arrivals(self.me ^ k)):
                self.copy(src, dst, sems[k, i], fsdp=self.me ^ k).wait_recv()
        yield
        for k in range(1, self.n):
            for i, (src, dst) in enumerate(pieces(self.me ^ k)):
                self.copy(src, dst, sems[k, i], fsdp=self.me ^ k).wait_send()

    def gather_rep(self, blk):
        sent = []
        waits = {0: [], 1: []}
        for i in range(self.bits):
            for half in (0, 1):
                b = i if half == 0 else self.bits - 1 - i
                before = [j if half == 0 else self.bits - 1 - j for j in range(i)]
                for cp in waits[half]:
                    cp.wait_recv()
                waits[half] = []
                peer = self.rep ^ (1 << b)
                for mask in range(1 << i):
                    flip = sum(((mask >> j) & 1) << before[j] for j in range(i))
                    r = self.rep ^ flip
                    sems = self.pair()
                    cp = self.copy(blk(half, r), blk(half, r), sems, rep=peer)
                    cp.start()
                    sent.append(cp)
                    waits[half].append(self.copy(blk(half, r), blk(half, r ^ (1 << b)), sems, rep=peer))
            yield
        for half in (0, 1):
            for cp in waits[half]:
                cp.wait_recv()
        yield
        for cp in sent:
            cp.wait_send()

    def scatter_rep(self, blk, land, done):
        sent = []
        waits = {0: [], 1: []}
        nb = self.bits

        def start(half, i):
            order = list(range(nb)) if half == 0 else list(range(nb))[::-1]
            peer = self.rep ^ (1 << order[i])
            rest = order[i + 1:]
            todo = []
            for combo in range(1 << len(rest)):
                def source(own, combo=combo):
                    value = self.bit(order[i]) if own else 1 - self.bit(order[i])
                    if i == 0:
                        r = value << order[0]
                        r = r + sum(((combo >> j) & 1) << rest[j] for j in range(len(rest)))
                        return blk(half, r)
                    return land(half, i - 1, value + 2 * combo)
                sems = self.pair()
                cp = self.copy(source(False), land(half, i, combo), sems, rep=peer)
                cp.start()
                sent.append(cp)
                todo.append((cp, land(half, i, combo), source(True)))
            return todo

        for i in range(nb):
            for half in (0, 1):
                if i == 0:
                    waits[half] = start(half, 0)
            if i == 0:
                yield
            for half in (0, 1):
                for cp, ref, own in waits[half]:
                    cp.wait_recv()
                    if i < nb - 1:
                        add_into(ref, ref, own)
                    else:
                        done(half, ref, own)
                if i < nb - 1:
                    waits[half] = start(half, i + 1)
            yield
        for cp in sent:
            cp.wait_send()


def each(ref, body):
    lead = ref.shape[:-2]
    count = ref.shape[-2] // 16
    total = count
    for size in lead:
        total *= size

    def step(t, carry):
        rows = pl.ds(pl.multiple_of((t % count) * 16, 16), 16)
        rest = t // count
        index = []
        for size in reversed(lead):
            index.append(rest % size)
            rest = rest // size
        body(tuple(reversed(index)) + (rows,))
        return carry

    lax.fori_loop(0, total, step, 0)


def add_into(dst, a, b):
    def body(at):
        dst[at] = (a[at].astype(F32) + b[at].astype(F32)).astype(dst.dtype)

    each(dst, body)


def keep(dst, a):
    def body(at):
        dst[at] = a[at].astype(dst.dtype)

    each(dst, body)


def accumulate(dst, a):
    def body(at):
        dst[at] = dst[at] + a[at].astype(F32)

    each(dst, body)


def finish(*tasks):
    for task in tasks:
        for _ in task:
            pass


def turns(order):
    for task in order:
        next(task, None)


def cut(width):
    low = width // 256 * 128
    return ((0, low), (low, width - low))


def column_blocks(ref):
    parts = cut(ref.shape[-1])
    lead = len(ref.shape) - 3

    def blk(half, r):
        start, size = parts[half]
        return ref.at[(slice(None),) * lead + (r, slice(None), pl.ds(start, size))]

    return blk


def own_piece(kit, src_of, dst_of, stage, groups, width):
    first, second = kit.sem(), kit.sem()
    loads = [
        pltpu.make_async_copy(src_of(g), stage.at[:, pl.ds(g * width, width)], kit.sem())
        for g in range(groups)
    ]
    for cp in loads:
        cp.start()
    yield
    for cp in loads:
        cp.wait()
    store = pltpu.make_async_copy(stage, dst_of, first)
    store.start()
    yield
    store.wait()


def column_slice(start, size):
    return pl.ds(pl.multiple_of(start, 128), size)


def reshard(kit, weight, cols, stage, groups):
    n, reps, part, total = cols.shape
    width = total // groups
    rows = pl.ds(pl.multiple_of(kit.rep * part, part), part)

    def source(g, d):
        return weight.at[rows, column_slice(g * (width * n) + d * width, width)]

    def pieces(d):
        return [
            (source(g, d), cols.at[kit.me, kit.rep, :, pl.ds(g * width, width)])
            for g in range(groups)
        ]

    def arrivals(d):
        return [
            (source(g, d), cols.at[d, kit.rep, :, pl.ds(g * width, width)])
            for g in range(groups)
        ]

    own = own_piece(
        kit, lambda g: source(g, kit.me), cols.at[kit.me, kit.rep], stage, groups, width
    )
    move = kit.exchange(pieces, arrivals)
    next(move)
    next(own)
    yield
    next(own)
    next(own, None)
    next(move)
    yield
    finish(move)


def unshard(kit, sums, out, groups):
    n, part, total = sums.shape
    width = total // groups

    def target(g, d):
        return out.at[kit.rep, :, column_slice(g * (width * n) + d * width, width)]

    def pieces(d):
        return [(sums.at[d, :, pl.ds(g * width, width)], target(g, kit.me)) for g in range(groups)]

    def arrivals(d):
        return [(sums.at[d, :, pl.ds(g * width, width)], target(g, d)) for g in range(groups)]

    own = [
        pltpu.make_async_copy(src, dst, kit.sem()) for src, dst in pieces(kit.me)
    ]
    for cp in own:
        cp.start()
    move = kit.exchange(pieces, arrivals)
    next(move)
    yield
    for cp in own:
        cp.wait()
    next(move)
    yield
    finish(move)


def call(body, ins, outs, scratch, count, ident, name):
    def spec(space):
        return pl.BlockSpec(memory_space=space)

    return pl.pallas_call(
        body,
        out_shape=[jax.ShapeDtypeStruct(s, d) for s, d, _ in outs],
        in_specs=[spec(space) for _, space in ins],
        out_specs=[spec(space) for _, _, space in outs],
        scratch_shapes=list(scratch) + [pltpu.SemaphoreType.DMA((count,))],
        compiler_params=pltpu.CompilerParams(
            collective_id=ident, has_side_effects=True, vmem_limit_bytes=LIMIT
        ),
        name=name,
    )(*[a for a, _ in ins])


ANY = pl.ANY
VMEM = pltpu.VMEM
SEMS = 200


def begin_kernel(sizes, n1, w_qkv, n1_full, cols, stage, sems):
    kit = Kit(sems, sizes)
    kit.barrier()
    move = reshard(kit, w_qkv, cols, stage, 3)
    next(move)
    rows = kit.gather_line(n1, n1_full, n1.shape[0])
    next(rows)
    next(move)
    spread = kit.gather_rep(column_blocks(cols))
    next(spread)
    finish_in_turn([rows, spread, move])


def finish_in_turn(tasks):
    tasks = list(tasks)
    done = object()
    while tasks:
        tasks = [t for t in tasks if next(t, done) is not done]


def begin(sizes, n1, w_qkv):
    n, reps = sizes
    rows, width = n1.shape
    depth = w_qkv.shape[0]
    part, own = depth // reps, w_qkv.shape[1] // n
    full, cols = call(
        functools.partial(begin_kernel, sizes),
        [(n1, VMEM), (w_qkv, ANY)],
        [((n * rows, width), BF16, ANY), ((n, reps, part, own), BF16, ANY)],
        [VMEM((part, own), BF16)],
        SEMS, 1, "begin",
    )
    return full, cols.reshape(n * depth, own)


def norm_rows(dst, src):
    def body(at):
        h = src[at]
        centred = h - jnp.mean(h, axis=-1, keepdims=True)
        inv = lax.rsqrt(jnp.mean(centred * centred, axis=-1, keepdims=True) + eps)
        dst[at] = (centred * inv).astype(BF16)

    each(dst, body)


def middle_kernel(sizes, partial, x, w_in, hidden, n2_full, cols, near, mine, left, right, n2, stage, sems):
    kit = Kit(sems, sizes)
    kit.barrier()
    total = kit.scatter_line(partial, hidden, x.shape[0], near, mine, left, right)
    next(total)
    move = reshard(kit, w_in, cols, stage, 2)
    next(total)
    next(move)
    for _ in range(kit.chips - 1):
        next(total)
    accumulated = next(total)

    def body(at):
        hidden[at] = hidden[at] + x[at].astype(F32)

    each(hidden, body)
    norm_rows(n2, hidden)
    rows = kit.gather_line(n2, n2_full, n2.shape[0])
    next(rows)
    next(move)
    spread = kit.gather_rep(column_blocks(cols))
    next(spread)
    finish_in_turn([rows, spread, move, total])


def middle(sizes, partial, x, w_in):
    n, reps = sizes
    rows, width = x.shape
    depth = w_in.shape[0]
    part, own = depth // reps, w_in.shape[1] // n
    lands = [VMEM((n // 2, rows, width), BF16) for _ in range(4)]
    hidden, full, cols = call(
        functools.partial(middle_kernel, sizes),
        [(partial, VMEM), (x, VMEM), (w_in, ANY)],
        [
            ((rows, width), F32, VMEM),
            ((n * rows, width), BF16, ANY),
            ((n, reps, part, own), BF16, ANY),
        ],
        lands + [VMEM((rows, width), BF16), VMEM((part, own), BF16)],
        SEMS, 2, "middle",
    )
    return hidden, full, cols.reshape(n * depth, own)


def lands_of(shape, reps):
    lead, (part, width) = shape[:-3], shape[-2:]
    bits = reps.bit_length() - 1
    places = []
    for start, size in cut(width):
        for i in range(bits):
            places.append(VMEM((1 << (bits - 1 - i),) + lead + (part, size), BF16))
    return places


def land_in(places):
    bits = len(places) // 2

    def land(half, i, j):
        return places[half * bits + i].at[j]

    return land


def put_half(out):
    parts = cut(out.shape[-1])

    def done(half, a, b):
        start, size = parts[half]
        add_into(out.at[(slice(None),) * (len(out.shape) - 1) + (pl.ds(start, size),)], a, b)

    return done


def back_kernel(sizes, partial, hidden, dy, g_in, g_down, resid, full, s_in, s_down, near, mine, left, right, low, *rest):
    sems = rest[-1]
    bits = sizes[1].bit_length() - 1
    kit = Kit(sems, sizes)
    kit.barrier()
    total = kit.scatter_line(partial, resid, dy.shape[0], near, mine, left, right)
    next(total)
    t_in = kit.scatter_rep(column_blocks(g_in), land_in(rest[: 2 * bits]), put_half(s_in))
    next(t_in)
    t_down = kit.scatter_rep(column_blocks(g_down), land_in(rest[2 * bits : 4 * bits]), put_half(s_down))
    next(t_down)
    next(total)
    for _ in range(kit.chips - 1):
        next(total)
    next(total)

    def body(at):
        h = hidden[at]
        centred = h - jnp.mean(h, axis=-1, keepdims=True)
        inv = lax.rsqrt(jnp.mean(centred * centred, axis=-1, keepdims=True) + eps)
        d = dy[at].astype(F32) + norm_back(centred * inv, inv, resid[at])
        resid[at] = d
        low[at] = d.astype(BF16)

    each(resid, body)
    rows = kit.gather_line(low, full, low.shape[0])
    next(rows)
    finish_in_turn([t_in, rows, t_down, total])


def back(sizes, partial, hidden, dy, g_in, g_down):
    n, reps = sizes
    rows, width = dy.shape
    g_in = g_in.reshape(n, reps, g_in.shape[0] // (n * reps), g_in.shape[1])
    g_down = g_down.reshape(reps, g_down.shape[0] // reps, g_down.shape[1])
    lands = [VMEM((n // 2, rows, width), BF16) for _ in range(4)]
    return call(
        functools.partial(back_kernel, sizes),
        [(partial, VMEM), (hidden, VMEM), (dy, VMEM), (g_in, VMEM), (g_down, VMEM)],
        [
            ((rows, width), F32, VMEM),
            ((n * rows, width), BF16, ANY),
            ((n,) + g_in.shape[2:], BF16, VMEM),
            (g_down.shape[1:], BF16, VMEM),
        ],
        lands + [VMEM((rows, width), BF16)] + lands_of(g_in.shape, reps) + lands_of(g_down.shape, reps),
        SEMS, 3, "back",
    )


def end_kernel(sizes, partial, s_in, s_down, g_qkv, g_out, total_out, o_in, o_down, o_qkv, o_out, near, mine, left, right, s_qkv, s_out, *rest):
    sems = rest[-1]
    bits = sizes[1].bit_length() - 1
    kit = Kit(sems, sizes)
    kit.barrier()
    total = kit.scatter_line(partial, total_out, total_out.shape[0], near, mine, left, right)
    next(total)
    move_in = unshard(kit, s_in, o_in, 2)
    next(move_in)
    t_qkv = kit.scatter_rep(column_blocks(g_qkv), land_in(rest[: 2 * bits]), put_half(s_qkv))
    next(t_qkv)
    own_down = pltpu.make_async_copy(s_down, o_down.at[kit.rep], kit.sem())
    own_down.start()
    own_down.wait()
    spread_down = kit.gather_rep(column_blocks(o_down))
    next(spread_down)
    next(total)
    for _ in range(bits):
        next(t_qkv)
    move_qkv = unshard(kit, s_qkv, o_qkv, 3)
    next(move_qkv)
    next(total)
    t_out = kit.scatter_rep(column_blocks(g_out), land_in(rest[2 * bits : 4 * bits]), put_half(s_out))
    next(t_out)
    next(spread_down)
    next(total)
    next(move_in)
    spread_in = kit.gather_rep(column_blocks(o_in))
    next(spread_in)
    next(move_qkv)
    spread_qkv = kit.gather_rep(column_blocks(o_qkv))
    next(spread_qkv)
    for _ in range(bits):
        next(t_out)
    own_out = pltpu.make_async_copy(s_out, o_out.at[kit.rep], kit.sem())
    own_out.start()
    own_out.wait()
    spread_out = kit.gather_rep(column_blocks(o_out))
    next(spread_out)
    finish_in_turn([total, spread_in, spread_qkv, spread_out, spread_down, move_in, move_qkv, t_qkv, t_out])


def end(sizes, partial, s_in, s_down, g_qkv, g_out):
    n, reps = sizes
    rows, width = partial.shape[0] // n, partial.shape[1]
    g_qkv = g_qkv.reshape(n, reps, g_qkv.shape[0] // (n * reps), g_qkv.shape[1])
    g_out = g_out.reshape(reps, g_out.shape[0] // reps, g_out.shape[1])
    lands = [VMEM((n // 2, rows, width), BF16) for _ in range(4)]
    total, o_in, o_down, o_qkv, o_out = call(
        functools.partial(end_kernel, sizes),
        [(partial, VMEM), (s_in, VMEM), (s_down, VMEM), (g_qkv, VMEM), (g_out, VMEM)],
        [
            ((rows, width), F32, VMEM),
            ((reps, s_in.shape[1], n * s_in.shape[2]), BF16, ANY),
            ((reps,) + s_down.shape, BF16, ANY),
            ((reps, g_qkv.shape[2], n * g_qkv.shape[3]), BF16, ANY),
            (g_out.shape, BF16, ANY),
        ],
        lands
        + [VMEM((n,) + g_qkv.shape[2:], BF16), VMEM(g_out.shape[1:], BF16)]
        + lands_of(g_qkv.shape, reps)
        + lands_of(g_out.shape, reps),
        SEMS, 4, "end",
    )
    return [total] + [o.reshape(-1, o.shape[-1]).astype(F32) for o in (o_in, o_down, o_qkv, o_out)]


def gather_rows(block):
    return lax.all_gather(block, "fsdp", axis=0, tiled=True)


def scatter_rows(partial):
    return lax.psum_scatter(
        partial.astype(BF16), "fsdp", scatter_dimension=0, tiled=True
    ).astype(F32)


def on_device(tokens, lengths, cotangent, w_qkv, w_out, w_in, w_down):
    rows = tokens.shape[1]
    width = tokens.shape[2]
    n = lax.axis_size("fsdp")
    slot_len = rows * n
    head_dim = HEAD_DIM
    own_width = width // n
    heads = own_width // head_dim
    scale = head_dim ** (-0.5)
    length = lengths[0]
    own_positions = lax.axis_index("fsdp") * rows + jnp.arange(rows, dtype=jnp.int32)
    valid = (own_positions < length).astype(F32)[:, None]
    positions = jnp.arange(slot_len, dtype=jnp.int32)
    cosine, sine = rotary_tables(positions, head_dim)

    sizes = (n, lax.axis_size("rep"))
    x_rows = tokens[0].astype(F32)
    normed1, inv1 = normalize(x_rows)
    n1_full, qkv_cols = begin(sizes, normed1.astype(BF16), w_qkv)
    dy_rows = valid * cotangent[0].astype(F32)
    dy_low = dy_rows.astype(BF16)
    dy_full = gather_rows(dy_low)

    qkv = dot(n1_full, qkv_cols)
    query = rotate(
        qkv[:, :own_width].reshape(slot_len, heads, head_dim), cosine, sine
    ).astype(BF16)
    keys = rotate(
        qkv[:, own_width : 2 * own_width].reshape(slot_len, heads, head_dim), cosine, sine
    ).astype(BF16)
    values = qkv[:, 2 * own_width :].reshape(slot_len, heads, head_dim).astype(BF16)
    allowed = (positions[None, :] <= positions[:, None]) & (positions[None, :] < length)

    raw = jnp.einsum("qhd,khd->hqk", query, keys, preferred_element_type=F32) * scale
    scores = jnp.where(allowed[None], raw, neg_big)
    top = jnp.max(scores, axis=-1, keepdims=True)
    log_total = top + jnp.log(jnp.sum(jnp.exp(scores - top), axis=-1, keepdims=True))
    probs = jnp.exp(scores - log_total)
    probs_low = probs.astype(BF16)
    attended = jnp.einsum("hqk,khd->qhd", probs_low, values, preferred_element_type=F32)
    att_low = attended.reshape(slot_len, own_width).astype(BF16)

    out_partial = dot(att_low, w_out).astype(BF16)
    hidden_in, n2_full, in_cols = middle(sizes, out_partial, tokens[0], w_in)
    gate_up = dot(n2_full, in_cols)
    units = gate_up.shape[1] // 2
    gate = gate_up[:, :units]
    upper = gate_up[:, units:]
    sigma = jax.nn.sigmoid(gate)
    silu_gate = gate * sigma
    act_low = (silu_gate * upper).astype(BF16)
    d_hidden = times_transpose(dy_full, w_down)
    d_gate = d_hidden * upper * sigma * (1.0 + gate * (1.0 - sigma))
    d_up = d_hidden * silu_gate
    dgu_low = jnp.concatenate([d_gate, d_up], axis=1).astype(BF16)
    dn2_partial = times_transpose(dgu_low, in_cols).astype(BF16)
    branch_partial = dot(act_low, w_down)
    grad_down = over_rows(act_low, dy_full).astype(BF16)
    grad_in = over_rows(n2_full, dgu_low).astype(BF16)
    d_resid, dres_full, sum_in, sum_down = back(
        sizes, dn2_partial, hidden_in, dy_low, grad_in, grad_down
    )
    branch = scatter_rows(branch_partial)
    output = (valid * (hidden_in + branch)).astype(BF16)
    grad_out = over_rows(att_low, dres_full).astype(BF16)

    datt = times_transpose(dres_full, w_out)
    datt_low = datt.astype(BF16).reshape(slot_len, heads, head_dim)
    delta = jnp.sum(datt_low.astype(F32) * attended, axis=-1).T
    d_probs = jnp.einsum("qhd,khd->hqk", datt_low, values, preferred_element_type=F32)
    d_scores = (probs * (d_probs - delta[..., None])).astype(BF16)
    dq = jnp.einsum("hqk,khd->qhd", d_scores, keys, preferred_element_type=F32) * scale
    dk = jnp.einsum("hqk,qhd->khd", d_scores, query, preferred_element_type=F32) * scale
    dv = jnp.einsum("hqk,qhd->khd", probs_low, datt_low, preferred_element_type=F32)
    dqkv_low = jnp.concatenate(
        [
            rotate_back(dq, cosine, sine).reshape(slot_len, own_width),
            rotate_back(dk, cosine, sine).reshape(slot_len, own_width),
            dv.reshape(slot_len, own_width),
        ],
        axis=1,
    ).astype(BF16)
    dn1_partial = times_transpose(dqkv_low, qkv_cols).astype(BF16)
    grad_qkv = over_rows(n1_full, dqkv_low).astype(BF16)
    d_norm1, all_in, all_down, all_qkv, all_out = end(
        sizes, dn1_partial, sum_in, sum_down, grad_qkv, grad_out
    )
    grad_tokens = (d_resid + norm_back(normed1, inv1, d_norm1)).astype(BF16)
    return (output[None], grad_tokens[None], all_qkv, all_out, all_in, all_down)


def solution(mesh):
    in_specs = (
        P("rep", "fsdp", None),
        P("rep"),
        P("rep", "fsdp", None),
        P("fsdp", None),
        P("fsdp", None),
        P("fsdp", None),
        P("fsdp", None),
    )
    out_specs = (
        P("rep", "fsdp", None),
        P("rep", "fsdp", None),
        P("fsdp", None),
        P("fsdp", None),
        P("fsdp", None),
        P("fsdp", None),
    )
    return jax.shard_map(
        on_device, mesh=mesh, in_specs=in_specs, out_specs=out_specs, check_vma=False
    )
```

```python
import functools

import jax
import jax.numpy as jnp
from jax import lax
from jax.experimental import pallas as pl
from jax.experimental.pallas import tpu as pltpu
from jax.sharding import PartitionSpec as P

HEAD_DIM = 128

eps = 1e-05
neg_big = -1e30
F32 = jnp.float32
BF16 = jnp.bfloat16


def normalize(rows):
    centred = rows - jnp.mean(rows, axis=-1, keepdims=True)
    inv_std = lax.rsqrt(jnp.mean(centred * centred, axis=-1, keepdims=True) + eps)
    return (centred * inv_std, inv_std)


def norm_back(normed, inv_std, grad):
    return inv_std * (
        grad
        - jnp.mean(grad, axis=-1, keepdims=True)
        - normed * jnp.mean(grad * normed, axis=-1, keepdims=True)
    )


def rotary_tables(positions, head_dim):
    half = head_dim // 2
    freqs = 10000.0 ** (-jnp.arange(half, dtype=F32) * 2.0 / head_dim)
    angles = positions.astype(F32)[:, None] * freqs[None, :]
    return (jnp.cos(angles), jnp.sin(angles))


def rotate(values, cosine, sine):
    half = values.shape[-1] // 2
    first = values[..., :half]
    second = values[..., half:]
    cosine = cosine[:, None, :]
    sine = sine[:, None, :]
    return jnp.concatenate(
        [first * cosine - second * sine, second * cosine + first * sine], axis=-1
    )


def rotate_back(grads, cosine, sine):
    return rotate(grads, cosine, -sine)


def times_transpose(left, weight):
    return lax.dot_general(
        left, weight, (((1,), (1,)), ((), ())), preferred_element_type=F32
    )


def over_rows(left, right):
    return lax.dot_general(
        left, right, (((0,), (0,)), ((), ())), preferred_element_type=F32
    )


def dot(left, right):
    return jnp.dot(left, right, preferred_element_type=F32)


MESH = pl.DeviceIdType.MESH
LIMIT = 67043328


class Kit:
    def __init__(self, sems, sizes):
        self.sems = sems
        self.used = 0
        self.n, self.reps = sizes
        self.chips = self.n // 2
        self.me = lax.axis_index("fsdp")
        self.rep = lax.axis_index("rep")
        self.chip = self.me // 2
        self.core = self.me % 2
        self.bits = self.reps.bit_length() - 1

    def sem(self):
        self.used += 1
        assert self.used <= self.sems.shape[0], "semaphores"
        return self.sems.at[self.used - 1]

    def barrier(self, fsdp=True, rep=True):
        wall = pltpu.get_barrier_semaphore()
        count = 0
        if fsdp:
            for k in range(1, self.n):
                pl.semaphore_signal(wall, inc=1, device_id={"fsdp": self.me ^ k}, device_id_type=MESH)
                count += 1
        if rep:
            for b in range(self.bits):
                pl.semaphore_signal(wall, inc=1, device_id={"rep": self.rep ^ (1 << b)}, device_id_type=MESH)
                count += 1
        pl.semaphore_wait(wall, count)

    def copy(self, src, dst, sems, fsdp=None, rep=None):
        where = {"fsdp": fsdp} if rep is None else {"rep": rep}
        return pltpu.make_async_remote_copy(
            src_ref=src, dst_ref=dst, send_sem=sems[0], recv_sem=sems[1],
            device_id=where, device_id_type=MESH,
        )

    def pair(self):
        return (self.sem(), self.sem())

    def bit(self, index):
        return (self.rep >> index) & 1

    def gather_line(self, src, dst, rows):
        C, z, c = self.chips, self.chip, self.core

        def blk(chip, core):
            return dst.at[pl.ds(pl.multiple_of((2 * chip + core) * rows, rows), rows)]

        local = pltpu.make_async_copy(src, blk(z, c), self.sem())
        local.start()
        partner = self.me ^ 1
        own_sems = self.pair()
        own_pair = self.copy(src, blk(z, c), own_sems, fsdp=partner)
        other_own = blk(z, 1 - c)
        ways = []
        for sign in (1, -1):
            sends = [self.pair() for _ in range(C - 1)]
            forwards = [self.pair() for _ in range(C - 1)]
            ways.append((sign, sends, forwards))

        def inside(chip):
            return (chip >= 0) & (chip < C)

        def hop(sign, sends, k):
            shard = z - sign * k
            ref = src if k == 0 else blk(shard, c)
            return self.copy(ref, blk(shard, c), sends[k], fsdp=2 * (z + sign) + c)

        def across(sign, forwards, k):
            shard = z - sign * k
            return self.copy(blk(shard, c), blk(shard, c), forwards[k - 1], fsdp=partner)

        for sign, sends, forwards in ways:
            @pl.when(inside(z + sign))
            def _():
                hop(sign, sends, 0).start()
        own_pair.start()
        for k in range(1, C):
            yield
            for sign, sends, forwards in ways:
                @pl.when(inside(z - sign * k))
                def _():
                    shard = z - sign * k
                    self.copy(blk(shard, c), blk(shard, c), sends[k - 1], fsdp=partner).wait_recv()
                    if k < C - 1:
                        @pl.when(inside(z + sign))
                        def _():
                            hop(sign, sends, k).start()
                    across(sign, forwards, k).start()
        yield
        local.wait()
        own_pair.wait_send()
        self.copy(src, other_own, own_sems, fsdp=partner).wait_recv()
        for k in range(0, C - 1):
            for sign, sends, forwards in ways:
                @pl.when(inside(z + sign) & inside(z - sign * k))
                def _():
                    hop(sign, sends, k).wait_send()
        for k in range(1, C):
            for sign, sends, forwards in ways:
                @pl.when(inside(z - sign * k))
                def _():
                    across(sign, forwards, k).wait_send()
                    shard = z - sign * k
                    self.copy(blk(shard, c), blk(shard, 1 - c), forwards[k - 1], fsdp=partner).wait_recv()

    def scatter_line(self, partial, total, rows, near, land, compute=None, stage=None):
        C, z, c = self.chips, self.chip, self.core
        partner = self.me ^ 1

        def blk(chip, core):
            return partial.at[pl.ds(pl.multiple_of((2 * chip + core) * rows, rows), rows)]

        order = []
        for j in range(C):
            for d in (C - 1 - j, j):
                if d not in order:
                    order.append(d)
        near_sems = [self.pair() for _ in range(C)]
        right_sems = [self.pair() for _ in range(C)]
        left_sems = [self.pair() for _ in range(C)]

        def swap(d):
            return self.copy(blk(d, 1 - c), near.at[d], near_sems[d], fsdp=partner)

        def to_right(d):
            return self.copy(near.at[d], land.at[d], right_sems[d], fsdp=2 * (z + 1) + c)

        def to_left(d):
            place = jnp.where(z - 1 == d, C, d)
            return self.copy(near.at[d], land.at[place], left_sems[d], fsdp=2 * (z - 1) + c)

        def arrived_left(d, last):
            return self.copy(near.at[d], land.at[C if last else d], left_sems[d], fsdp=partner)

        def settle(d):
            own = blk(d, c)
            if stage is not None:
                load = pltpu.make_async_copy(own, stage, self.sem())
                load.start()
                load.wait()
                own = stage
            swap(d).wait_recv()
            add_into(near.at[d], near.at[d], own)
            if d > 0:
                @pl.when(z == 0)
                def _():
                    to_right(d).start()
            if d < C - 1:
                @pl.when(z == C - 1)
                def _():
                    to_left(d).start()

        for i, d in enumerate(order):
            if compute is not None:
                compute(d)
            swap(d).start()
            if i > 0 and compute is not None:
                settle(order[i - 1])
        yield
        for d in order if compute is None else order[-1:]:
            settle(d)
        for j in range(C - 1):
            yield
            d = C - 1 - j
            if d > 1:
                @pl.when((z > 0) & (z < d))
                def _():
                    to_right(d).wait_recv()
                    add_into(near.at[d], near.at[d], land.at[d])
                    to_right(d).start()
            e = j
            if e < C - 2:
                @pl.when((z < C - 1) & (z > e))
                def _():
                    arrived_left(e, False).wait_recv()
                    add_into(near.at[e], near.at[e], land.at[e])
                    to_left(e).start()
        yield
        keep(total, near.at[z])
        for d in range(C):
            if d > 0:
                @pl.when(z == d)
                def _():
                    to_right(d).wait_recv()
                    accumulate(total, land.at[d])
            if d < C - 1:
                @pl.when(z == d)
                def _():
                    arrived_left(d, True).wait_recv()
                    accumulate(total, land.at[C])
        yield
        for d in range(C):
            swap(d).wait_send()
            @pl.when(z < d)
            def _():
                to_right(d).wait_send()
            @pl.when(z > d)
            def _():
                to_left(d).wait_send()

    def exchange(self, pieces, arrivals):
        sems = {}
        for k in range(1, self.n):
            for i, (src, dst) in enumerate(pieces(self.me ^ k)):
                sems[k, i] = self.pair()
                self.copy(src, dst, sems[k, i], fsdp=self.me ^ k).start()
        yield
        for k in range(1, self.n):
            for i, (src, dst) in enumerate(arrivals(self.me ^ k)):
                self.copy(src, dst, sems[k, i], fsdp=self.me ^ k).wait_recv()
        yield
        for k in range(1, self.n):
            for i, (src, dst) in enumerate(pieces(self.me ^ k)):
                self.copy(src, dst, sems[k, i], fsdp=self.me ^ k).wait_send()

    def gather_rep(self, blk):
        sent = []
        waits = {0: [], 1: []}
        for i in range(self.bits):
            for half in (0, 1):
                b = i if half == 0 else self.bits - 1 - i
                before = [j if half == 0 else self.bits - 1 - j for j in range(i)]
                for cp in waits[half]:
                    cp.wait_recv()
                waits[half] = []
                peer = self.rep ^ (1 << b)
                for mask in range(1 << i):
                    flip = sum(((mask >> j) & 1) << before[j] for j in range(i))
                    r = self.rep ^ flip
                    sems = self.pair()
                    cp = self.copy(blk(half, r), blk(half, r), sems, rep=peer)
                    cp.start()
                    sent.append(cp)
                    waits[half].append(self.copy(blk(half, r), blk(half, r ^ (1 << b)), sems, rep=peer))
            yield
        for half in (0, 1):
            for cp in waits[half]:
                cp.wait_recv()
        yield
        for cp in sent:
            cp.wait_send()

    def scatter_rep(self, blk, land, done, stage=None):
        sent = []
        waits = {0: [], 1: []}
        nb = self.bits

        def start(half, i):
            order = list(range(nb)) if half == 0 else list(range(nb))[::-1]
            peer = self.rep ^ (1 << order[i])
            rest = order[i + 1:]
            todo = []
            for combo in range(1 << len(rest)):
                def source(own, combo=combo):
                    value = self.bit(order[i]) if own else 1 - self.bit(order[i])
                    if i == 0:
                        r = value << order[0]
                        r = r + sum(((combo >> j) & 1) << rest[j] for j in range(len(rest)))
                        return blk(half, r)
                    return land(half, i - 1, value + 2 * combo)
                sems = self.pair()
                cp = self.copy(source(False), land(half, i, combo), sems, rep=peer)
                cp.start()
                sent.append(cp)
                todo.append((cp, land(half, i, combo), source(True)))
            return todo

        for i in range(nb):
            for half in (0, 1):
                if i == 0:
                    waits[half] = start(half, 0)
            if i == 0:
                yield
            for half in (0, 1):
                for cp, ref, own in waits[half]:
                    if stage is not None and i == 0:
                        load = pltpu.make_async_copy(own, stage[half], self.sem())
                        load.start()
                        load.wait()
                        own = stage[half]
                    cp.wait_recv()
                    if i < nb - 1:
                        add_into(ref, ref, own)
                    else:
                        done(half, ref, own)
                if i < nb - 1:
                    waits[half] = start(half, i + 1)
            yield
        for cp in sent:
            cp.wait_send()


def each(ref, body):
    lead = ref.shape[:-2]
    count = ref.shape[-2] // 16
    total = count
    for size in lead:
        total *= size

    def step(t, carry):
        rows = pl.ds(pl.multiple_of((t % count) * 16, 16), 16)
        rest = t // count
        index = []
        for size in reversed(lead):
            index.append(rest % size)
            rest = rest // size
        body(tuple(reversed(index)) + (rows,))
        return carry

    lax.fori_loop(0, total, step, 0)


def add_into(dst, a, b):
    def body(at):
        dst[at] = (a[at].astype(F32) + b[at].astype(F32)).astype(dst.dtype)

    each(dst, body)


def keep(dst, a):
    def body(at):
        dst[at] = a[at].astype(dst.dtype)

    each(dst, body)


def accumulate(dst, a):
    def body(at):
        dst[at] = dst[at] + a[at].astype(F32)

    each(dst, body)


def finish(*tasks):
    for task in tasks:
        for _ in task:
            pass


def turns(order):
    for task in order:
        next(task, None)


def cut(width):
    low = width // 256 * 128
    return ((0, low), (low, width - low))


def column_blocks(ref):
    parts = cut(ref.shape[-1])
    lead = len(ref.shape) - 3

    def blk(half, r):
        start, size = parts[half]
        return ref.at[(slice(None),) * lead + (r, slice(None), pl.ds(start, size))]

    return blk


def own_piece(kit, src_of, dst_of, stage, groups, width):
    first, second = kit.sem(), kit.sem()
    loads = [
        pltpu.make_async_copy(src_of(g), stage.at[:, pl.ds(g * width, width)], kit.sem())
        for g in range(groups)
    ]
    for cp in loads:
        cp.start()
    yield
    for cp in loads:
        cp.wait()
    store = pltpu.make_async_copy(stage, dst_of, first)
    store.start()
    yield
    store.wait()


def column_slice(start, size):
    return pl.ds(pl.multiple_of(start, 128), size)


def reshard(kit, weight, cols, stage, groups):
    n, reps, part, total = cols.shape
    width = total // groups
    rows = pl.ds(pl.multiple_of(kit.rep * part, part), part)

    def source(g, d):
        return weight.at[rows, column_slice(g * (width * n) + d * width, width)]

    def pieces(d):
        return [
            (source(g, d), cols.at[kit.me, kit.rep, :, pl.ds(g * width, width)])
            for g in range(groups)
        ]

    def arrivals(d):
        return [
            (source(g, d), cols.at[d, kit.rep, :, pl.ds(g * width, width)])
            for g in range(groups)
        ]

    own = own_piece(
        kit, lambda g: source(g, kit.me), cols.at[kit.me, kit.rep], stage, groups, width
    )
    move = kit.exchange(pieces, arrivals)
    next(move)
    next(own)
    yield
    next(own)
    next(own, None)
    next(move)
    yield
    finish(move)


def unshard(kit, sums, out, groups):
    n, part, total = sums.shape
    width = total // groups

    def target(g, d):
        return out.at[kit.rep, :, column_slice(g * (width * n) + d * width, width)]

    def pieces(d):
        return [(sums.at[d, :, pl.ds(g * width, width)], target(g, kit.me)) for g in range(groups)]

    def arrivals(d):
        return [(sums.at[d, :, pl.ds(g * width, width)], target(g, d)) for g in range(groups)]

    own = [
        pltpu.make_async_copy(src, dst, kit.sem()) for src, dst in pieces(kit.me)
    ]
    for cp in own:
        cp.start()
    move = kit.exchange(pieces, arrivals)
    next(move)
    yield
    for cp in own:
        cp.wait()
    next(move)
    yield
    finish(move)


def call(body, ins, outs, scratch, count, ident, name):
    def spec(space):
        return pl.BlockSpec(memory_space=space)

    return pl.pallas_call(
        body,
        out_shape=[jax.ShapeDtypeStruct(s, d) for s, d, _ in outs],
        in_specs=[spec(space) for _, space in ins],
        out_specs=[spec(space) for _, _, space in outs],
        scratch_shapes=list(scratch) + [pltpu.SemaphoreType.DMA((count,))],
        compiler_params=pltpu.CompilerParams(
            collective_id=ident, has_side_effects=True, vmem_limit_bytes=LIMIT
        ),
        name=name,
    )(*[a for a, _ in ins])


ANY = pl.ANY
VMEM = pltpu.VMEM


def begin_kernel(sizes, n1, w_qkv, n1_full, cols, stage, sems):
    kit = Kit(sems, sizes)
    kit.barrier()
    move = reshard(kit, w_qkv, cols, stage, 3)
    next(move)
    rows = kit.gather_line(n1, n1_full, n1.shape[0])
    next(rows)
    next(move)
    spread = kit.gather_rep(column_blocks(cols))
    next(spread)
    finish_in_turn([rows, spread, move])


def finish_in_turn(tasks):
    tasks = list(tasks)
    done = object()
    while tasks:
        tasks = [t for t in tasks if next(t, done) is not done]


def begin(sizes, n1, w_qkv):
    n, reps = sizes
    rows, width = n1.shape
    depth = w_qkv.shape[0]
    part, own = depth // reps, w_qkv.shape[1] // n
    full, cols = call(
        functools.partial(begin_kernel, sizes),
        [(n1, VMEM), (w_qkv, ANY)],
        [((n * rows, width), BF16, ANY), ((n, reps, part, own), BF16, ANY)],
        [VMEM((part, own), BF16)],
        20 * n, 1, "begin",
    )
    return full, cols.reshape(n * depth, own)


def norm_rows(dst, src):
    def body(at):
        h = src[at]
        centred = h - jnp.mean(h, axis=-1, keepdims=True)
        inv = lax.rsqrt(jnp.mean(centred * centred, axis=-1, keepdims=True) + eps)
        dst[at] = (centred * inv).astype(BF16)

    each(dst, body)


def middle_kernel(sizes, partial, x, w_in, hidden, n2_full, cols, near, land, n2, stage, sems):
    kit = Kit(sems, sizes)
    kit.barrier()
    move = reshard(kit, w_in, cols, stage, 2)
    next(move)
    total = kit.scatter_line(partial, hidden, x.shape[0], near, land)
    next(total)
    next(total)
    next(move)
    spread = kit.gather_rep(column_blocks(cols))
    next(spread)
    for _ in range(kit.chips - 1):
        next(total)
    next(total)

    def body(at):
        hidden[at] = hidden[at] + x[at].astype(F32)

    each(hidden, body)
    norm_rows(n2, hidden)
    rows = kit.gather_line(n2, n2_full, n2.shape[0])
    next(rows)
    finish_in_turn([spread, rows, move, total])


def line_lands(n, rows, width):
    return [VMEM((n // 2, rows, width), BF16), VMEM((n // 2 + 1, rows, width), BF16)]


def middle(sizes, partial, x, w_in):
    n, reps = sizes
    rows, width = x.shape
    depth = w_in.shape[0]
    part, own = depth // reps, w_in.shape[1] // n
    lands = line_lands(n, rows, width)
    hidden, full, cols = call(
        functools.partial(middle_kernel, sizes),
        [(partial, VMEM), (x, VMEM), (w_in, ANY)],
        [
            ((rows, width), F32, VMEM),
            ((n * rows, width), BF16, ANY),
            ((n, reps, part, own), BF16, ANY),
        ],
        lands + [VMEM((rows, width), BF16), VMEM((part, own), BF16)],
        24 * n, 2, "middle",
    )
    return hidden, full, cols.reshape(n * depth, own)


def lands_of(shape, reps):
    lead, (part, width) = shape[:-3], shape[-2:]
    bits = reps.bit_length() - 1
    places = []
    for start, size in cut(width):
        for i in range(bits):
            places.append(VMEM((1 << (bits - 1 - i),) + lead + (part, size), BF16))
    return places


def land_in(places):
    bits = len(places) // 2

    def land(half, i, j):
        return places[half * bits + i].at[j]

    return land


def put_half(out):
    parts = cut(out.shape[-1])

    def done(half, a, b):
        start, size = parts[half]
        add_into(out.at[(slice(None),) * (len(out.shape) - 1) + (pl.ds(start, size),)], a, b)

    return done


def times_tiles(left, at_rows, right, out, transposed, tile):
    count = out.shape[1] // tile

    def step(t, carry):
        cols = pl.ds(pl.multiple_of(t * tile, tile), tile)
        if transposed:
            value = times_transpose(left[at_rows, :], right[cols, :])
        else:
            value = dot(left[at_rows, :], right[:, cols])
        out[at_rows, cols] = value.astype(BF16)
        return carry

    lax.fori_loop(0, count, step, 0)


def own_stages(shape):
    return [VMEM(shape[:-3] + (shape[-2], size), BF16) for _, size in cut(shape[-1])]


def load_all(kit, pairs):
    copies = [pltpu.make_async_copy(src, dst, kit.sem()) for src, dst in pairs]
    for cp in copies:
        cp.start()
    return copies


def wait_all(copies):
    for cp in copies:
        cp.wait()


def back_kernel(sizes, dgu_h, cols_h, act_h, down_h, hidden, dy, g_in, g_down, resid, out, full, s_in, s_down, dgu, cols, act, down, dn2, near, land, low, *rest):
    sems = rest[-1]
    rows = dy.shape[0]
    bits = sizes[1].bit_length() - 1
    kit = Kit(sems, sizes)
    loads = load_all(kit, [(dgu_h, dgu), (cols_h, cols)])
    later = load_all(kit, [(act_h, act), (down_h, down)])
    kit.barrier()
    t_in = kit.scatter_rep(
        column_blocks(g_in), land_in(rest[: 2 * bits]), put_half(s_in), rest[4 * bits : 4 * bits + 2]
    )
    next(t_in)
    t_down = kit.scatter_rep(
        column_blocks(g_down), land_in(rest[2 * bits : 4 * bits]), put_half(s_down), rest[4 * bits + 2 : 4 * bits + 4]
    )
    next(t_down)

    def first(d):
        times_tiles(dgu, pl.ds(d * 2 * rows, 2 * rows), cols, dn2, True, 256)

    wait_all(loads)
    total = kit.scatter_line(dn2, resid, rows, near, land, first)
    next(total)
    wait_all(later)
    for d in range(kit.chips):
        next(total)
        times_tiles(act, pl.ds(d * 2 * rows, 2 * rows), down, out, False, 256)
    next(total)

    def body(at):
        h = hidden[at]
        centred = h - jnp.mean(h, axis=-1, keepdims=True)
        inv = lax.rsqrt(jnp.mean(centred * centred, axis=-1, keepdims=True) + eps)
        d = dy[at].astype(F32) + norm_back(centred * inv, inv, resid[at])
        resid[at] = d
        low[at] = d.astype(BF16)

    each(resid, body)
    line = kit.gather_line(low, full, rows)
    next(line)
    finish_in_turn([line, t_in, t_down, total])


def back(sizes, dgu, in_cols, act, w_down, hidden, dy, g_in, g_down):
    n, reps = sizes
    rows, width = dy.shape
    g_in = g_in.reshape(n, reps, g_in.shape[0] // (n * reps), g_in.shape[1])
    g_down = g_down.reshape(reps, g_down.shape[0] // reps, g_down.shape[1])
    own = [(a, ANY) for a in (dgu, in_cols, act, w_down)]
    return call(
        functools.partial(back_kernel, sizes),
        own + [(hidden, VMEM), (dy, VMEM), (g_in, ANY), (g_down, ANY)],
        [
            ((rows, width), F32, VMEM),
            ((n * rows, width), BF16, VMEM),
            ((n * rows, width), BF16, ANY),
            ((n,) + g_in.shape[2:], BF16, VMEM),
            (g_down.shape[1:], BF16, VMEM),
        ],
        [VMEM(a.shape, a.dtype) for a, _ in own]
        + [VMEM((n * rows, width), BF16)]
        + line_lands(n, rows, width)
        + [VMEM((rows, width), BF16)]
        + lands_of(g_in.shape, reps)
        + lands_of(g_down.shape, reps)
        + own_stages(g_in.shape)
        + own_stages(g_down.shape),
        20 * n, 3, "back",
    )


def attend_back(q, k, v, datt, att, lse, length, acc_q, acc_k, acc_v):
    slot, own = q.shape
    heads = own // HEAD_DIM
    size = min(256, slot)
    scale = HEAD_DIM ** (-0.5)

    def zero(at):
        for acc in (acc_q, acc_k, acc_v):
            acc[at] = jnp.zeros((16, own), F32)

    each(acc_q, zero)
    for head in range(heads):
        cols = slice(head * HEAD_DIM, (head + 1) * HEAD_DIM)

        def query_block(i, carry):
            at = pl.ds(pl.multiple_of(i * size, size), size)
            qb, db = q[at, cols], datt[at, cols]
            delta = jnp.sum(db.astype(F32) * att[at, cols], axis=-1, keepdims=True)
            level = lse[at, head : head + 1]
            rows = i * size + lax.broadcasted_iota(jnp.int32, (size, size), 0)

            def key_block(j, carry):
                there = pl.ds(pl.multiple_of(j * size, size), size)
                kb, vb = k[there, cols], v[there, cols]
                keys = j * size + lax.broadcasted_iota(jnp.int32, (size, size), 1)
                scores = times_transpose(qb, kb) * scale
                scores = jnp.where((keys <= rows) & (keys < length), scores, neg_big)
                probs = jnp.exp(scores - level)
                grads = (probs * (times_transpose(db, vb) - delta)).astype(BF16)
                acc_v[there, cols] = acc_v[there, cols] + over_rows(probs.astype(BF16), db)
                acc_k[there, cols] = acc_k[there, cols] + over_rows(grads, qb)
                acc_q[at, cols] = acc_q[at, cols] + dot(grads, kb)
                return carry

            return lax.fori_loop(0, i + 1, key_block, carry)

        lax.fori_loop(0, slot // size, query_block, 0)


def turn_back(acc, cosine, sine, out, start):
    slot, own = acc.shape
    scale = HEAD_DIM ** (-0.5)
    size = 128

    def step(i, carry):
        at = pl.ds(pl.multiple_of(i * size, size), size)
        for head in range(own // HEAD_DIM):
            low = head * HEAD_DIM
            value = acc[at, low : low + HEAD_DIM] * scale
            turned = value * cosine[at, :] + pltpu.roll(value, HEAD_DIM // 2, 1) * sine[at, :]
            out[at, start + low : start + low + HEAD_DIM] = turned.astype(BF16)
        return carry

    lax.fori_loop(0, slot // size, step, 0)


def rows_tiles(left, right, out, tile):
    def step(t, carry):
        cols = pl.ds(pl.multiple_of(t * tile, tile), tile)
        out[cols, :] = over_rows(left[:, cols], right[...]).astype(BF16)
        return carry

    lax.fori_loop(0, left.shape[1] // tile, step, 0)


def end_kernel(sizes, *refs):
    n, reps = sizes
    bits = reps.bit_length() - 1
    (length, dres_h, w_out_h, q_h, att_h, low_h, lse_h, cos_h, sin_h, cols_h, n1_h, part_h, s_in, s_down) = refs[:14]
    total_out, branch, o_in, o_down, o_qkv, o_out = refs[14:20]
    (dres, w_out, q, k, v, att, att_low, lse, cosine, sine, cols, n1, datt, acc_q, acc_k, acc_v, dqkv, g_qkv, g_out, dn1, near, land, near_b, land_b, stage, s_qkv, s_out) = refs[20:47]
    rest = refs[47:]
    rows = total_out.shape[0]
    own = q.shape[1]
    kit = Kit(rest[-1], sizes)
    loads = load_all(
        kit,
        [(dres_h, dres), (w_out_h, w_out)]
        + [(q_h.at[:, pl.ds(i * own, own)], ref) for i, ref in enumerate((q, k, v))]
        + [(att_h, att), (lse_h, lse)],
    )
    later = load_all(
        kit, [(low_h, att_low), (cos_h, cosine), (sin_h, sine), (cols_h, cols), (n1_h, n1)]
    )
    own_down = pltpu.make_async_copy(s_down, o_down.at[kit.rep], kit.sem())
    own_down.start()
    kit.barrier()
    move_in = unshard(kit, s_in, o_in, 2)
    next(move_in)
    own_down.wait()
    spread_down = kit.gather_rep(column_blocks(o_down))
    next(spread_down)
    wait_all(loads)

    def project(i, carry):
        at = pl.ds(pl.multiple_of(i * 2 * rows, 2 * rows), 2 * rows)
        datt[at, :] = times_transpose(dres[at, :], w_out[...]).astype(BF16)
        return carry

    lax.fori_loop(0, kit.chips, project, 0)
    attend_back(q, k, v, datt, att, lse, length[0], acc_q, acc_k, acc_v)
    next(spread_down)
    wait_all(later)
    turn_back(acc_q, cosine, sine, dqkv, 0)
    turn_back(acc_k, cosine, sine, dqkv, own)

    def place(at):
        dqkv[at + (pl.ds(2 * own, own),)] = acc_v[at].astype(BF16)

    each(acc_v, place)
    rows_tiles(n1, dqkv, g_qkv, 256)
    parts = g_qkv.shape[0] // (n * reps)
    t_qkv = kit.scatter_rep(
        column_blocks(g_qkv.reshape(n, reps, parts, 3 * own)), land_in(rest[: 2 * bits]), put_half(s_qkv)
    )
    next(t_qkv)

    def first(d):
        times_tiles(dqkv, pl.ds(d * 2 * rows, 2 * rows), cols, dn1, True, 256)

    total = kit.scatter_line(dn1, total_out, rows, near, land, first)
    next(total)
    rows_tiles(att_low, dres, g_out, 128)
    t_out = kit.scatter_rep(
        column_blocks(g_out.reshape(reps, g_out.shape[0] // reps, g_out.shape[1])),
        land_in(rest[2 * bits : 4 * bits]),
        put_half(s_out),
    )
    next(t_out)
    next(total)
    next(move_in)
    spread_in = kit.gather_rep(column_blocks(o_in))
    next(spread_in)
    next(total)
    for _ in range(bits):
        next(t_qkv)
    move_qkv = unshard(kit, s_qkv, o_qkv, 3)
    next(move_qkv)
    for _ in range(bits):
        next(t_out)
    own_out = pltpu.make_async_copy(s_out, o_out.at[kit.rep], kit.sem())
    own_out.start()
    for _ in range(kit.chips - 1):
        next(total)
    other = kit.scatter_line(part_h, branch, rows, near_b, land_b, stage=stage)
    next(other)
    own_out.wait()
    spread_out = kit.gather_rep(column_blocks(o_out))
    next(spread_out)
    next(other)
    next(move_qkv)
    spread_qkv = kit.gather_rep(column_blocks(o_qkv))
    next(spread_qkv)
    finish_in_turn([other, spread_in, spread_qkv, spread_out, total, spread_down, move_in, move_qkv, t_qkv, t_out])


def end(sizes, length, dres, w_out, qkv, att, att_low, lse, cosine, sine, cols, n1, part, s_in, s_down):
    n, reps = sizes
    slot, width = dres.shape
    rows, own = slot // n, w_out.shape[0]
    g_qkv = (n, reps, width // (n * reps), 3 * own)
    g_out = (reps, own // reps, width)
    big = lambda *shape: VMEM(shape, BF16)
    wide = lambda *shape: VMEM(shape, F32)
    any_of = [(a, ANY) for a in (dres, w_out, qkv, att, att_low, lse, cosine, sine, cols, n1, part)]
    total, branch, o_in, o_down, o_qkv, o_out = call(
        functools.partial(end_kernel, sizes),
        [(length, pltpu.SMEM)] + any_of + [(s_in, VMEM), (s_down, VMEM)],
        [
            ((rows, width), F32, VMEM),
            ((rows, width), F32, VMEM),
            ((reps, s_in.shape[1], n * s_in.shape[2]), BF16, ANY),
            ((reps,) + s_down.shape, BF16, ANY),
            ((reps, g_qkv[2], n * g_qkv[3]), BF16, ANY),
            (g_out, BF16, ANY),
        ],
        [big(slot, width), big(own, width), big(slot, own), big(slot, own), big(slot, own)]
        + [wide(slot, own), big(slot, own), wide(slot, 128), wide(slot, 128), wide(slot, 128)]
        + [big(width, 3 * own), big(slot, width), big(slot, own)]
        + [wide(slot, own)] * 3
        + [big(slot, 3 * own), big(width, 3 * own), big(own, width), big(slot, width)]
        + line_lands(n, rows, width) * 2
        + [big(rows, width), big(n, g_qkv[2], 3 * own), big(*g_out[1:])]
        + lands_of(g_qkv, reps)
        + lands_of(g_out, reps),
        32 * n, 4, "end",
    )
    return [total, branch] + [o.reshape(-1, o.shape[-1]).astype(F32) for o in (o_in, o_down, o_qkv, o_out)]


def after(value, *tokens):
    return lax.optimization_barrier((value,) + tokens)[0]


def gather_rows(block):
    return lax.all_gather(block, "fsdp", axis=0, tiled=True)


def on_device(tokens, lengths, cotangent, w_qkv, w_out, w_in, w_down):
    rows = tokens.shape[1]
    width = tokens.shape[2]
    n = lax.axis_size("fsdp")
    slot_len = rows * n
    head_dim = HEAD_DIM
    own_width = width // n
    heads = own_width // head_dim
    scale = head_dim ** (-0.5)
    length = lengths[0]
    own_positions = lax.axis_index("fsdp") * rows + jnp.arange(rows, dtype=jnp.int32)
    valid = (own_positions < length).astype(F32)[:, None]
    positions = jnp.arange(slot_len, dtype=jnp.int32)
    cosine, sine = rotary_tables(positions, head_dim)

    sizes = (n, lax.axis_size("rep"))
    x_rows = tokens[0].astype(F32)
    normed1, inv1 = normalize(x_rows)
    n1_full, qkv_cols = begin(sizes, normed1.astype(BF16), w_qkv)
    dy_rows = valid * cotangent[0].astype(F32)
    dy_low = dy_rows.astype(BF16)
    dy_full = gather_rows(after(dy_low, n1_full))

    qkv = dot(n1_full, qkv_cols)
    query = rotate(
        qkv[:, :own_width].reshape(slot_len, heads, head_dim), cosine, sine
    ).astype(BF16)
    keys = rotate(
        qkv[:, own_width : 2 * own_width].reshape(slot_len, heads, head_dim), cosine, sine
    ).astype(BF16)
    values = qkv[:, 2 * own_width :].reshape(slot_len, heads, head_dim).astype(BF16)
    allowed = (positions[None, :] <= positions[:, None]) & (positions[None, :] < length)

    raw = jnp.einsum("qhd,khd->hqk", query, keys, preferred_element_type=F32) * scale
    scores = jnp.where(allowed[None], raw, neg_big)
    top = jnp.max(scores, axis=-1, keepdims=True)
    log_total = top + jnp.log(jnp.sum(jnp.exp(scores - top), axis=-1, keepdims=True))
    probs = jnp.exp(scores - log_total)
    probs_low = probs.astype(BF16)
    attended = jnp.einsum("hqk,khd->qhd", probs_low, values, preferred_element_type=F32)
    att_low = attended.reshape(slot_len, own_width).astype(BF16)

    out_partial = dot(att_low, w_out).astype(BF16)
    hidden_in, n2_full, in_cols = middle(sizes, out_partial, tokens[0], w_in)
    gate_up = dot(n2_full, in_cols)
    units = gate_up.shape[1] // 2
    gate = gate_up[:, :units]
    upper = gate_up[:, units:]
    sigma = jax.nn.sigmoid(gate)
    silu_gate = gate * sigma
    act_low = (silu_gate * upper).astype(BF16)
    d_hidden = times_transpose(dy_full, w_down)
    d_gate = d_hidden * upper * sigma * (1.0 + gate * (1.0 - sigma))
    d_up = d_hidden * silu_gate
    dgu_low = jnp.concatenate([d_gate, d_up], axis=1).astype(BF16)
    grad_down = over_rows(act_low, dy_full).astype(BF16)
    grad_in = over_rows(n2_full, dgu_low).astype(BF16)
    d_resid, branch_partial, dres_full, sum_in, sum_down = back(
        sizes, dgu_low, in_cols, act_low, w_down, hidden_in, dy_low, grad_in, grad_down
    )

    qkv_low = jnp.concatenate(
        [m.reshape(slot_len, own_width) for m in (query, keys, values)], axis=1
    )
    level = jnp.pad(log_total[..., 0].T, ((0, 0), (0, 128 - heads)))
    d_norm1, branch, all_in, all_down, all_qkv, all_out = end(
        sizes,
        lengths,
        dres_full,
        w_out,
        qkv_low,
        attended.reshape(slot_len, own_width),
        att_low,
        level,
        jnp.concatenate([cosine, cosine], axis=1),
        jnp.concatenate([sine, -sine], axis=1),
        qkv_cols,
        n1_full,
        branch_partial,
        sum_in,
        sum_down,
    )
    output = (valid * (hidden_in + branch)).astype(BF16)
    grad_tokens = (d_resid + norm_back(normed1, inv1, d_norm1)).astype(BF16)
    return (output[None], grad_tokens[None], all_qkv, all_out, all_in, all_down)


def solution(mesh):
    in_specs = (
        P("rep", "fsdp", None),
        P("rep"),
        P("rep", "fsdp", None),
        P("fsdp", None),
        P("fsdp", None),
        P("fsdp", None),
        P("fsdp", None),
    )
    out_specs = (
        P("rep", "fsdp", None),
        P("rep", "fsdp", None),
        P("fsdp", None),
        P("fsdp", None),
        P("fsdp", None),
        P("fsdp", None),
    )
    return jax.shard_map(
        on_device, mesh=mesh, in_specs=in_specs, out_specs=out_specs, check_vma=False
    )
```

```python
import functools

import jax
import jax.numpy as jnp
from jax import lax
from jax.experimental import pallas as pl
from jax.experimental.pallas import tpu as pltpu
from jax.sharding import PartitionSpec as P

HEAD_DIM = 128

eps = 1e-05
neg_big = -1e30
F32 = jnp.float32
BF16 = jnp.bfloat16


def normalize(rows):
    centred = rows - jnp.mean(rows, axis=-1, keepdims=True)
    inv_std = lax.rsqrt(jnp.mean(centred * centred, axis=-1, keepdims=True) + eps)
    return (centred * inv_std, inv_std)


def norm_back(normed, inv_std, grad):
    return inv_std * (
        grad
        - jnp.mean(grad, axis=-1, keepdims=True)
        - normed * jnp.mean(grad * normed, axis=-1, keepdims=True)
    )


def rotary_tables(positions, head_dim):
    half = head_dim // 2
    freqs = 10000.0 ** (-jnp.arange(half, dtype=F32) * 2.0 / head_dim)
    angles = positions.astype(F32)[:, None] * freqs[None, :]
    return (jnp.cos(angles), jnp.sin(angles))


def times_transpose(left, weight):
    return lax.dot_general(
        left, weight, (((1,), (1,)), ((), ())), preferred_element_type=F32
    )


def over_rows(left, right):
    return lax.dot_general(
        left, right, (((0,), (0,)), ((), ())), preferred_element_type=F32
    )


def dot(left, right):
    return jnp.dot(left, right, preferred_element_type=F32)


MESH = pl.DeviceIdType.MESH
LIMIT = 67043328


class Kit:
    def __init__(self, sems, sizes):
        self.sems = sems
        self.used = 0
        self.n, self.reps = sizes
        self.chips = self.n // 2
        self.me = lax.axis_index("fsdp")
        self.rep = lax.axis_index("rep")
        self.chip = self.me // 2
        self.core = self.me % 2
        self.bits = self.reps.bit_length() - 1

    def sem(self):
        self.used += 1
        assert self.used <= self.sems.shape[0], "semaphores"
        return self.sems.at[self.used - 1]

    def barrier(self, fsdp=True, rep=True):
        wall = pltpu.get_barrier_semaphore()
        count = 0
        if fsdp:
            for k in range(1, self.n):
                pl.semaphore_signal(wall, inc=1, device_id={"fsdp": self.me ^ k}, device_id_type=MESH)
                count += 1
        if rep:
            for b in range(self.bits):
                pl.semaphore_signal(wall, inc=1, device_id={"rep": self.rep ^ (1 << b)}, device_id_type=MESH)
                count += 1
        pl.semaphore_wait(wall, count)

    def copy(self, src, dst, sems, fsdp=None, rep=None):
        where = {"fsdp": fsdp} if rep is None else {"rep": rep}
        return pltpu.make_async_remote_copy(
            src_ref=src, dst_ref=dst, send_sem=sems[0], recv_sem=sems[1],
            device_id=where, device_id_type=MESH,
        )

    def pair(self):
        return (self.sem(), self.sem())

    def bit(self, index):
        return (self.rep >> index) & 1

    def gather_line(self, src, dst, rows):
        C, z, c = self.chips, self.chip, self.core

        def blk(chip, core):
            return dst.at[pl.ds(pl.multiple_of((2 * chip + core) * rows, rows), rows)]

        local = pltpu.make_async_copy(src, blk(z, c), self.sem())
        local.start()
        partner = self.me ^ 1
        own_sems = self.pair()
        own_pair = self.copy(src, blk(z, c), own_sems, fsdp=partner)
        other_own = blk(z, 1 - c)
        ways = []
        for sign in (1, -1):
            sends = [self.pair() for _ in range(C - 1)]
            forwards = [self.pair() for _ in range(C - 1)]
            ways.append((sign, sends, forwards))

        def inside(chip):
            return (chip >= 0) & (chip < C)

        def hop(sign, sends, k):
            shard = z - sign * k
            ref = src if k == 0 else blk(shard, c)
            return self.copy(ref, blk(shard, c), sends[k], fsdp=2 * (z + sign) + c)

        def across(sign, forwards, k):
            shard = z - sign * k
            return self.copy(blk(shard, c), blk(shard, c), forwards[k - 1], fsdp=partner)

        for sign, sends, forwards in ways:
            @pl.when(inside(z + sign))
            def _():
                hop(sign, sends, 0).start()
        own_pair.start()
        for k in range(1, C):
            yield
            for sign, sends, forwards in ways:
                @pl.when(inside(z - sign * k))
                def _():
                    shard = z - sign * k
                    self.copy(blk(shard, c), blk(shard, c), sends[k - 1], fsdp=partner).wait_recv()
                    if k < C - 1:
                        @pl.when(inside(z + sign))
                        def _():
                            hop(sign, sends, k).start()
                    across(sign, forwards, k).start()
        yield
        local.wait()
        own_pair.wait_send()
        self.copy(src, other_own, own_sems, fsdp=partner).wait_recv()
        for k in range(0, C - 1):
            for sign, sends, forwards in ways:
                @pl.when(inside(z + sign) & inside(z - sign * k))
                def _():
                    hop(sign, sends, k).wait_send()
        for k in range(1, C):
            for sign, sends, forwards in ways:
                @pl.when(inside(z - sign * k))
                def _():
                    across(sign, forwards, k).wait_send()
                    shard = z - sign * k
                    self.copy(blk(shard, c), blk(shard, 1 - c), forwards[k - 1], fsdp=partner).wait_recv()

    def scatter_line(self, partial, total, rows, near, land, compute=None, stage=None):
        C, z, c = self.chips, self.chip, self.core
        partner = self.me ^ 1

        def blk(chip, core):
            return partial.at[pl.ds(pl.multiple_of((2 * chip + core) * rows, rows), rows)]

        order = []
        for j in range(C):
            for d in (C - 1 - j, j):
                if d not in order:
                    order.append(d)
        near_sems = [self.pair() for _ in range(C)]
        right_sems = [self.pair() for _ in range(C)]
        left_sems = [self.pair() for _ in range(C)]

        def swap(d):
            return self.copy(blk(d, 1 - c), near.at[d], near_sems[d], fsdp=partner)

        def to_right(d):
            return self.copy(near.at[d], land.at[d], right_sems[d], fsdp=2 * (z + 1) + c)

        def to_left(d):
            place = jnp.where(z - 1 == d, C, d)
            return self.copy(near.at[d], land.at[place], left_sems[d], fsdp=2 * (z - 1) + c)

        def arrived_left(d, last):
            return self.copy(near.at[d], land.at[C if last else d], left_sems[d], fsdp=partner)

        def settle(d):
            own = blk(d, c)
            if stage is not None:
                load = pltpu.make_async_copy(own, stage, self.sem())
                load.start()
                load.wait()
                own = stage
            swap(d).wait_recv()
            add_into(near.at[d], near.at[d], own)
            if d > 0:
                @pl.when(z == 0)
                def _():
                    to_right(d).start()
            if d < C - 1:
                @pl.when(z == C - 1)
                def _():
                    to_left(d).start()

        for i, d in enumerate(order):
            if compute is not None:
                compute(d)
            swap(d).start()
            if i > 0 and compute is not None:
                settle(order[i - 1])
        yield
        for d in order if compute is None else order[-1:]:
            settle(d)
        for j in range(C - 1):
            yield
            d = C - 1 - j
            if d > 1:
                @pl.when((z > 0) & (z < d))
                def _():
                    to_right(d).wait_recv()
                    add_into(near.at[d], near.at[d], land.at[d])
                    to_right(d).start()
            e = j
            if e < C - 2:
                @pl.when((z < C - 1) & (z > e))
                def _():
                    arrived_left(e, False).wait_recv()
                    add_into(near.at[e], near.at[e], land.at[e])
                    to_left(e).start()
        yield
        keep(total, near.at[z])
        for d in range(C):
            if d > 0:
                @pl.when(z == d)
                def _():
                    to_right(d).wait_recv()
                    accumulate(total, land.at[d])
            if d < C - 1:
                @pl.when(z == d)
                def _():
                    arrived_left(d, True).wait_recv()
                    accumulate(total, land.at[C])
        yield
        for d in range(C):
            swap(d).wait_send()
            @pl.when(z < d)
            def _():
                to_right(d).wait_send()
            @pl.when(z > d)
            def _():
                to_left(d).wait_send()

    def exchange(self, pieces, arrivals):
        sems = {}
        for k in range(1, self.n):
            for i, (src, dst) in enumerate(pieces(self.me ^ k)):
                sems[k, i] = self.pair()
                self.copy(src, dst, sems[k, i], fsdp=self.me ^ k).start()
        yield
        for k in range(1, self.n):
            for i, (src, dst) in enumerate(arrivals(self.me ^ k)):
                self.copy(src, dst, sems[k, i], fsdp=self.me ^ k).wait_recv()
        yield
        for k in range(1, self.n):
            for i, (src, dst) in enumerate(pieces(self.me ^ k)):
                self.copy(src, dst, sems[k, i], fsdp=self.me ^ k).wait_send()

    def gather_rep(self, blk):
        sent = []
        waits = {0: [], 1: []}
        for i in range(self.bits):
            for half in (0, 1):
                b = i if half == 0 else self.bits - 1 - i
                before = [j if half == 0 else self.bits - 1 - j for j in range(i)]
                for cp in waits[half]:
                    cp.wait_recv()
                waits[half] = []
                peer = self.rep ^ (1 << b)
                for mask in range(1 << i):
                    flip = sum(((mask >> j) & 1) << before[j] for j in range(i))
                    r = self.rep ^ flip
                    sems = self.pair()
                    cp = self.copy(blk(half, r), blk(half, r), sems, rep=peer)
                    cp.start()
                    sent.append(cp)
                    waits[half].append(self.copy(blk(half, r), blk(half, r ^ (1 << b)), sems, rep=peer))
            yield
        for half in (0, 1):
            for cp in waits[half]:
                cp.wait_recv()
        yield
        for cp in sent:
            cp.wait_send()

    def scatter_rep(self, blk, land, done, stage=None):
        sent = []
        waits = {0: [], 1: []}
        nb = self.bits

        def start(half, i):
            order = list(range(nb)) if half == 0 else list(range(nb))[::-1]
            peer = self.rep ^ (1 << order[i])
            rest = order[i + 1:]
            todo = []
            for combo in range(1 << len(rest)):
                def source(own, combo=combo):
                    value = self.bit(order[i]) if own else 1 - self.bit(order[i])
                    if i == 0:
                        r = value << order[0]
                        r = r + sum(((combo >> j) & 1) << rest[j] for j in range(len(rest)))
                        return blk(half, r)
                    return land(half, i - 1, value + 2 * combo)
                sems = self.pair()
                cp = self.copy(source(False), land(half, i, combo), sems, rep=peer)
                cp.start()
                sent.append(cp)
                todo.append((cp, land(half, i, combo), source(True)))
            return todo

        for i in range(nb):
            for half in (0, 1):
                if i == 0:
                    waits[half] = start(half, 0)
            if i == 0:
                yield
            for half in (0, 1):
                for cp, ref, own in waits[half]:
                    if stage is not None and i == 0:
                        load = pltpu.make_async_copy(own, stage[half], self.sem())
                        load.start()
                        load.wait()
                        own = stage[half]
                    cp.wait_recv()
                    if i < nb - 1:
                        add_into(ref, ref, own)
                    else:
                        done(half, ref, own)
                if i < nb - 1:
                    waits[half] = start(half, i + 1)
            yield
        for cp in sent:
            cp.wait_send()


def each(ref, body):
    lead = ref.shape[:-2]
    count = ref.shape[-2] // 16
    total = count
    for size in lead:
        total *= size

    def step(t, carry):
        rows = pl.ds(pl.multiple_of((t % count) * 16, 16), 16)
        rest = t // count
        index = []
        for size in reversed(lead):
            index.append(rest % size)
            rest = rest // size
        body(tuple(reversed(index)) + (rows,))
        return carry

    lax.fori_loop(0, total, step, 0)


def add_into(dst, a, b):
    def body(at):
        dst[at] = (a[at].astype(F32) + b[at].astype(F32)).astype(dst.dtype)

    each(dst, body)


def keep(dst, a):
    def body(at):
        dst[at] = a[at].astype(dst.dtype)

    each(dst, body)


def accumulate(dst, a):
    def body(at):
        dst[at] = dst[at] + a[at].astype(F32)

    each(dst, body)


def finish(*tasks):
    for task in tasks:
        for _ in task:
            pass


def turns(order):
    for task in order:
        next(task, None)


def cut(width):
    low = width // 256 * 128
    return ((0, low), (low, width - low))


def column_blocks(ref):
    parts = cut(ref.shape[-1])
    lead = len(ref.shape) - 3

    def blk(half, r):
        start, size = parts[half]
        return ref.at[(slice(None),) * lead + (r, slice(None), pl.ds(start, size))]

    return blk


def own_piece(kit, src_of, dst_of, stage, groups, width):
    first, second = kit.sem(), kit.sem()
    loads = [
        pltpu.make_async_copy(src_of(g), stage.at[:, pl.ds(g * width, width)], kit.sem())
        for g in range(groups)
    ]
    for cp in loads:
        cp.start()
    yield
    for cp in loads:
        cp.wait()
    store = pltpu.make_async_copy(stage, dst_of, first)
    store.start()
    yield
    store.wait()


def column_slice(start, size):
    return pl.ds(pl.multiple_of(start, 128), size)


def reshard(kit, weight, cols, stage, groups):
    n, reps, part, total = cols.shape
    width = total // groups
    rows = pl.ds(pl.multiple_of(kit.rep * part, part), part)

    def source(g, d):
        return weight.at[rows, column_slice(g * (width * n) + d * width, width)]

    def pieces(d):
        return [
            (source(g, d), cols.at[kit.me, kit.rep, :, pl.ds(g * width, width)])
            for g in range(groups)
        ]

    def arrivals(d):
        return [
            (source(g, d), cols.at[d, kit.rep, :, pl.ds(g * width, width)])
            for g in range(groups)
        ]

    own = own_piece(
        kit, lambda g: source(g, kit.me), cols.at[kit.me, kit.rep], stage, groups, width
    )
    move = kit.exchange(pieces, arrivals)
    next(move)
    next(own)
    yield
    next(own)
    next(own, None)
    next(move)
    yield
    finish(move)


def unshard(kit, sums, out, groups):
    n, part, total = sums.shape
    width = total // groups

    def target(g, d):
        return out.at[kit.rep, :, column_slice(g * (width * n) + d * width, width)]

    def pieces(d):
        return [(sums.at[d, :, pl.ds(g * width, width)], target(g, kit.me)) for g in range(groups)]

    def arrivals(d):
        return [(sums.at[d, :, pl.ds(g * width, width)], target(g, d)) for g in range(groups)]

    own = [
        pltpu.make_async_copy(src, dst, kit.sem()) for src, dst in pieces(kit.me)
    ]
    for cp in own:
        cp.start()
    move = kit.exchange(pieces, arrivals)
    next(move)
    yield
    for cp in own:
        cp.wait()
    next(move)
    yield
    finish(move)


def call(body, ins, outs, scratch, count, ident, name):
    def spec(space):
        return pl.BlockSpec(memory_space=space)

    return pl.pallas_call(
        body,
        out_shape=[jax.ShapeDtypeStruct(s, d) for s, d, _ in outs],
        in_specs=[spec(space) for _, space in ins],
        out_specs=[spec(space) for _, _, space in outs],
        scratch_shapes=list(scratch) + [pltpu.SemaphoreType.DMA((count,))],
        compiler_params=pltpu.CompilerParams(
            collective_id=ident, has_side_effects=True, vmem_limit_bytes=LIMIT
        ),
        name=name,
    )(*[a for a, _ in ins])


ANY = pl.ANY
VMEM = pltpu.VMEM


def finish_in_turn(tasks):
    tasks = list(tasks)
    done = object()
    while tasks:
        tasks = [t for t in tasks if next(t, done) is not done]


def norm_rows(dst, src):
    def body(at):
        h = src[at]
        centred = h - jnp.mean(h, axis=-1, keepdims=True)
        inv = lax.rsqrt(jnp.mean(centred * centred, axis=-1, keepdims=True) + eps)
        dst[at] = (centred * inv).astype(BF16)

    each(dst, body)


def line_lands(n, rows, width):
    return [VMEM((n // 2, rows, width), BF16), VMEM((n // 2 + 1, rows, width), BF16)]


def lands_of(shape, reps):
    lead, (part, width) = shape[:-3], shape[-2:]
    bits = reps.bit_length() - 1
    places = []
    for start, size in cut(width):
        for i in range(bits):
            places.append(VMEM((1 << (bits - 1 - i),) + lead + (part, size), BF16))
    return places


def land_in(places):
    bits = len(places) // 2

    def land(half, i, j):
        return places[half * bits + i].at[j]

    return land


def put_half(out):
    parts = cut(out.shape[-1])

    def done(half, a, b):
        start, size = parts[half]
        add_into(out.at[(slice(None),) * (len(out.shape) - 1) + (pl.ds(start, size),)], a, b)

    return done


def times_tiles(left, at_rows, right, out, transposed, tile):
    count = out.shape[1] // tile

    def step(t, carry):
        cols = pl.ds(pl.multiple_of(t * tile, tile), tile)
        if transposed:
            value = times_transpose(left[at_rows, :], right[cols, :])
        else:
            value = dot(left[at_rows, :], right[:, cols])
        out[at_rows, cols] = value.astype(BF16)
        return carry

    lax.fori_loop(0, count, step, 0)


def own_stages(shape):
    return [VMEM(shape[:-3] + (shape[-2], size), BF16) for _, size in cut(shape[-1])]


def load_all(kit, pairs):
    copies = [pltpu.make_async_copy(src, dst, kit.sem()) for src, dst in pairs]
    for cp in copies:
        cp.start()
    return copies


def wait_all(copies):
    for cp in copies:
        cp.wait()


def project_qkv(n1, cols, cosine, sine, qkv):
    slot, total = qkv.shape
    own = total // 3
    size = 256

    def step(i, carry):
        at = pl.ds(pl.multiple_of(i * size, size), size)
        value = dot(n1[at, :], cols[...])
        for low in range(0, 2 * own, HEAD_DIM):
            part = value[:, low : low + HEAD_DIM]
            turned = part * cosine[at, :] - pltpu.roll(part, HEAD_DIM // 2, 1) * sine[at, :]
            qkv[at, low : low + HEAD_DIM] = turned.astype(BF16)
        qkv[at, 2 * own :] = value[:, 2 * own :].astype(BF16)
        return carry

    lax.fori_loop(0, slot // size, step, 0)


def attend(qkv, length, att, att_low, lse):
    slot, own = att.shape
    heads = own // HEAD_DIM
    size = min(256, slot)
    scale = HEAD_DIM ** (-0.5)
    for i in range(slot // size):
        at = slice(i * size, (i + 1) * size)
        width = (i + 1) * size
        rows = i * size + lax.broadcasted_iota(jnp.int32, (size, width), 0)
        keys = lax.broadcasted_iota(jnp.int32, (size, width), 1)
        allowed = (keys <= rows) & (keys < length)
        for head in range(heads):
            low = head * HEAD_DIM
            q = qkv[at, low : low + HEAD_DIM]
            k = qkv[:width, own + low : own + low + HEAD_DIM]
            v = qkv[:width, 2 * own + low : 2 * own + low + HEAD_DIM]
            scores = jnp.where(allowed, times_transpose(q, k) * scale, neg_big)
            top = jnp.max(scores, axis=-1, keepdims=True)
            level = top + jnp.log(jnp.sum(jnp.exp(scores - top), axis=-1, keepdims=True))
            probs = jnp.exp(scores - level).astype(BF16)
            value = dot(probs, v)
            att[at, low : low + HEAD_DIM] = value
            att_low[at, low : low + HEAD_DIM] = value.astype(BF16)
            lse[at, head:] = jnp.broadcast_to(level, (size, 128 - head))


def front_kernel(sizes, *refs):
    (length, x, dy, w_qkv, w_in, w_out_h, cos_h, sin_h) = refs[:8]
    (hidden, qkv, att, att_low, lse, n1_full, n2_full, dy_full, qkv_cols, in_cols) = refs[8:18]
    (n_low, n1, cols, w_out, cosine, sine, partial, near, land, stage, stage_in, sems) = refs[18:]
    kit = Kit(sems, sizes)
    rows = x.shape[0]
    loads = load_all(kit, [(w_out_h, w_out), (cos_h, cosine), (sin_h, sine)])

    def widen(at):
        hidden[at] = x[at].astype(F32)

    each(hidden, widen)
    norm_rows(n_low.at[0], hidden)
    kit.barrier()
    move = reshard(kit, w_qkv, qkv_cols, stage, 3)
    next(move)
    line = kit.gather_line(n_low.at[0], n1_full, rows)
    next(line)
    next(move)
    spread = kit.gather_rep(column_blocks(qkv_cols))
    next(spread)
    finish_in_turn([line, spread, move])
    move_in = reshard(kit, w_in, in_cols, stage_in, 2)
    next(move_in)
    n, reps, part, own = qkv_cols.shape
    more = [(n1_full, n1)] + [
        (qkv_cols.at[d, r], cols.at[pl.ds((d * reps + r) * part, part)]) for d in range(n) for r in range(reps)
    ]
    wait_all(loads + load_all(kit, more))
    project_qkv(n1, cols, cosine, sine, qkv)
    attend(qkv, length[0], att, att_low, lse)

    def first(d):
        times_tiles(att_low, pl.ds(d * 2 * rows, 2 * rows), w_out, partial, False, 256)

    total = kit.scatter_line(partial, hidden, rows, near, land, first)
    next(total)
    next(total)
    next(move_in)
    spread_in = kit.gather_rep(column_blocks(in_cols))
    next(spread_in)
    for _ in range(kit.chips - 2):
        next(total)
    next(spread_in)
    next(total)
    next(total)

    def body(at):
        hidden[at] = hidden[at] + x[at].astype(F32)

    each(hidden, body)
    norm_rows(n_low.at[1], hidden)
    gather = kit.gather_line(n_low.at[1], n2_full, rows)
    next(gather)
    other = kit.gather_line(dy, dy_full, rows)
    next(other)
    finish_in_turn([gather, other, spread_in, move_in, total])


def front(sizes, length, x, dy, w_qkv, w_in, w_out, cosine, sine):
    n, reps = sizes
    rows, width = x.shape
    slot = n * rows
    depth = w_qkv.shape[0]
    part, own_qkv, own_in = depth // reps, w_qkv.shape[1] // n, w_in.shape[1] // n
    own = w_out.shape[0]
    big = lambda *shape: VMEM(shape, BF16)
    wide = lambda *shape: VMEM(shape, F32)
    outs = call(
        functools.partial(front_kernel, sizes),
        [(length, pltpu.SMEM), (x, VMEM), (dy, VMEM)]
        + [(a, ANY) for a in (w_qkv, w_in, w_out, cosine, sine)],
        [
            ((rows, width), F32, VMEM),
            ((slot, 3 * own), BF16, VMEM),
            ((slot, own), F32, VMEM),
            ((slot, own), BF16, VMEM),
            ((slot, 128), F32, VMEM),
            ((slot, width), BF16, ANY),
            ((slot, width), BF16, ANY),
            ((slot, width), BF16, ANY),
            ((n, reps, part, own_qkv), BF16, ANY),
            ((n, reps, part, own_in), BF16, ANY),
        ],
        [big(2, rows, width), big(slot, width), big(n * depth, own_qkv), big(own, width)]
        + [wide(slot, 128), wide(slot, 128), big(slot, width)]
        + line_lands(n, rows, width)
        + [big(part, own_qkv), big(part, own_in)],
        64 * n, 1, "front",
    )
    return list(outs[:8]) + [o.reshape(n * depth, -1) for o in outs[8:]]


def back_kernel(sizes, dgu_h, cols_h, act_h, down_h, hidden, dy, g_in, g_down, resid, out, full, s_in, s_down, dgu, cols, act, down, dn2, near, land, low, *rest):
    sems = rest[-1]
    rows = dy.shape[0]
    bits = sizes[1].bit_length() - 1
    kit = Kit(sems, sizes)
    loads = load_all(kit, [(dgu_h, dgu), (cols_h, cols)])
    later = load_all(kit, [(act_h, act), (down_h, down)])
    kit.barrier()
    t_in = kit.scatter_rep(
        column_blocks(g_in), land_in(rest[: 2 * bits]), put_half(s_in), rest[4 * bits : 4 * bits + 2]
    )
    next(t_in)
    t_down = kit.scatter_rep(
        column_blocks(g_down), land_in(rest[2 * bits : 4 * bits]), put_half(s_down), rest[4 * bits + 2 : 4 * bits + 4]
    )
    next(t_down)

    def first(d):
        times_tiles(dgu, pl.ds(d * 2 * rows, 2 * rows), cols, dn2, True, 256)

    wait_all(loads)
    total = kit.scatter_line(dn2, resid, rows, near, land, first)
    next(total)
    wait_all(later)
    for d in range(kit.chips):
        next(total)
        times_tiles(act, pl.ds(d * 2 * rows, 2 * rows), down, out, False, 256)
    next(total)

    def body(at):
        h = hidden[at]
        centred = h - jnp.mean(h, axis=-1, keepdims=True)
        inv = lax.rsqrt(jnp.mean(centred * centred, axis=-1, keepdims=True) + eps)
        d = dy[at].astype(F32) + norm_back(centred * inv, inv, resid[at])
        resid[at] = d
        low[at] = d.astype(BF16)

    each(resid, body)
    line = kit.gather_line(low, full, rows)
    next(line)
    finish_in_turn([line, t_in, t_down, total])


def back(sizes, dgu, in_cols, act, w_down, hidden, dy, g_in, g_down):
    n, reps = sizes
    rows, width = dy.shape
    g_in = g_in.reshape(n, reps, g_in.shape[0] // (n * reps), g_in.shape[1])
    g_down = g_down.reshape(reps, g_down.shape[0] // reps, g_down.shape[1])
    own = [(a, ANY) for a in (dgu, in_cols, act, w_down)]
    return call(
        functools.partial(back_kernel, sizes),
        own + [(hidden, VMEM), (dy, VMEM), (g_in, ANY), (g_down, ANY)],
        [
            ((rows, width), F32, VMEM),
            ((n * rows, width), BF16, VMEM),
            ((n * rows, width), BF16, ANY),
            ((n,) + g_in.shape[2:], BF16, VMEM),
            (g_down.shape[1:], BF16, VMEM),
        ],
        [VMEM(a.shape, a.dtype) for a, _ in own]
        + [VMEM((n * rows, width), BF16)]
        + line_lands(n, rows, width)
        + [VMEM((rows, width), BF16)]
        + lands_of(g_in.shape, reps)
        + lands_of(g_down.shape, reps)
        + own_stages(g_in.shape)
        + own_stages(g_down.shape),
        20 * n, 3, "back",
    )


def attend_back(q, k, v, datt, att, lse, length, acc_q, acc_k, acc_v, between):
    slot, own = q.shape
    heads = own // HEAD_DIM
    size = min(256, slot)
    scale = HEAD_DIM ** (-0.5)

    def zero(at):
        for acc in (acc_q, acc_k, acc_v):
            acc[at] = jnp.zeros((16, own), F32)

    each(acc_q, zero)
    for head in range(heads):
        cols = slice(head * HEAD_DIM, (head + 1) * HEAD_DIM)

        def query_block(i, carry):
            at = pl.ds(pl.multiple_of(i * size, size), size)
            qb, db = q[at, cols], datt[at, cols]
            delta = jnp.sum(db.astype(F32) * att[at, cols], axis=-1, keepdims=True)
            level = lse[at, head : head + 1]
            rows = i * size + lax.broadcasted_iota(jnp.int32, (size, size), 0)

            def key_block(j, carry):
                there = pl.ds(pl.multiple_of(j * size, size), size)
                kb, vb = k[there, cols], v[there, cols]
                keys = j * size + lax.broadcasted_iota(jnp.int32, (size, size), 1)
                scores = times_transpose(qb, kb) * scale
                scores = jnp.where((keys <= rows) & (keys < length), scores, neg_big)
                probs = jnp.exp(scores - level)
                grads = (probs * (times_transpose(db, vb) - delta)).astype(BF16)
                acc_v[there, cols] = acc_v[there, cols] + over_rows(probs.astype(BF16), db)
                acc_k[there, cols] = acc_k[there, cols] + over_rows(grads, qb)
                acc_q[at, cols] = acc_q[at, cols] + dot(grads, kb)
                return carry

            return lax.fori_loop(0, i + 1, key_block, carry)

        lax.fori_loop(0, slot // size, query_block, 0)
        between(head)


def turn_back(acc, cosine, sine, out, start):
    slot, own = acc.shape
    scale = HEAD_DIM ** (-0.5)
    size = 128

    def step(i, carry):
        at = pl.ds(pl.multiple_of(i * size, size), size)
        for head in range(own // HEAD_DIM):
            low = head * HEAD_DIM
            value = acc[at, low : low + HEAD_DIM] * scale
            turned = value * cosine[at, :] + pltpu.roll(value, HEAD_DIM // 2, 1) * sine[at, :]
            out[at, start + low : start + low + HEAD_DIM] = turned.astype(BF16)
        return carry

    lax.fori_loop(0, slot // size, step, 0)


def rows_tiles(left, right, out, tile):
    def step(t, carry):
        cols = pl.ds(pl.multiple_of(t * tile, tile), tile)
        out[cols, :] = over_rows(left[:, cols], right[...]).astype(BF16)
        return carry

    lax.fori_loop(0, left.shape[1] // tile, step, 0)


def end_kernel(sizes, *refs):
    n, reps = sizes
    bits = reps.bit_length() - 1
    (length, dres_h, w_out_h, q_h, att_h, low_h, lse_h, cos_h, sin_h, cols_h, n1_h, part_h, s_in, s_down) = refs[:14]
    total_out, branch, o_in, o_down, o_qkv, o_out = refs[14:20]
    (dres, w_out, q, k, v, att, att_low, lse, cosine, sine, cols, n1, datt, acc_q, acc_k, acc_v, dqkv, g_qkv, g_out, dn1, near, land, near_b, land_b, stage, s_qkv, s_out) = refs[20:47]
    rest = refs[47:]
    rows = total_out.shape[0]
    own = q.shape[1]
    kit = Kit(rest[-1], sizes)
    loads = load_all(
        kit,
        [(dres_h, dres), (w_out_h, w_out)]
        + [(q_h.at[:, pl.ds(i * own, own)], ref) for i, ref in enumerate((q, k, v))]
        + [(att_h, att), (lse_h, lse)],
    )
    later = load_all(
        kit, [(low_h, att_low), (cos_h, cosine), (sin_h, sine), (cols_h, cols), (n1_h, n1)]
    )
    own_down = pltpu.make_async_copy(s_down, o_down.at[kit.rep], kit.sem())
    own_down.start()
    kit.barrier()
    move_in = unshard(kit, s_in, o_in, 2)
    next(move_in)
    own_down.wait()
    spread_down = kit.gather_rep(column_blocks(o_down))
    next(spread_down)
    wait_all(loads)

    def project(i, carry):
        at = pl.ds(pl.multiple_of(i * 2 * rows, 2 * rows), 2 * rows)
        datt[at, :] = times_transpose(dres[at, :], w_out[...]).astype(BF16)
        return carry

    lax.fori_loop(0, kit.chips, project, 0)
    def between(head):
        if head == 0:
            next(spread_down)

    attend_back(q, k, v, datt, att, lse, length[0], acc_q, acc_k, acc_v, between)
    wait_all(later)
    turn_back(acc_q, cosine, sine, dqkv, 0)
    turn_back(acc_k, cosine, sine, dqkv, own)

    def place(at):
        dqkv[at + (pl.ds(2 * own, own),)] = acc_v[at].astype(BF16)

    each(acc_v, place)
    rows_tiles(n1, dqkv, g_qkv, 256)
    parts = g_qkv.shape[0] // (n * reps)
    t_qkv = kit.scatter_rep(
        column_blocks(g_qkv.reshape(n, reps, parts, 3 * own)), land_in(rest[: 2 * bits]), put_half(s_qkv)
    )
    next(t_qkv)

    def first(d):
        times_tiles(dqkv, pl.ds(d * 2 * rows, 2 * rows), cols, dn1, True, 256)

    total = kit.scatter_line(dn1, total_out, rows, near, land, first)
    next(total)
    next(move_in)
    spread_in = kit.gather_rep(column_blocks(o_in))
    next(spread_in)
    next(total)
    rows_tiles(att_low, dres, g_out, 128)
    t_out = kit.scatter_rep(
        column_blocks(g_out.reshape(reps, g_out.shape[0] // reps, g_out.shape[1])),
        land_in(rest[2 * bits : 4 * bits]),
        put_half(s_out),
    )
    next(t_out)
    next(total)
    next(t_qkv)
    for _ in range(kit.chips - 2):
        next(total)
    for _ in range(bits - 1):
        next(t_qkv)
    move_qkv = unshard(kit, s_qkv, o_qkv, 3)
    next(move_qkv)
    next(spread_in)
    for _ in range(bits):
        next(t_out)
    own_out = pltpu.make_async_copy(s_out, o_out.at[kit.rep], kit.sem())
    own_out.start()
    other = kit.scatter_line(part_h, branch, rows, near_b, land_b, stage=stage)
    next(other)
    next(total)
    next(other)
    own_out.wait()
    spread_out = kit.gather_rep(column_blocks(o_out))
    next(spread_out)
    next(move_qkv)
    spread_qkv = kit.gather_rep(column_blocks(o_qkv))
    next(spread_qkv)
    finish_in_turn([other, spread_qkv, spread_out, spread_in, total, spread_down, move_in, move_qkv, t_qkv, t_out])


def end(sizes, length, dres, w_out, qkv, att, att_low, lse, cosine, sine, cols, n1, part, s_in, s_down):
    n, reps = sizes
    slot, width = dres.shape
    rows, own = slot // n, w_out.shape[0]
    g_qkv = (n, reps, width // (n * reps), 3 * own)
    g_out = (reps, own // reps, width)
    big = lambda *shape: VMEM(shape, BF16)
    wide = lambda *shape: VMEM(shape, F32)
    any_of = [(a, ANY) for a in (dres, w_out, qkv, att, att_low, lse, cosine, sine, cols, n1, part)]
    total, branch, o_in, o_down, o_qkv, o_out = call(
        functools.partial(end_kernel, sizes),
        [(length, pltpu.SMEM)] + any_of + [(s_in, VMEM), (s_down, VMEM)],
        [
            ((rows, width), F32, VMEM),
            ((rows, width), F32, VMEM),
            ((reps, s_in.shape[1], n * s_in.shape[2]), BF16, ANY),
            ((reps,) + s_down.shape, BF16, ANY),
            ((reps, g_qkv[2], n * g_qkv[3]), BF16, ANY),
            (g_out, BF16, ANY),
        ],
        [big(slot, width), big(own, width), big(slot, own), big(slot, own), big(slot, own)]
        + [wide(slot, own), big(slot, own), wide(slot, 128), wide(slot, 128), wide(slot, 128)]
        + [big(width, 3 * own), big(slot, width), big(slot, own)]
        + [wide(slot, own)] * 3
        + [big(slot, 3 * own), big(width, 3 * own), big(own, width), big(slot, width)]
        + line_lands(n, rows, width) * 2
        + [big(rows, width), big(n, g_qkv[2], 3 * own), big(*g_out[1:])]
        + lands_of(g_qkv, reps)
        + lands_of(g_out, reps),
        32 * n, 4, "end",
    )
    return [total, branch] + [o.reshape(-1, o.shape[-1]).astype(F32) for o in (o_in, o_down, o_qkv, o_out)]


def on_device(tokens, lengths, cotangent, w_qkv, w_out, w_in, w_down):
    rows = tokens.shape[1]
    width = tokens.shape[2]
    n = lax.axis_size("fsdp")
    slot_len = rows * n
    head_dim = HEAD_DIM
    length = lengths[0]
    own_positions = lax.axis_index("fsdp") * rows + jnp.arange(rows, dtype=jnp.int32)
    valid = (own_positions < length).astype(F32)[:, None]
    positions = jnp.arange(slot_len, dtype=jnp.int32)
    cosine, sine = rotary_tables(positions, head_dim)

    sizes = (n, lax.axis_size("rep"))
    dy_rows = valid * cotangent[0].astype(F32)
    dy_low = dy_rows.astype(BF16)
    turn_cos = jnp.concatenate([cosine, cosine], axis=1)
    turn_sin = jnp.concatenate([sine, -sine], axis=1)
    hidden_in, qkv_low, attended, att_low, level, n1_full, n2_full, dy_full, qkv_cols, in_cols = front(
        sizes, lengths, tokens[0], dy_low, w_qkv, w_in, w_out, turn_cos, turn_sin
    )
    gate_up = dot(n2_full, in_cols)
    units = gate_up.shape[1] // 2
    gate = gate_up[:, :units]
    upper = gate_up[:, units:]
    sigma = jax.nn.sigmoid(gate)
    silu_gate = gate * sigma
    act_low = (silu_gate * upper).astype(BF16)
    d_hidden = times_transpose(dy_full, w_down)
    d_gate = d_hidden * upper * sigma * (1.0 + gate * (1.0 - sigma))
    d_up = d_hidden * silu_gate
    dgu_low = jnp.concatenate([d_gate, d_up], axis=1).astype(BF16)
    grad_down = over_rows(act_low, dy_full).astype(BF16)
    grad_in = over_rows(n2_full, dgu_low).astype(BF16)
    d_resid, branch_partial, dres_full, sum_in, sum_down = back(
        sizes, dgu_low, in_cols, act_low, w_down, hidden_in, dy_low, grad_in, grad_down
    )

    d_norm1, branch, all_in, all_down, all_qkv, all_out = end(
        sizes,
        lengths,
        dres_full,
        w_out,
        qkv_low,
        attended,
        att_low,
        level,
        turn_cos,
        turn_sin,
        qkv_cols,
        n1_full,
        branch_partial,
        sum_in,
        sum_down,
    )
    output = (valid * (hidden_in + branch)).astype(BF16)
    normed1, inv1 = normalize(tokens[0].astype(F32))
    grad_tokens = (d_resid + norm_back(normed1, inv1, d_norm1)).astype(BF16)
    return (output[None], grad_tokens[None], all_qkv, all_out, all_in, all_down)


def solution(mesh):
    in_specs = (
        P("rep", "fsdp", None),
        P("rep"),
        P("rep", "fsdp", None),
        P("fsdp", None),
        P("fsdp", None),
        P("fsdp", None),
        P("fsdp", None),
    )
    out_specs = (
        P("rep", "fsdp", None),
        P("rep", "fsdp", None),
        P("fsdp", None),
        P("fsdp", None),
        P("fsdp", None),
        P("fsdp", None),
    )
    return jax.shard_map(
        on_device, mesh=mesh, in_specs=in_specs, out_specs=out_specs, check_vma=False
    )
```

```python
import functools

import jax
import jax.numpy as jnp
from jax import lax
from jax.experimental import pallas as pl
from jax.experimental.pallas import tpu as pltpu
from jax.sharding import PartitionSpec as P

HEAD_DIM = 128

eps = 1e-05
neg_big = -1e30
F32 = jnp.float32
BF16 = jnp.bfloat16


def normalize(rows):
    centred = rows - jnp.mean(rows, axis=-1, keepdims=True)
    inv_std = lax.rsqrt(jnp.mean(centred * centred, axis=-1, keepdims=True) + eps)
    return (centred * inv_std, inv_std)


def norm_back(normed, inv_std, grad):
    return inv_std * (
        grad
        - jnp.mean(grad, axis=-1, keepdims=True)
        - normed * jnp.mean(grad * normed, axis=-1, keepdims=True)
    )


def rotary_tables(positions, head_dim):
    half = head_dim // 2
    freqs = 10000.0 ** (-jnp.arange(half, dtype=F32) * 2.0 / head_dim)
    angles = positions.astype(F32)[:, None] * freqs[None, :]
    return (jnp.cos(angles), jnp.sin(angles))


def times_transpose(left, weight):
    return lax.dot_general(
        left, weight, (((1,), (1,)), ((), ())), preferred_element_type=F32
    )


def over_rows(left, right):
    return lax.dot_general(
        left, right, (((0,), (0,)), ((), ())), preferred_element_type=F32
    )


def dot(left, right):
    return jnp.dot(left, right, preferred_element_type=F32)


MESH = pl.DeviceIdType.MESH
LIMIT = 67043328


class Kit:
    def __init__(self, sems, sizes):
        self.sems = sems
        self.used = 0
        self.n, self.reps = sizes
        self.chips = self.n // 2
        self.me = lax.axis_index("fsdp")
        self.rep = lax.axis_index("rep")
        self.chip = self.me // 2
        self.core = self.me % 2
        self.bits = self.reps.bit_length() - 1

    def sem(self):
        self.used += 1
        assert self.used <= self.sems.shape[0], "semaphores"
        return self.sems.at[self.used - 1]

    def barrier(self, fsdp=True, rep=True):
        wall = pltpu.get_barrier_semaphore()
        count = 0
        if fsdp:
            for k in range(1, self.n):
                pl.semaphore_signal(wall, inc=1, device_id={"fsdp": self.me ^ k}, device_id_type=MESH)
                count += 1
        if rep:
            for b in range(self.bits):
                pl.semaphore_signal(wall, inc=1, device_id={"rep": self.rep ^ (1 << b)}, device_id_type=MESH)
                count += 1
        pl.semaphore_wait(wall, count)

    def copy(self, src, dst, sems, fsdp=None, rep=None):
        where = {"fsdp": fsdp} if rep is None else {"rep": rep}
        return pltpu.make_async_remote_copy(
            src_ref=src, dst_ref=dst, send_sem=sems[0], recv_sem=sems[1],
            device_id=where, device_id_type=MESH,
        )

    def pair(self):
        return (self.sem(), self.sem())

    def bit(self, index):
        return (self.rep >> index) & 1

    def gather_line(self, src, dst, rows):
        C, z, c = self.chips, self.chip, self.core

        def blk(chip, core):
            return dst.at[pl.ds(pl.multiple_of((2 * chip + core) * rows, rows), rows)]

        local = pltpu.make_async_copy(src, blk(z, c), self.sem())
        local.start()
        partner = self.me ^ 1
        own_sems = self.pair()
        own_pair = self.copy(src, blk(z, c), own_sems, fsdp=partner)
        other_own = blk(z, 1 - c)
        ways = []
        for sign in (1, -1):
            sends = [self.pair() for _ in range(C - 1)]
            forwards = [self.pair() for _ in range(C - 1)]
            ways.append((sign, sends, forwards))

        def inside(chip):
            return (chip >= 0) & (chip < C)

        def hop(sign, sends, k):
            shard = z - sign * k
            ref = src if k == 0 else blk(shard, c)
            return self.copy(ref, blk(shard, c), sends[k], fsdp=2 * (z + sign) + c)

        def across(sign, forwards, k):
            shard = z - sign * k
            return self.copy(blk(shard, c), blk(shard, c), forwards[k - 1], fsdp=partner)

        for sign, sends, forwards in ways:
            @pl.when(inside(z + sign))
            def _():
                hop(sign, sends, 0).start()
        own_pair.start()
        for k in range(1, C):
            yield
            for sign, sends, forwards in ways:
                @pl.when(inside(z - sign * k))
                def _():
                    shard = z - sign * k
                    self.copy(blk(shard, c), blk(shard, c), sends[k - 1], fsdp=partner).wait_recv()
                    if k < C - 1:
                        @pl.when(inside(z + sign))
                        def _():
                            hop(sign, sends, k).start()
                    across(sign, forwards, k).start()
        yield
        local.wait()
        own_pair.wait_send()
        self.copy(src, other_own, own_sems, fsdp=partner).wait_recv()
        for k in range(0, C - 1):
            for sign, sends, forwards in ways:
                @pl.when(inside(z + sign) & inside(z - sign * k))
                def _():
                    hop(sign, sends, k).wait_send()
        for k in range(1, C):
            for sign, sends, forwards in ways:
                @pl.when(inside(z - sign * k))
                def _():
                    across(sign, forwards, k).wait_send()
                    shard = z - sign * k
                    self.copy(blk(shard, c), blk(shard, 1 - c), forwards[k - 1], fsdp=partner).wait_recv()

    def scatter_line(self, partial, total, rows, near, land, compute=None, stage=None):
        C, z, c = self.chips, self.chip, self.core
        partner = self.me ^ 1

        def blk(chip, core):
            return partial.at[pl.ds(pl.multiple_of((2 * chip + core) * rows, rows), rows)]

        order = []
        for j in range(C):
            for d in (C - 1 - j, j):
                if d not in order:
                    order.append(d)
        near_sems = [self.pair() for _ in range(C)]
        right_sems = [self.pair() for _ in range(C)]
        left_sems = [self.pair() for _ in range(C)]

        def swap(d):
            return self.copy(blk(d, 1 - c), near.at[d], near_sems[d], fsdp=partner)

        def to_right(d):
            return self.copy(near.at[d], land.at[d], right_sems[d], fsdp=2 * (z + 1) + c)

        def to_left(d):
            place = jnp.where(z - 1 == d, C, d)
            return self.copy(near.at[d], land.at[place], left_sems[d], fsdp=2 * (z - 1) + c)

        def arrived_left(d, last):
            return self.copy(near.at[d], land.at[C if last else d], left_sems[d], fsdp=partner)

        def settle(d):
            own = blk(d, c)
            if stage is not None:
                load = pltpu.make_async_copy(own, stage, self.sem())
                load.start()
                load.wait()
                own = stage
            swap(d).wait_recv()
            add_into(near.at[d], near.at[d], own)
            if d > 0:
                @pl.when(z == 0)
                def _():
                    to_right(d).start()
            if d < C - 1:
                @pl.when(z == C - 1)
                def _():
                    to_left(d).start()

        for i, d in enumerate(order):
            if compute is not None:
                compute(d)
            swap(d).start()
            if i > 0 and compute is not None:
                settle(order[i - 1])
        yield
        for d in order if compute is None else order[-1:]:
            settle(d)
        for j in range(C - 1):
            yield
            d = C - 1 - j
            if d > 1:
                @pl.when((z > 0) & (z < d))
                def _():
                    to_right(d).wait_recv()
                    add_into(near.at[d], near.at[d], land.at[d])
                    to_right(d).start()
            e = j
            if e < C - 2:
                @pl.when((z < C - 1) & (z > e))
                def _():
                    arrived_left(e, False).wait_recv()
                    add_into(near.at[e], near.at[e], land.at[e])
                    to_left(e).start()
        yield
        keep(total, near.at[z])
        for d in range(C):
            if d > 0:
                @pl.when(z == d)
                def _():
                    to_right(d).wait_recv()
                    accumulate(total, land.at[d])
            if d < C - 1:
                @pl.when(z == d)
                def _():
                    arrived_left(d, True).wait_recv()
                    accumulate(total, land.at[C])
        yield
        for d in range(C):
            swap(d).wait_send()
            @pl.when(z < d)
            def _():
                to_right(d).wait_send()
            @pl.when(z > d)
            def _():
                to_left(d).wait_send()

    def exchange(self, pieces, arrivals):
        sems = {}
        for k in range(1, self.n):
            for i, (src, dst) in enumerate(pieces(self.me ^ k)):
                sems[k, i] = self.pair()
                self.copy(src, dst, sems[k, i], fsdp=self.me ^ k).start()
        yield
        for k in range(1, self.n):
            for i, (src, dst) in enumerate(arrivals(self.me ^ k)):
                self.copy(src, dst, sems[k, i], fsdp=self.me ^ k).wait_recv()
        yield
        for k in range(1, self.n):
            for i, (src, dst) in enumerate(pieces(self.me ^ k)):
                self.copy(src, dst, sems[k, i], fsdp=self.me ^ k).wait_send()

    def gather_rep(self, blk):
        sent = []
        waits = {0: [], 1: []}
        for i in range(self.bits):
            for half in (0, 1):
                b = i if half == 0 else self.bits - 1 - i
                before = [j if half == 0 else self.bits - 1 - j for j in range(i)]
                for cp in waits[half]:
                    cp.wait_recv()
                waits[half] = []
                peer = self.rep ^ (1 << b)
                for mask in range(1 << i):
                    flip = sum(((mask >> j) & 1) << before[j] for j in range(i))
                    r = self.rep ^ flip
                    sems = self.pair()
                    cp = self.copy(blk(half, r), blk(half, r), sems, rep=peer)
                    cp.start()
                    sent.append(cp)
                    waits[half].append(self.copy(blk(half, r), blk(half, r ^ (1 << b)), sems, rep=peer))
            yield
        for half in (0, 1):
            for cp in waits[half]:
                cp.wait_recv()
        yield
        for cp in sent:
            cp.wait_send()

    def scatter_rep(self, blk, land, done, stage=None):
        sent = []
        waits = {0: [], 1: []}
        nb = self.bits

        def start(half, i):
            order = list(range(nb)) if half == 0 else list(range(nb))[::-1]
            peer = self.rep ^ (1 << order[i])
            rest = order[i + 1:]
            todo = []
            for combo in range(1 << len(rest)):
                def source(own, combo=combo):
                    value = self.bit(order[i]) if own else 1 - self.bit(order[i])
                    if i == 0:
                        r = value << order[0]
                        r = r + sum(((combo >> j) & 1) << rest[j] for j in range(len(rest)))
                        return blk(half, r)
                    return land(half, i - 1, value + 2 * combo)
                sems = self.pair()
                cp = self.copy(source(False), land(half, i, combo), sems, rep=peer)
                cp.start()
                sent.append(cp)
                todo.append((cp, land(half, i, combo), source(True)))
            return todo

        for i in range(nb):
            for half in (0, 1):
                if i == 0:
                    waits[half] = start(half, 0)
            if i == 0:
                yield
            for half in (0, 1):
                for cp, ref, own in waits[half]:
                    if stage is not None and i == 0:
                        load = pltpu.make_async_copy(own, stage[half], self.sem())
                        load.start()
                        load.wait()
                        own = stage[half]
                    cp.wait_recv()
                    if i < nb - 1:
                        add_into(ref, ref, own)
                    else:
                        done(half, ref, own)
                if i < nb - 1:
                    waits[half] = start(half, i + 1)
            yield
        for cp in sent:
            cp.wait_send()


def each(ref, body):
    lead = ref.shape[:-2]
    height = 16
    while height * ref.shape[-1] < 16 * 2048 and ref.shape[-2] % (2 * height) == 0:
        height *= 2
    count = ref.shape[-2] // height
    total = count
    for size in lead:
        total *= size

    def step(t, carry):
        rows = pl.ds(pl.multiple_of((t % count) * height, height), height)
        rest = t // count
        index = []
        for size in reversed(lead):
            index.append(rest % size)
            rest = rest // size
        body(tuple(reversed(index)) + (rows,))
        return carry

    lax.fori_loop(0, total, step, 0)


def add_into(dst, a, b):
    def body(at):
        dst[at] = (a[at].astype(F32) + b[at].astype(F32)).astype(dst.dtype)

    each(dst, body)


def keep(dst, a):
    def body(at):
        dst[at] = a[at].astype(dst.dtype)

    each(dst, body)


def accumulate(dst, a):
    def body(at):
        dst[at] = dst[at] + a[at].astype(F32)

    each(dst, body)


def finish(*tasks):
    for task in tasks:
        for _ in task:
            pass


def turns(order):
    for task in order:
        next(task, None)


def cut(width):
    low = width // 256 * 128
    return ((0, low), (low, width - low))


def column_blocks(ref):
    parts = cut(ref.shape[-1])
    lead = len(ref.shape) - 3

    def blk(half, r):
        start, size = parts[half]
        return ref.at[(slice(None),) * lead + (r, slice(None), pl.ds(start, size))]

    return blk


def own_piece(kit, src_of, dst_of, stage, groups, width):
    first, second = kit.sem(), kit.sem()
    loads = [
        pltpu.make_async_copy(src_of(g), stage.at[:, pl.ds(g * width, width)], kit.sem())
        for g in range(groups)
    ]
    for cp in loads:
        cp.start()
    yield
    for cp in loads:
        cp.wait()
    store = pltpu.make_async_copy(stage, dst_of, first)
    store.start()
    yield
    store.wait()


def column_slice(start, size):
    return pl.ds(pl.multiple_of(start, 128), size)


def reshard(kit, weight, cols, stage, groups):
    n, reps, part, total = cols.shape
    width = total // groups
    rows = pl.ds(pl.multiple_of(kit.rep * part, part), part)

    def source(g, d):
        return weight.at[rows, column_slice(g * (width * n) + d * width, width)]

    def pieces(d):
        return [
            (source(g, d), cols.at[kit.me, kit.rep, :, pl.ds(g * width, width)])
            for g in range(groups)
        ]

    def arrivals(d):
        return [
            (source(g, d), cols.at[d, kit.rep, :, pl.ds(g * width, width)])
            for g in range(groups)
        ]

    own = own_piece(
        kit, lambda g: source(g, kit.me), cols.at[kit.me, kit.rep], stage, groups, width
    )
    move = kit.exchange(pieces, arrivals)
    next(move)
    next(own)
    yield
    next(own)
    next(own, None)
    next(move)
    yield
    finish(move)


def unshard(kit, sums, out, groups, only=None):
    n, part, total = sums.shape
    width = total // groups
    chosen = range(groups) if only is None else (only,)

    def target(g, d):
        return out.at[kit.rep, :, column_slice(g * (width * n) + d * width, width)]

    def pieces(d):
        return [(sums.at[d, :, pl.ds(g * width, width)], target(g, kit.me)) for g in chosen]

    def arrivals(d):
        return [(sums.at[d, :, pl.ds(g * width, width)], target(g, d)) for g in chosen]

    own = [
        pltpu.make_async_copy(src, dst, kit.sem()) for src, dst in pieces(kit.me)
    ]
    for cp in own:
        cp.start()
    move = kit.exchange(pieces, arrivals)
    next(move)
    yield
    for cp in own:
        cp.wait()
    next(move)
    yield
    finish(move)


def call(body, ins, outs, scratch, count, ident, name):
    def spec(space):
        return pl.BlockSpec(memory_space=space)

    return pl.pallas_call(
        body,
        out_shape=[jax.ShapeDtypeStruct(s, d) for s, d, _ in outs],
        in_specs=[spec(space) for _, space in ins],
        out_specs=[spec(space) for _, _, space in outs],
        scratch_shapes=list(scratch) + [pltpu.SemaphoreType.DMA((count,))],
        compiler_params=pltpu.CompilerParams(
            collective_id=ident, has_side_effects=True, vmem_limit_bytes=LIMIT
        ),
        name=name,
    )(*[a for a, _ in ins])


ANY = pl.ANY
VMEM = pltpu.VMEM


def finish_in_turn(tasks):
    tasks = list(tasks)
    done = object()
    while tasks:
        tasks = [t for t in tasks if next(t, done) is not done]


def norm_rows(dst, src):
    def body(at):
        h = src[at]
        centred = h - jnp.mean(h, axis=-1, keepdims=True)
        inv = lax.rsqrt(jnp.mean(centred * centred, axis=-1, keepdims=True) + eps)
        dst[at] = (centred * inv).astype(BF16)

    each(dst, body)


def line_lands(n, rows, width):
    return [VMEM((n // 2, rows, width), BF16), VMEM((n // 2 + 1, rows, width), BF16)]


def lands_of(shape, reps):
    lead, (part, width) = shape[:-3], shape[-2:]
    bits = reps.bit_length() - 1
    places = []
    for start, size in cut(width):
        for i in range(bits):
            places.append(VMEM((1 << (bits - 1 - i),) + lead + (part, size), BF16))
    return places


def land_in(places):
    bits = len(places) // 2

    def land(half, i, j):
        return places[half * bits + i].at[j]

    return land


def put_half(out):
    parts = cut(out.shape[-1])

    def done(half, a, b):
        start, size = parts[half]
        add_into(out.at[(slice(None),) * (len(out.shape) - 1) + (pl.ds(start, size),)], a, b)

    return done


def times_tiles(left, at_rows, right, out, transposed, tile):
    count = out.shape[1] // tile

    def step(t, carry):
        cols = pl.ds(pl.multiple_of(t * tile, tile), tile)
        if transposed:
            value = times_transpose(left[at_rows, :], right[cols, :])
        else:
            value = dot(left[at_rows, :], right[:, cols])
        out[at_rows, cols] = value.astype(BF16)
        return carry

    lax.fori_loop(0, count, step, 0)


def load_all(kit, pairs):
    copies = [pltpu.make_async_copy(src, dst, kit.sem()) for src, dst in pairs]
    for cp in copies:
        cp.start()
    return copies


def wait_all(copies):
    for cp in copies:
        cp.wait()


def project_qkv(n1, cols, cosine, sine, qkv):
    slot, total = qkv.shape
    own = total // 3
    size = 256

    def step(i, carry):
        at = pl.ds(pl.multiple_of(i * size, size), size)
        value = dot(n1[at, :], cols[...])
        for low in range(0, 2 * own, HEAD_DIM):
            part = value[:, low : low + HEAD_DIM]
            turned = part * cosine[at, :] - pltpu.roll(part, HEAD_DIM // 2, 1) * sine[at, :]
            qkv[at, low : low + HEAD_DIM] = turned.astype(BF16)
        qkv[at, 2 * own :] = value[:, 2 * own :].astype(BF16)
        return carry

    lax.fori_loop(0, slot // size, step, 0)


def attend(qkv, length, att, att_low, lse):
    slot, own = att.shape
    heads = own // HEAD_DIM
    size = min(256, slot)
    scale = HEAD_DIM ** (-0.5)
    for i in range(slot // size):
        at = slice(i * size, (i + 1) * size)
        width = (i + 1) * size
        rows = i * size + lax.broadcasted_iota(jnp.int32, (size, width), 0)
        keys = lax.broadcasted_iota(jnp.int32, (size, width), 1)
        allowed = (keys <= rows) & (keys < length)
        for head in range(heads):
            low = head * HEAD_DIM
            q = qkv[at, low : low + HEAD_DIM]
            k = qkv[:width, own + low : own + low + HEAD_DIM]
            v = qkv[:width, 2 * own + low : 2 * own + low + HEAD_DIM]
            scores = jnp.where(allowed, times_transpose(q, k) * scale, neg_big)
            top = jnp.max(scores, axis=-1, keepdims=True)
            level = top + jnp.log(jnp.sum(jnp.exp(scores - top), axis=-1, keepdims=True))
            probs = jnp.exp(scores - level).astype(BF16)
            value = dot(probs, v)
            att[at, low : low + HEAD_DIM] = value
            att_low[at, low : low + HEAD_DIM] = value.astype(BF16)
            lse[at, head:] = jnp.broadcast_to(level, (size, 128 - head))


def front_kernel(sizes, *refs):
    (length, x, w_qkv, w_in, w_out_h, cos_h, sin_h) = refs[:7]
    (hidden, qkv, att, att_low, lse, n1_full, n2_full, qkv_cols, in_cols) = refs[7:16]
    (n_low, n1, cols, w_out, cosine, sine, partial, near, land, stage, stage_in, sems) = refs[16:]
    kit = Kit(sems, sizes)
    rows = x.shape[0]
    loads = load_all(kit, [(w_out_h, w_out), (cos_h, cosine), (sin_h, sine)])

    def widen(at):
        hidden[at] = x[at].astype(F32)

    each(hidden, widen)
    norm_rows(n_low.at[0], hidden)
    kit.barrier()
    move = reshard(kit, w_qkv, qkv_cols, stage, 3)
    next(move)
    line = kit.gather_line(n_low.at[0], n1_full, rows)
    next(line)
    next(move)
    spread = kit.gather_rep(column_blocks(qkv_cols))
    next(spread)
    finish_in_turn([line, spread, move])
    move_in = reshard(kit, w_in, in_cols, stage_in, 2)
    next(move_in)
    n, reps, part, own = qkv_cols.shape
    more = [(n1_full, n1)] + [
        (qkv_cols.at[d, r], cols.at[pl.ds((d * reps + r) * part, part)]) for d in range(n) for r in range(reps)
    ]
    wait_all(loads + load_all(kit, more))
    project_qkv(n1, cols, cosine, sine, qkv)
    attend(qkv, length[0], att, att_low, lse)

    def first(d):
        times_tiles(att_low, pl.ds(d * 2 * rows, 2 * rows), w_out, partial, False, 256)

    total = kit.scatter_line(partial, hidden, rows, near, land, first)
    next(total)
    next(total)
    next(move_in)
    spread_in = kit.gather_rep(column_blocks(in_cols))
    next(spread_in)
    for _ in range(kit.chips - 2):
        next(total)
    next(spread_in)
    next(total)
    next(total)

    def body(at):
        hidden[at] = hidden[at] + x[at].astype(F32)

    each(hidden, body)
    norm_rows(n_low.at[1], hidden)
    gather = kit.gather_line(n_low.at[1], n2_full, rows)
    next(gather)
    finish_in_turn([gather, spread_in, move_in, total])


def front(sizes, length, x, w_qkv, w_in, w_out, cosine, sine):
    n, reps = sizes
    rows, width = x.shape
    slot = n * rows
    depth = w_qkv.shape[0]
    part, own_qkv, own_in = depth // reps, w_qkv.shape[1] // n, w_in.shape[1] // n
    own = w_out.shape[0]
    big = lambda *shape: VMEM(shape, BF16)
    wide = lambda *shape: VMEM(shape, F32)
    outs = call(
        functools.partial(front_kernel, sizes),
        [(length, pltpu.SMEM), (x, VMEM)]
        + [(a, ANY) for a in (w_qkv, w_in, w_out, cosine, sine)],
        [
            ((rows, width), F32, VMEM),
            ((slot, 3 * own), BF16, VMEM),
            ((slot, own), F32, VMEM),
            ((slot, own), BF16, VMEM),
            ((slot, 128), F32, VMEM),
            ((slot, width), BF16, ANY),
            ((slot, width), BF16, ANY),
            ((n, reps, part, own_qkv), BF16, ANY),
            ((n, reps, part, own_in), BF16, ANY),
        ],
        [big(2, rows, width), big(slot, width), big(n * depth, own_qkv), big(own, width)]
        + [wide(slot, 128), wide(slot, 128), big(slot, width)]
        + line_lands(n, rows, width)
        + [big(part, own_qkv), big(part, own_in)],
        64 * n, 1, "front",
    )
    return list(outs[:7]) + [o.reshape(n * depth, -1) for o in outs[7:]]


def gated(n2, cols, at, act, slopes):
    units = act.shape[1]
    tile = 256

    def step(t, carry):
        low = pl.ds(pl.multiple_of(t * tile, tile), tile)
        high = pl.ds(pl.multiple_of(units + t * tile, tile), tile)
        gate = dot(n2[at, :], cols[:, low])
        upper = dot(n2[at, :], cols[:, high])
        sigma = 1.0 / (1.0 + jnp.exp(-gate))
        silu_gate = gate * sigma
        act[at, low] = (silu_gate * upper).astype(BF16)
        slopes[at, low] = (upper * sigma * (1.0 + gate * (1.0 - sigma))).astype(BF16)
        slopes[at, high] = silu_gate.astype(BF16)
        return carry

    lax.fori_loop(0, units // tile, step, 0)


def gated_back(dy, down, at, dgu):
    units = down.shape[0]
    tile = 256

    def step(t, carry):
        low = pl.ds(pl.multiple_of(t * tile, tile), tile)
        high = pl.ds(pl.multiple_of(units + t * tile, tile), tile)
        value = times_transpose(dy[at, :], down[low, :])
        dgu[at, low] = (value * dgu[at, low].astype(F32)).astype(BF16)
        dgu[at, high] = (value * dgu[at, high].astype(F32)).astype(BF16)
        return carry

    lax.fori_loop(0, units // tile, step, 0)


def back_kernel(sizes, *refs):
    (n2_h, cols_h, down_h, hidden, dy) = refs[:5]
    (resid, branch_h, dy_full, full, s_in, s_down) = refs[5:11]
    (n2, cols, down, dy_rows, act, dgu, g_in, g_down, near, land, low) = refs[11:22]
    rest = refs[22:]
    n, reps = sizes
    rows = dy.shape[0]
    bits = reps.bit_length() - 1
    kit = Kit(rest[-1], sizes)
    loads = load_all(kit, [(n2_h, n2), (cols_h, cols)])
    later = load_all(kit, [(down_h, down)])

    def chunk(d):
        return pl.ds(d * 2 * rows, 2 * rows)

    kit.barrier()
    line_dy = kit.gather_line(dy, dy_full, rows)
    next(line_dy)
    wait_all(loads)
    for d in range(kit.chips):
        gated(n2, cols, chunk(d), act, dgu)
        if d > 0:
            next(line_dy)
    finish(line_dy)
    wait_all(later + load_all(kit, [(dy_full, dy_rows)]))
    rows_tiles(act, dy_rows, g_down, 256)
    t_down = kit.scatter_rep(
        column_blocks(g_down.reshape(reps, g_down.shape[0] // reps, g_down.shape[1])),
        land_in(rest[4 * bits : 6 * bits]),
        put_half(s_down),
    )
    next(t_down)

    def first(d):
        gated_back(dy_rows, down, chunk(d), dgu)
        times_tiles(dgu, chunk(d), cols, dy_rows, True, 256)

    total = kit.scatter_line(dy_rows, resid, rows, near, land, first)
    next(total)
    next(total)
    units = act.shape[1]
    blocks = g_in.reshape(n, reps, g_in.shape[0] // (n * reps), 2 * units)
    parts_in = []
    for g in range(2):
        window = pl.ds(g * units, units)
        rows_tiles(n2, dgu, g_in, 256, window)
        if g == 0:
            next(t_down)
        part = kit.scatter_rep(
            column_blocks(blocks.at[:, :, :, window]),
            land_in(rest[2 * g * bits : 2 * (g + 1) * bits]),
            put_half(s_in.at[:, :, window]),
        )
        next(part)
        parts_in.append(part)
        if g == 0:
            next(total)
    next(total)
    for d in range(kit.chips):
        times_tiles(act, chunk(d), down, n2, False, 256)
    for _ in range(kit.chips - 3):
        next(total)
    store = pltpu.make_async_copy(n2, branch_h, kit.sem())
    store.start()
    next(total)

    def body(at):
        h = hidden[at]
        centred = h - jnp.mean(h, axis=-1, keepdims=True)
        inv = lax.rsqrt(jnp.mean(centred * centred, axis=-1, keepdims=True) + eps)
        d = dy[at].astype(F32) + norm_back(centred * inv, inv, resid[at])
        resid[at] = d
        low[at] = d.astype(BF16)

    each(resid, body)
    line = kit.gather_line(low, full, rows)
    next(line)
    finish_in_turn([parts_in[0], line, parts_in[1], t_down, total])
    store.wait()


def back(sizes, n2_full, in_cols, w_down, hidden, dy):
    n, reps = sizes
    rows, width = dy.shape
    units = w_down.shape[0]
    g_in = (n, reps, width // (n * reps), 2 * units)
    g_down = (reps, units // reps, width)
    big = lambda *shape: VMEM(shape, BF16)
    return call(
        functools.partial(back_kernel, sizes),
        [(n2_full, ANY), (in_cols, ANY), (w_down, ANY), (hidden, VMEM), (dy, VMEM)],
        [
            ((rows, width), F32, VMEM),
            ((n * rows, width), BF16, ANY),
            ((n * rows, width), BF16, ANY),
            ((n * rows, width), BF16, ANY),
            ((n,) + g_in[2:], BF16, VMEM),
            (g_down[1:], BF16, VMEM),
        ],
        [big(n * rows, width), big(width, 2 * units), big(units, width), big(n * rows, width)]
        + [big(n * rows, units), big(n * rows, 2 * units), big(width, 2 * units), big(units, width)]
        + line_lands(n, rows, width)
        + [big(rows, width)]
        + lands_of(g_in[:3] + (units,), reps) * 2
        + lands_of(g_down, reps),
        28 * n, 3, "back",
    )


def attend_back(q, k, v, datt, att, lse, length, acc_q, acc_k, acc_v, between):
    slot, own = q.shape
    heads = own // HEAD_DIM
    size = min(256, slot)
    scale = HEAD_DIM ** (-0.5)

    def zero(at):
        for acc in (acc_q, acc_k, acc_v):
            acc[at] = jnp.zeros_like(acc[at])

    each(acc_q, zero)
    for head in range(heads):
        cols = slice(head * HEAD_DIM, (head + 1) * HEAD_DIM)

        def query_block(i, carry):
            at = pl.ds(pl.multiple_of(i * size, size), size)
            qb, db = q[at, cols], datt[at, cols]
            delta = jnp.sum(db.astype(F32) * att[at, cols], axis=-1, keepdims=True)
            level = lse[at, head : head + 1]
            rows = i * size + lax.broadcasted_iota(jnp.int32, (size, size), 0)

            def key_block(j, carry):
                there = pl.ds(pl.multiple_of(j * size, size), size)
                kb, vb = k[there, cols], v[there, cols]
                keys = j * size + lax.broadcasted_iota(jnp.int32, (size, size), 1)
                scores = times_transpose(qb, kb) * scale
                scores = jnp.where((keys <= rows) & (keys < length), scores, neg_big)
                probs = jnp.exp(scores - level)
                grads = (probs * (times_transpose(db, vb) - delta)).astype(BF16)
                acc_v[there, cols] = acc_v[there, cols] + over_rows(probs.astype(BF16), db)
                acc_k[there, cols] = acc_k[there, cols] + over_rows(grads, qb)
                acc_q[at, cols] = acc_q[at, cols] + dot(grads, kb)
                return carry

            return lax.fori_loop(0, i + 1, key_block, carry)

        lax.fori_loop(0, slot // size, query_block, 0)
        between(head)


def turn_back(acc, cosine, sine, out, start):
    slot, own = acc.shape
    scale = HEAD_DIM ** (-0.5)
    size = 128

    def step(i, carry):
        at = pl.ds(pl.multiple_of(i * size, size), size)
        for head in range(own // HEAD_DIM):
            low = head * HEAD_DIM
            value = acc[at, low : low + HEAD_DIM] * scale
            turned = value * cosine[at, :] + pltpu.roll(value, HEAD_DIM // 2, 1) * sine[at, :]
            out[at, start + low : start + low + HEAD_DIM] = turned.astype(BF16)
        return carry

    lax.fori_loop(0, slot // size, step, 0)


def rows_tiles(left, right, out, tile, window=slice(None)):
    def step(t, carry):
        cols = pl.ds(pl.multiple_of(t * tile, tile), tile)
        out[cols, window] = over_rows(left[:, cols], right[:, window]).astype(BF16)
        return carry

    lax.fori_loop(0, left.shape[1] // tile, step, 0)


def end_kernel(sizes, *refs):
    n, reps = sizes
    bits = reps.bit_length() - 1
    (length, dres_h, w_out_h, q_h, att_h, low_h, lse_h, cos_h, sin_h, cols_h, n1_h, part_h, s_in, s_down) = refs[:14]
    total_out, branch, o_in, o_down, o_qkv, o_out = refs[14:20]
    (dres, w_out, q, k, v, att, att_low, lse, cosine, sine, cols, n1, datt, acc_q, acc_k, acc_v, dqkv, g_qkv, g_out, dn1, near, land, near_b, land_b, stage, s_qkv, s_out) = refs[20:47]
    rest = refs[47:]
    rows = total_out.shape[0]
    own = q.shape[1]
    kit = Kit(rest[-1], sizes)
    loads = load_all(
        kit,
        [(dres_h, dres), (w_out_h, w_out)]
        + [(q_h.at[:, pl.ds(i * own, own)], ref) for i, ref in enumerate((q, k, v))]
        + [(att_h, att), (lse_h, lse)],
    )
    later = load_all(
        kit, [(low_h, att_low), (cos_h, cosine), (sin_h, sine), (cols_h, cols), (n1_h, n1)]
    )
    own_down = pltpu.make_async_copy(s_down, o_down.at[kit.rep], kit.sem())
    own_down.start()
    kit.barrier()
    moves_in = [unshard(kit, s_in, o_in, 2, g) for g in range(2)]
    for move in moves_in:
        next(move)
    own_down.wait()
    spread_down = kit.gather_rep(column_blocks(o_down))
    next(spread_down)
    wait_all(loads)

    def project(i, carry):
        at = pl.ds(pl.multiple_of(i * 2 * rows, 2 * rows), 2 * rows)
        datt[at, :] = times_transpose(dres[at, :], w_out[...]).astype(BF16)
        return carry

    lax.fori_loop(0, kit.chips, project, 0)
    def between(head):
        if head == 0:
            next(spread_down)

    attend_back(q, k, v, datt, att, lse, length[0], acc_q, acc_k, acc_v, between)
    wait_all(later)
    turn_back(acc_q, cosine, sine, dqkv, 0)
    turn_back(acc_k, cosine, sine, dqkv, own)

    def place(at):
        dqkv[at + (pl.ds(2 * own, own),)] = acc_v[at].astype(BF16)

    each(acc_v, place)
    rows_tiles(n1, dqkv, g_qkv, 256)
    parts = g_qkv.shape[0] // (n * reps)
    t_qkv = kit.scatter_rep(
        column_blocks(g_qkv.reshape(n, reps, parts, 3 * own)), land_in(rest[: 2 * bits]), put_half(s_qkv)
    )
    next(t_qkv)

    def first(d):
        times_tiles(dqkv, pl.ds(d * 2 * rows, 2 * rows), cols, dn1, True, 256)

    total = kit.scatter_line(dn1, total_out, rows, near, land, first)
    next(total)
    next(total)
    rows_tiles(att_low, dres, g_out, 128)
    t_out = kit.scatter_rep(
        column_blocks(g_out.reshape(reps, g_out.shape[0] // reps, g_out.shape[1])),
        land_in(rest[2 * bits : 4 * bits]),
        put_half(s_out),
    )
    next(t_out)
    units = o_in.shape[2] // 2
    spreads = []
    for g in range(2):
        next(moves_in[g])
        spread = kit.gather_rep(column_blocks(o_in.at[:, :, pl.ds(g * units, units)]))
        next(spread)
        spreads.append(spread)
    next(total)
    next(t_qkv)
    next(total)
    next(spreads[0])
    for _ in range(bits - 1):
        next(t_qkv)
    move_qkv = unshard(kit, s_qkv, o_qkv, 3)
    next(move_qkv)
    for _ in range(kit.chips - 3):
        next(total)
    next(spreads[1])
    for _ in range(bits):
        next(t_out)
    own_out = pltpu.make_async_copy(s_out, o_out.at[kit.rep], kit.sem())
    own_out.start()
    other = kit.scatter_line(part_h, branch, rows, near_b, land_b, stage=stage)
    next(other)
    next(total)
    next(other)
    own_out.wait()
    spread_out = kit.gather_rep(column_blocks(o_out))
    next(spread_out)
    next(move_qkv)
    spread_qkv = kit.gather_rep(column_blocks(o_qkv))
    next(spread_qkv)
    for _ in range(kit.chips):
        next(other)
    finish_in_turn(
        [spread_qkv, spread_out, other, total, spread_down]
        + spreads + moves_in + [move_qkv, t_qkv, t_out]
    )


def end(sizes, length, dres, w_out, qkv, att, att_low, lse, cosine, sine, cols, n1, part, s_in, s_down):
    n, reps = sizes
    slot, width = dres.shape
    rows, own = slot // n, w_out.shape[0]
    g_qkv = (n, reps, width // (n * reps), 3 * own)
    g_out = (reps, own // reps, width)
    big = lambda *shape: VMEM(shape, BF16)
    wide = lambda *shape: VMEM(shape, F32)
    any_of = [(a, ANY) for a in (dres, w_out, qkv, att, att_low, lse, cosine, sine, cols, n1, part)]
    total, branch, o_in, o_down, o_qkv, o_out = call(
        functools.partial(end_kernel, sizes),
        [(length, pltpu.SMEM)] + any_of + [(s_in, VMEM), (s_down, VMEM)],
        [
            ((rows, width), F32, VMEM),
            ((rows, width), F32, VMEM),
            ((reps, s_in.shape[1], n * s_in.shape[2]), BF16, ANY),
            ((reps,) + s_down.shape, BF16, ANY),
            ((reps, g_qkv[2], n * g_qkv[3]), BF16, ANY),
            (g_out, BF16, ANY),
        ],
        [big(slot, width), big(own, width), big(slot, own), big(slot, own), big(slot, own)]
        + [wide(slot, own), big(slot, own), wide(slot, 128), wide(slot, 128), wide(slot, 128)]
        + [big(width, 3 * own), big(slot, width), big(slot, own)]
        + [wide(slot, own)] * 3
        + [big(slot, 3 * own), big(width, 3 * own), big(own, width), big(slot, width)]
        + line_lands(n, rows, width) * 2
        + [big(rows, width), big(n, g_qkv[2], 3 * own), big(*g_out[1:])]
        + lands_of(g_qkv, reps)
        + lands_of(g_out, reps),
        32 * n, 4, "end",
    )
    return [total, branch] + [o.reshape(-1, o.shape[-1]).astype(F32) for o in (o_in, o_down, o_qkv, o_out)]


def on_device(tokens, lengths, cotangent, w_qkv, w_out, w_in, w_down):
    rows = tokens.shape[1]
    width = tokens.shape[2]
    n = lax.axis_size("fsdp")
    slot_len = rows * n
    head_dim = HEAD_DIM
    length = lengths[0]
    own_positions = lax.axis_index("fsdp") * rows + jnp.arange(rows, dtype=jnp.int32)
    valid = (own_positions < length).astype(F32)[:, None]
    positions = jnp.arange(slot_len, dtype=jnp.int32)
    cosine, sine = rotary_tables(positions, head_dim)

    sizes = (n, lax.axis_size("rep"))
    dy_rows = valid * cotangent[0].astype(F32)
    dy_low = dy_rows.astype(BF16)
    turn_cos = jnp.concatenate([cosine, cosine], axis=1)
    turn_sin = jnp.concatenate([sine, -sine], axis=1)
    hidden_in, qkv_low, attended, att_low, level, n1_full, n2_full, qkv_cols, in_cols = front(
        sizes, lengths, tokens[0], w_qkv, w_in, w_out, turn_cos, turn_sin
    )
    d_resid, branch_partial, _, dres_full, sum_in, sum_down = back(
        sizes, n2_full, in_cols, w_down, hidden_in, dy_low
    )
    d_norm1, branch, all_in, all_down, all_qkv, all_out = end(
        sizes,
        lengths,
        dres_full,
        w_out,
        qkv_low,
        attended,
        att_low,
        level,
        turn_cos,
        turn_sin,
        qkv_cols,
        n1_full,
        branch_partial,
        sum_in,
        sum_down,
    )
    output = (valid * (hidden_in + branch)).astype(BF16)
    normed1, inv1 = normalize(tokens[0].astype(F32))
    grad_tokens = (d_resid + norm_back(normed1, inv1, d_norm1)).astype(BF16)
    return (output[None], grad_tokens[None], all_qkv, all_out, all_in, all_down)


def solution(mesh):
    in_specs = (
        P("rep", "fsdp", None),
        P("rep"),
        P("rep", "fsdp", None),
        P("fsdp", None),
        P("fsdp", None),
        P("fsdp", None),
        P("fsdp", None),
    )
    out_specs = (
        P("rep", "fsdp", None),
        P("rep", "fsdp", None),
        P("fsdp", None),
        P("fsdp", None),
        P("fsdp", None),
        P("fsdp", None),
    )
    return jax.shard_map(
        on_device, mesh=mesh, in_specs=in_specs, out_specs=out_specs, check_vma=False
    )
```

```python
import functools

import jax
import jax.numpy as jnp
from jax import lax
from jax.experimental import pallas as pl
from jax.experimental.pallas import tpu as pltpu
from jax.sharding import PartitionSpec as P

HEAD_DIM = 128

eps = 1e-05
neg_big = -1e30
F32 = jnp.float32
BF16 = jnp.bfloat16


def normalize(rows):
    centred = rows - jnp.mean(rows, axis=-1, keepdims=True)
    inv_std = lax.rsqrt(jnp.mean(centred * centred, axis=-1, keepdims=True) + eps)
    return (centred * inv_std, inv_std)


def norm_back(normed, inv_std, grad):
    return inv_std * (
        grad
        - jnp.mean(grad, axis=-1, keepdims=True)
        - normed * jnp.mean(grad * normed, axis=-1, keepdims=True)
    )


def rotary_tables(positions, head_dim):
    half = head_dim // 2
    freqs = 10000.0 ** (-jnp.arange(half, dtype=F32) * 2.0 / head_dim)
    angles = positions.astype(F32)[:, None] * freqs[None, :]
    return (jnp.cos(angles), jnp.sin(angles))


def times_transpose(left, weight):
    return lax.dot_general(
        left, weight, (((1,), (1,)), ((), ())), preferred_element_type=F32
    )


def over_rows(left, right):
    return lax.dot_general(
        left, right, (((0,), (0,)), ((), ())), preferred_element_type=F32
    )


def dot(left, right):
    return jnp.dot(left, right, preferred_element_type=F32)


MESH = pl.DeviceIdType.MESH
LIMIT = 67043328


class Kit:
    def __init__(self, sems, sizes):
        self.sems = sems
        self.used = 0
        self.n, self.reps = sizes
        self.chips = self.n // 2
        self.me = lax.axis_index("fsdp")
        self.rep = lax.axis_index("rep")
        self.chip = self.me // 2
        self.core = self.me % 2
        self.bits = self.reps.bit_length() - 1

    def sem(self):
        self.used += 1
        assert self.used <= self.sems.shape[0], "semaphores"
        return self.sems.at[self.used - 1]

    def barrier(self, fsdp=True, rep=True):
        wall = pltpu.get_barrier_semaphore()
        count = 0
        if fsdp:
            for k in range(1, self.n):
                pl.semaphore_signal(wall, inc=1, device_id={"fsdp": self.me ^ k}, device_id_type=MESH)
                count += 1
        if rep:
            for b in range(self.bits):
                pl.semaphore_signal(wall, inc=1, device_id={"rep": self.rep ^ (1 << b)}, device_id_type=MESH)
                count += 1
        pl.semaphore_wait(wall, count)

    def copy(self, src, dst, sems, fsdp=None, rep=None):
        where = {"fsdp": fsdp} if rep is None else {"rep": rep}
        return pltpu.make_async_remote_copy(
            src_ref=src, dst_ref=dst, send_sem=sems[0], recv_sem=sems[1],
            device_id=where, device_id_type=MESH,
        )

    def pair(self):
        return (self.sem(), self.sem())

    def bit(self, index):
        return (self.rep >> index) & 1

    def gather_line(self, src, dst, rows):
        C, z, c = self.chips, self.chip, self.core

        def blk(chip, core):
            return dst.at[pl.ds(pl.multiple_of((2 * chip + core) * rows, rows), rows)]

        local = pltpu.make_async_copy(src, blk(z, c), self.sem())
        local.start()
        partner = self.me ^ 1
        own_sems = self.pair()
        own_pair = self.copy(src, blk(z, c), own_sems, fsdp=partner)
        other_own = blk(z, 1 - c)
        ways = []
        for sign in (1, -1):
            sends = [self.pair() for _ in range(C - 1)]
            forwards = [self.pair() for _ in range(C - 1)]
            ways.append((sign, sends, forwards))

        def inside(chip):
            return (chip >= 0) & (chip < C)

        def hop(sign, sends, k):
            shard = z - sign * k
            ref = src if k == 0 else blk(shard, c)
            return self.copy(ref, blk(shard, c), sends[k], fsdp=2 * (z + sign) + c)

        def across(sign, forwards, k):
            shard = z - sign * k
            return self.copy(blk(shard, c), blk(shard, c), forwards[k - 1], fsdp=partner)

        for sign, sends, forwards in ways:
            @pl.when(inside(z + sign))
            def _():
                hop(sign, sends, 0).start()
        own_pair.start()
        for k in range(1, C):
            yield
            for sign, sends, forwards in ways:
                @pl.when(inside(z - sign * k))
                def _():
                    shard = z - sign * k
                    self.copy(blk(shard, c), blk(shard, c), sends[k - 1], fsdp=partner).wait_recv()
                    if k < C - 1:
                        @pl.when(inside(z + sign))
                        def _():
                            hop(sign, sends, k).start()
                    across(sign, forwards, k).start()
        yield
        local.wait()
        own_pair.wait_send()
        self.copy(src, other_own, own_sems, fsdp=partner).wait_recv()
        for k in range(0, C - 1):
            for sign, sends, forwards in ways:
                @pl.when(inside(z + sign) & inside(z - sign * k))
                def _():
                    hop(sign, sends, k).wait_send()
        for k in range(1, C):
            for sign, sends, forwards in ways:
                @pl.when(inside(z - sign * k))
                def _():
                    across(sign, forwards, k).wait_send()
                    shard = z - sign * k
                    self.copy(blk(shard, c), blk(shard, 1 - c), forwards[k - 1], fsdp=partner).wait_recv()

    def scatter_line(self, partial, total, rows, near, land, compute=None, stage=None):
        C, z, c = self.chips, self.chip, self.core
        partner = self.me ^ 1

        def blk(chip, core):
            return partial.at[pl.ds(pl.multiple_of((2 * chip + core) * rows, rows), rows)]

        order = []
        for j in range(C):
            for d in (C - 1 - j, j):
                if d not in order:
                    order.append(d)
        near_sems = [self.pair() for _ in range(C)]
        right_sems = [self.pair() for _ in range(C)]
        left_sems = [self.pair() for _ in range(C)]

        def swap(d):
            return self.copy(blk(d, 1 - c), near.at[d], near_sems[d], fsdp=partner)

        def to_right(d):
            return self.copy(near.at[d], land.at[d], right_sems[d], fsdp=2 * (z + 1) + c)

        def to_left(d):
            place = jnp.where(z - 1 == d, C, d)
            return self.copy(near.at[d], land.at[place], left_sems[d], fsdp=2 * (z - 1) + c)

        def arrived_left(d, last):
            return self.copy(near.at[d], land.at[C if last else d], left_sems[d], fsdp=partner)

        def settle(d):
            own = blk(d, c)
            if stage is not None:
                load = pltpu.make_async_copy(own, stage, self.sem())
                load.start()
                load.wait()
                own = stage
            swap(d).wait_recv()
            add_into(near.at[d], near.at[d], own)
            if d > 0:
                @pl.when(z == 0)
                def _():
                    to_right(d).start()
            if d < C - 1:
                @pl.when(z == C - 1)
                def _():
                    to_left(d).start()

        for i, d in enumerate(order):
            if compute is not None:
                compute(d)
            swap(d).start()
            if i > 0 and compute is not None:
                settle(order[i - 1])
        yield
        for d in order if compute is None else order[-1:]:
            settle(d)
        for j in range(C - 1):
            yield
            d = C - 1 - j
            if d > 1:
                @pl.when((z > 0) & (z < d))
                def _():
                    to_right(d).wait_recv()
                    add_into(near.at[d], near.at[d], land.at[d])
                    to_right(d).start()
            e = j
            if e < C - 2:
                @pl.when((z < C - 1) & (z > e))
                def _():
                    arrived_left(e, False).wait_recv()
                    add_into(near.at[e], near.at[e], land.at[e])
                    to_left(e).start()
        yield
        keep(total, near.at[z])
        for d in range(C):
            if d > 0:
                @pl.when(z == d)
                def _():
                    to_right(d).wait_recv()
                    accumulate(total, land.at[d])
            if d < C - 1:
                @pl.when(z == d)
                def _():
                    arrived_left(d, True).wait_recv()
                    accumulate(total, land.at[C])
        yield
        for d in range(C):
            swap(d).wait_send()
            @pl.when(z < d)
            def _():
                to_right(d).wait_send()
            @pl.when(z > d)
            def _():
                to_left(d).wait_send()

    def exchange(self, pieces, arrivals):
        sems = {}
        for k in range(1, self.n):
            for i, (src, dst) in enumerate(pieces(self.me ^ k)):
                sems[k, i] = self.pair()
                self.copy(src, dst, sems[k, i], fsdp=self.me ^ k).start()
        yield
        for k in range(1, self.n):
            for i, (src, dst) in enumerate(arrivals(self.me ^ k)):
                self.copy(src, dst, sems[k, i], fsdp=self.me ^ k).wait_recv()
        yield
        for k in range(1, self.n):
            for i, (src, dst) in enumerate(pieces(self.me ^ k)):
                self.copy(src, dst, sems[k, i], fsdp=self.me ^ k).wait_send()

    def gather_rep(self, blk):
        sent = []
        waits = {0: [], 1: []}
        for i in range(self.bits):
            for half in (0, 1):
                b = i if half == 0 else self.bits - 1 - i
                before = [j if half == 0 else self.bits - 1 - j for j in range(i)]
                for cp in waits[half]:
                    cp.wait_recv()
                waits[half] = []
                peer = self.rep ^ (1 << b)
                for mask in range(1 << i):
                    flip = sum(((mask >> j) & 1) << before[j] for j in range(i))
                    r = self.rep ^ flip
                    sems = self.pair()
                    cp = self.copy(blk(half, r), blk(half, r), sems, rep=peer)
                    cp.start()
                    sent.append(cp)
                    waits[half].append(self.copy(blk(half, r), blk(half, r ^ (1 << b)), sems, rep=peer))
            yield
        for half in (0, 1):
            for cp in waits[half]:
                cp.wait_recv()
        yield
        for cp in sent:
            cp.wait_send()

    def scatter_rep(self, blk, land, done, stage=None):
        sent = []
        waits = {0: [], 1: []}
        nb = self.bits

        def start(half, i):
            order = list(range(nb)) if half == 0 else list(range(nb))[::-1]
            peer = self.rep ^ (1 << order[i])
            rest = order[i + 1:]
            todo = []
            for combo in range(1 << len(rest)):
                def source(own, combo=combo):
                    value = self.bit(order[i]) if own else 1 - self.bit(order[i])
                    if i == 0:
                        r = value << order[0]
                        r = r + sum(((combo >> j) & 1) << rest[j] for j in range(len(rest)))
                        return blk(half, r)
                    return land(half, i - 1, value + 2 * combo)
                sems = self.pair()
                cp = self.copy(source(False), land(half, i, combo), sems, rep=peer)
                cp.start()
                sent.append(cp)
                todo.append((cp, land(half, i, combo), source(True)))
            return todo

        for i in range(nb):
            for half in (0, 1):
                if i == 0:
                    waits[half] = start(half, 0)
            if i == 0:
                yield
            for half in (0, 1):
                for cp, ref, own in waits[half]:
                    if stage is not None and i == 0:
                        load = pltpu.make_async_copy(own, stage[half], self.sem())
                        load.start()
                        load.wait()
                        own = stage[half]
                    cp.wait_recv()
                    if i < nb - 1:
                        add_into(ref, ref, own)
                    else:
                        done(half, ref, own)
                if i < nb - 1:
                    waits[half] = start(half, i + 1)
            yield
        for cp in sent:
            cp.wait_send()


def each(ref, body):
    lead = ref.shape[:-2]
    height = 16
    while height * ref.shape[-1] < 16 * 2048 and ref.shape[-2] % (2 * height) == 0:
        height *= 2
    count = ref.shape[-2] // height
    total = count
    for size in lead:
        total *= size

    def step(t, carry):
        rows = pl.ds(pl.multiple_of((t % count) * height, height), height)
        rest = t // count
        index = []
        for size in reversed(lead):
            index.append(rest % size)
            rest = rest // size
        body(tuple(reversed(index)) + (rows,))
        return carry

    lax.fori_loop(0, total, step, 0)


def add_into(dst, a, b):
    def body(at):
        dst[at] = (a[at].astype(F32) + b[at].astype(F32)).astype(dst.dtype)

    each(dst, body)


def keep(dst, a):
    def body(at):
        dst[at] = a[at].astype(dst.dtype)

    each(dst, body)


def accumulate(dst, a):
    def body(at):
        dst[at] = dst[at] + a[at].astype(F32)

    each(dst, body)


def finish(*tasks):
    for task in tasks:
        for _ in task:
            pass


def turns(order):
    for task in order:
        next(task, None)


def cut(width):
    low = width // 256 * 128
    return ((0, low), (low, width - low))


def column_blocks(ref):
    parts = cut(ref.shape[-1])
    lead = len(ref.shape) - 3

    def blk(half, r):
        start, size = parts[half]
        return ref.at[(slice(None),) * lead + (r, slice(None), pl.ds(start, size))]

    return blk


def own_piece(kit, src_of, dst_of, stage, groups, width):
    first, second = kit.sem(), kit.sem()
    loads = [
        pltpu.make_async_copy(src_of(g), stage.at[:, pl.ds(g * width, width)], kit.sem())
        for g in range(groups)
    ]
    for cp in loads:
        cp.start()
    yield
    for cp in loads:
        cp.wait()
    store = pltpu.make_async_copy(stage, dst_of, first)
    store.start()
    yield
    store.wait()


def column_slice(start, size):
    return pl.ds(pl.multiple_of(start, 128), size)


def reshard(kit, weight, cols, stage, groups):
    n, reps, part, total = cols.shape
    width = total // groups
    rows = pl.ds(pl.multiple_of(kit.rep * part, part), part)

    def source(g, d):
        return weight.at[rows, column_slice(g * (width * n) + d * width, width)]

    def pieces(d):
        return [
            (source(g, d), cols.at[kit.me, kit.rep, :, pl.ds(g * width, width)])
            for g in range(groups)
        ]

    def arrivals(d):
        return [
            (source(g, d), cols.at[d, kit.rep, :, pl.ds(g * width, width)])
            for g in range(groups)
        ]

    own = own_piece(
        kit, lambda g: source(g, kit.me), cols.at[kit.me, kit.rep], stage, groups, width
    )
    move = kit.exchange(pieces, arrivals)
    next(move)
    next(own)
    yield
    next(own)
    next(own, None)
    next(move)
    yield
    finish(move)


def unshard(kit, sums, out, groups, only=None):
    n, part, total = sums.shape
    width = total // groups
    chosen = range(groups) if only is None else (only,)

    def target(g, d):
        return out.at[kit.rep, :, column_slice(g * (width * n) + d * width, width)]

    def pieces(d):
        return [(sums.at[d, :, pl.ds(g * width, width)], target(g, kit.me)) for g in chosen]

    def arrivals(d):
        return [(sums.at[d, :, pl.ds(g * width, width)], target(g, d)) for g in chosen]

    own = [
        pltpu.make_async_copy(src, dst, kit.sem()) for src, dst in pieces(kit.me)
    ]
    for cp in own:
        cp.start()
    move = kit.exchange(pieces, arrivals)
    next(move)
    yield
    for cp in own:
        cp.wait()
    next(move)
    yield
    finish(move)


def call(body, ins, outs, scratch, count, ident, name):
    def spec(space):
        return pl.BlockSpec(memory_space=space)

    return pl.pallas_call(
        body,
        out_shape=[jax.ShapeDtypeStruct(s, d) for s, d, _ in outs],
        in_specs=[spec(space) for _, space in ins],
        out_specs=[spec(space) for _, _, space in outs],
        scratch_shapes=list(scratch) + [pltpu.SemaphoreType.DMA((count,))],
        compiler_params=pltpu.CompilerParams(
            collective_id=ident, has_side_effects=True, vmem_limit_bytes=LIMIT
        ),
        name=name,
    )(*[a for a, _ in ins])


ANY = pl.ANY
VMEM = pltpu.VMEM


def finish_in_turn(tasks):
    tasks = list(tasks)
    done = object()
    while tasks:
        tasks = [t for t in tasks if next(t, done) is not done]


def norm_rows(dst, src):
    def body(at):
        h = src[at]
        centred = h - jnp.mean(h, axis=-1, keepdims=True)
        inv = lax.rsqrt(jnp.mean(centred * centred, axis=-1, keepdims=True) + eps)
        dst[at] = (centred * inv).astype(BF16)

    each(dst, body)


def line_lands(n, rows, width):
    return [VMEM((n // 2, rows, width), BF16), VMEM((n // 2 + 1, rows, width), BF16)]


def lands_of(shape, reps):
    lead, (part, width) = shape[:-3], shape[-2:]
    bits = reps.bit_length() - 1
    places = []
    for start, size in cut(width):
        for i in range(bits):
            places.append(VMEM((1 << (bits - 1 - i),) + lead + (part, size), BF16))
    return places


def land_in(places):
    bits = len(places) // 2

    def land(half, i, j):
        return places[half * bits + i].at[j]

    return land


def put_half(out):
    parts = cut(out.shape[-1])

    def done(half, a, b):
        start, size = parts[half]
        add_into(out.at[(slice(None),) * (len(out.shape) - 1) + (pl.ds(start, size),)], a, b)

    return done


def times_tiles(left, at_rows, right, out, transposed, tile):
    count = out.shape[1] // tile

    def step(t, carry):
        cols = pl.ds(pl.multiple_of(t * tile, tile), tile)
        if transposed:
            value = times_transpose(left[at_rows, :], right[cols, :])
        else:
            value = dot(left[at_rows, :], right[:, cols])
        out[at_rows, cols] = value.astype(BF16)
        return carry

    lax.fori_loop(0, count, step, 0)


def load_all(kit, pairs):
    copies = [pltpu.make_async_copy(src, dst, kit.sem()) for src, dst in pairs]
    for cp in copies:
        cp.start()
    return copies


def wait_all(copies):
    for cp in copies:
        cp.wait()


def project_qkv(n1, cols, cosine, sine, qkv):
    slot, total = qkv.shape
    own = total // 3
    size = 256

    def step(i, carry):
        at = pl.ds(pl.multiple_of(i * size, size), size)
        value = dot(n1[at, :], cols[...])
        for low in range(0, 2 * own, HEAD_DIM):
            part = value[:, low : low + HEAD_DIM]
            turned = part * cosine[at, :] - pltpu.roll(part, HEAD_DIM // 2, 1) * sine[at, :]
            qkv[at, low : low + HEAD_DIM] = turned.astype(BF16)
        qkv[at, 2 * own :] = value[:, 2 * own :].astype(BF16)
        return carry

    lax.fori_loop(0, slot // size, step, 0)


def attend(qkv, length, att, att_low, lse):
    slot, own = att.shape
    heads = own // HEAD_DIM
    size = min(256, slot)
    scale = HEAD_DIM ** (-0.5)
    for i in range(slot // size):
        at = slice(i * size, (i + 1) * size)
        width = (i + 1) * size
        rows = i * size + lax.broadcasted_iota(jnp.int32, (size, width), 0)
        keys = lax.broadcasted_iota(jnp.int32, (size, width), 1)
        allowed = (keys <= rows) & (keys < length)
        for head in range(heads):
            low = head * HEAD_DIM
            q = qkv[at, low : low + HEAD_DIM]
            k = qkv[:width, own + low : own + low + HEAD_DIM]
            v = qkv[:width, 2 * own + low : 2 * own + low + HEAD_DIM]
            scores = jnp.where(allowed, times_transpose(q, k) * scale, neg_big)
            top = jnp.max(scores, axis=-1, keepdims=True)
            level = top + jnp.log(jnp.sum(jnp.exp(scores - top), axis=-1, keepdims=True))
            probs = jnp.exp(scores - level).astype(BF16)
            value = dot(probs, v)
            att[at, low : low + HEAD_DIM] = value
            att_low[at, low : low + HEAD_DIM] = value.astype(BF16)
            lse[at, head:] = jnp.broadcast_to(level, (size, 128 - head))


def front_kernel(sizes, *refs):
    (length, x, w_qkv, w_in, w_out_h, cos_h, sin_h) = refs[:7]
    (hidden, qkv, att, att_low, lse, n1_full, n2_full, qkv_cols, in_cols) = refs[7:16]
    (n_low, n1, cols, w_out, cosine, sine, partial, near, land, stage, stage_in, sems) = refs[16:]
    kit = Kit(sems, sizes)
    rows = x.shape[0]
    loads = load_all(kit, [(w_out_h, w_out), (cos_h, cosine), (sin_h, sine)])

    def widen(at):
        hidden[at] = x[at].astype(F32)

    each(hidden, widen)
    norm_rows(n_low.at[0], hidden)
    kit.barrier()
    move = reshard(kit, w_qkv, qkv_cols, stage, 3)
    next(move)
    line = kit.gather_line(n_low.at[0], n1_full, rows)
    next(line)
    next(move)
    spread = kit.gather_rep(column_blocks(qkv_cols))
    next(spread)
    finish_in_turn([line, spread, move])
    move_in = reshard(kit, w_in, in_cols, stage_in, 2)
    next(move_in)
    n, reps, part, own = qkv_cols.shape
    more = [(n1_full, n1)] + [
        (qkv_cols.at[d, r], cols.at[pl.ds((d * reps + r) * part, part)]) for d in range(n) for r in range(reps)
    ]
    wait_all(loads + load_all(kit, more))
    project_qkv(n1, cols, cosine, sine, qkv)
    attend(qkv, length[0], att, att_low, lse)

    def first(d):
        times_tiles(att_low, pl.ds(d * 2 * rows, 2 * rows), w_out, partial, False, 256)

    total = kit.scatter_line(partial, hidden, rows, near, land, first)
    next(total)
    next(total)
    next(move_in)
    spread_in = kit.gather_rep(column_blocks(in_cols))
    next(spread_in)
    for _ in range(kit.chips - 2):
        next(total)
    next(spread_in)
    next(total)
    next(total)

    def body(at):
        hidden[at] = hidden[at] + x[at].astype(F32)

    each(hidden, body)
    norm_rows(n_low.at[1], hidden)
    gather = kit.gather_line(n_low.at[1], n2_full, rows)
    next(gather)
    finish_in_turn([gather, spread_in, move_in, total])


def front(sizes, length, x, w_qkv, w_in, w_out, cosine, sine):
    n, reps = sizes
    rows, width = x.shape
    slot = n * rows
    depth = w_qkv.shape[0]
    part, own_qkv, own_in = depth // reps, w_qkv.shape[1] // n, w_in.shape[1] // n
    own = w_out.shape[0]
    big = lambda *shape: VMEM(shape, BF16)
    wide = lambda *shape: VMEM(shape, F32)
    outs = call(
        functools.partial(front_kernel, sizes),
        [(length, pltpu.SMEM), (x, VMEM)]
        + [(a, ANY) for a in (w_qkv, w_in, w_out, cosine, sine)],
        [
            ((rows, width), F32, VMEM),
            ((slot, 3 * own), BF16, VMEM),
            ((slot, own), F32, VMEM),
            ((slot, own), BF16, VMEM),
            ((slot, 128), F32, VMEM),
            ((slot, width), BF16, ANY),
            ((slot, width), BF16, ANY),
            ((n, reps, part, own_qkv), BF16, ANY),
            ((n, reps, part, own_in), BF16, ANY),
        ],
        [big(2, rows, width), big(slot, width), big(n * depth, own_qkv), big(own, width)]
        + [wide(slot, 128), wide(slot, 128), big(slot, width)]
        + line_lands(n, rows, width)
        + [big(part, own_qkv), big(part, own_in)],
        64 * n, 1, "front",
    )
    return list(outs[:7]) + [o.reshape(n * depth, -1) for o in outs[7:]]


def gated(n2, cols, at, act, slopes):
    units = act.shape[1]
    tile = 256

    def step(t, carry):
        low = pl.ds(pl.multiple_of(t * tile, tile), tile)
        high = pl.ds(pl.multiple_of(units + t * tile, tile), tile)
        gate = dot(n2[at, :], cols[:, low])
        upper = dot(n2[at, :], cols[:, high])
        sigma = 1.0 / (1.0 + jnp.exp(-gate))
        silu_gate = gate * sigma
        act[at, low] = (silu_gate * upper).astype(BF16)
        slopes[at, low] = (upper * sigma * (1.0 + gate * (1.0 - sigma))).astype(BF16)
        slopes[at, high] = silu_gate.astype(BF16)
        return carry

    lax.fori_loop(0, units // tile, step, 0)


def gated_back(dy, down, at, dgu):
    units = down.shape[0]
    tile = 256

    def step(t, carry):
        low = pl.ds(pl.multiple_of(t * tile, tile), tile)
        high = pl.ds(pl.multiple_of(units + t * tile, tile), tile)
        value = times_transpose(dy[at, :], down[low, :])
        dgu[at, low] = (value * dgu[at, low].astype(F32)).astype(BF16)
        dgu[at, high] = (value * dgu[at, high].astype(F32)).astype(BF16)
        return carry

    lax.fori_loop(0, units // tile, step, 0)


def back_kernel(sizes, *refs):
    (n2_h, cols_h, down_h, hidden, dy) = refs[:5]
    (resid, branch_h, dy_full, full, s_in, s_down) = refs[5:11]
    (n2, cols, down, dy_rows, act, dgu, g_in, g_down, near, land, low) = refs[11:22]
    rest = refs[22:]
    n, reps = sizes
    rows = dy.shape[0]
    bits = reps.bit_length() - 1
    kit = Kit(rest[-1], sizes)
    loads = load_all(kit, [(n2_h, n2), (cols_h, cols)])
    later = load_all(kit, [(down_h, down)])

    def chunk(d):
        return pl.ds(d * 2 * rows, 2 * rows)

    kit.barrier()
    line_dy = kit.gather_line(dy, dy_full, rows)
    next(line_dy)
    wait_all(loads)
    for d in range(kit.chips):
        gated(n2, cols, chunk(d), act, dgu)
        if d > 0:
            next(line_dy)
    finish(line_dy)
    wait_all(later + load_all(kit, [(dy_full, dy_rows)]))
    rows_tiles(act, dy_rows, g_down, 256)
    t_down = kit.scatter_rep(
        column_blocks(g_down.reshape(reps, g_down.shape[0] // reps, g_down.shape[1])),
        land_in(rest[4 * bits : 6 * bits]),
        put_half(s_down),
    )
    next(t_down)

    def first(d):
        gated_back(dy_rows, down, chunk(d), dgu)
        times_tiles(dgu, chunk(d), cols, dy_rows, True, 256)

    total = kit.scatter_line(dy_rows, resid, rows, near, land, first)
    next(total)
    next(total)
    units = act.shape[1]
    blocks = g_in.reshape(n, reps, g_in.shape[0] // (n * reps), 2 * units)
    parts_in = []
    for g in range(2):
        window = pl.ds(g * units, units)
        rows_tiles(n2, dgu, g_in, 256, window)
        if g == 0:
            next(t_down)
        part = kit.scatter_rep(
            column_blocks(blocks.at[:, :, :, window]),
            land_in(rest[2 * g * bits : 2 * (g + 1) * bits]),
            put_half(s_in.at[:, :, window]),
        )
        next(part)
        parts_in.append(part)
        if g == 0:
            next(total)
    next(total)
    for d in range(kit.chips):
        times_tiles(act, chunk(d), down, n2, False, 256)
    for _ in range(kit.chips - 3):
        next(total)
    store = pltpu.make_async_copy(n2, branch_h, kit.sem())
    store.start()
    next(total)

    def body(at):
        h = hidden[at]
        centred = h - jnp.mean(h, axis=-1, keepdims=True)
        inv = lax.rsqrt(jnp.mean(centred * centred, axis=-1, keepdims=True) + eps)
        d = dy[at].astype(F32) + norm_back(centred * inv, inv, resid[at])
        resid[at] = d
        low[at] = d.astype(BF16)

    each(resid, body)
    line = kit.gather_line(low, full, rows)
    next(line)
    finish_in_turn([parts_in[0], line, parts_in[1], t_down, total])
    store.wait()


def back(sizes, n2_full, in_cols, w_down, hidden, dy):
    n, reps = sizes
    rows, width = dy.shape
    units = w_down.shape[0]
    g_in = (n, reps, width // (n * reps), 2 * units)
    g_down = (reps, units // reps, width)
    big = lambda *shape: VMEM(shape, BF16)
    return call(
        functools.partial(back_kernel, sizes),
        [(n2_full, ANY), (in_cols, ANY), (w_down, ANY), (hidden, VMEM), (dy, VMEM)],
        [
            ((rows, width), F32, VMEM),
            ((n * rows, width), BF16, ANY),
            ((n * rows, width), BF16, ANY),
            ((n * rows, width), BF16, ANY),
            ((n,) + g_in[2:], BF16, VMEM),
            (g_down[1:], BF16, VMEM),
        ],
        [big(n * rows, width), big(width, 2 * units), big(units, width), big(n * rows, width)]
        + [big(n * rows, units), big(n * rows, 2 * units), big(width, 2 * units), big(units, width)]
        + line_lands(n, rows, width)
        + [big(rows, width)]
        + lands_of(g_in[:3] + (units,), reps) * 2
        + lands_of(g_down, reps),
        28 * n, 3, "back",
    )


def attend_back(q, k, v, datt, att, lse, length, acc_q, acc_k, acc_v, between):
    slot, own = q.shape
    heads = own // HEAD_DIM
    size = min(256, slot)
    scale = HEAD_DIM ** (-0.5)

    def zero(at):
        for acc in (acc_q, acc_k, acc_v):
            acc[at] = jnp.zeros_like(acc[at])

    each(acc_q, zero)
    for head in range(heads):
        cols = slice(head * HEAD_DIM, (head + 1) * HEAD_DIM)

        def query_block(i, carry):
            at = pl.ds(pl.multiple_of(i * size, size), size)
            qb, db = q[at, cols], datt[at, cols]
            delta = jnp.sum(db.astype(F32) * att[at, cols], axis=-1, keepdims=True)
            level = lse[at, head : head + 1]
            rows = i * size + lax.broadcasted_iota(jnp.int32, (size, size), 0)

            def key_block(j, carry):
                there = pl.ds(pl.multiple_of(j * size, size), size)
                kb, vb = k[there, cols], v[there, cols]
                keys = j * size + lax.broadcasted_iota(jnp.int32, (size, size), 1)
                scores = times_transpose(qb, kb) * scale
                scores = jnp.where((keys <= rows) & (keys < length), scores, neg_big)
                probs = jnp.exp(scores - level)
                grads = (probs * (times_transpose(db, vb) - delta)).astype(BF16)
                acc_v[there, cols] = acc_v[there, cols] + over_rows(probs.astype(BF16), db)
                acc_k[there, cols] = acc_k[there, cols] + over_rows(grads, qb)
                acc_q[at, cols] = acc_q[at, cols] + dot(grads, kb)
                return carry

            return lax.fori_loop(0, i + 1, key_block, carry)

        lax.fori_loop(0, slot // size, query_block, 0)
        between(head)


def turn_back(acc, cosine, sine, out, start):
    slot, own = acc.shape
    scale = HEAD_DIM ** (-0.5)
    size = 128

    def step(i, carry):
        at = pl.ds(pl.multiple_of(i * size, size), size)
        for head in range(own // HEAD_DIM):
            low = head * HEAD_DIM
            value = acc[at, low : low + HEAD_DIM] * scale
            turned = value * cosine[at, :] + pltpu.roll(value, HEAD_DIM // 2, 1) * sine[at, :]
            out[at, start + low : start + low + HEAD_DIM] = turned.astype(BF16)
        return carry

    lax.fori_loop(0, slot // size, step, 0)


def rows_tiles(left, right, out, tile, window=slice(None)):
    def step(t, carry):
        cols = pl.ds(pl.multiple_of(t * tile, tile), tile)
        out[cols, window] = over_rows(left[:, cols], right[:, window]).astype(BF16)
        return carry

    lax.fori_loop(0, left.shape[1] // tile, step, 0)


def end_kernel(sizes, *refs):
    n, reps = sizes
    bits = reps.bit_length() - 1
    (length, dres_h, w_out_h, q_h, att_h, low_h, lse_h, cos_h, sin_h, cols_h, n1_h, part_h, s_in, s_down) = refs[:14]
    total_out, branch, o_in, o_down, o_qkv, o_out = refs[14:20]
    (dres, w_out, q, k, v, att, att_low, lse, cosine, sine, cols, n1, datt, acc_q, acc_k, acc_v, dqkv, g_qkv, g_out, dn1, near, land, near_b, land_b, stage, s_qkv, s_out) = refs[20:47]
    rest = refs[47:]
    rows = total_out.shape[0]
    own = q.shape[1]
    kit = Kit(rest[-1], sizes)
    loads = load_all(
        kit,
        [(dres_h, dres), (w_out_h, w_out)]
        + [(q_h.at[:, pl.ds(i * own, own)], ref) for i, ref in enumerate((q, k, v))]
        + [(att_h, att), (lse_h, lse)],
    )
    later = load_all(
        kit, [(low_h, att_low), (cos_h, cosine), (sin_h, sine), (cols_h, cols), (n1_h, n1)]
    )
    own_down = pltpu.make_async_copy(s_down, o_down.at[kit.rep], kit.sem())
    own_down.start()
    kit.barrier()
    moves_in = [unshard(kit, s_in, o_in, 2, g) for g in range(2)]
    for move in moves_in:
        next(move)
    own_down.wait()
    spread_down = kit.gather_rep(column_blocks(o_down))
    next(spread_down)
    wait_all(loads)

    def project(i, carry):
        at = pl.ds(pl.multiple_of(i * 2 * rows, 2 * rows), 2 * rows)
        datt[at, :] = times_transpose(dres[at, :], w_out[...]).astype(BF16)
        return carry

    lax.fori_loop(0, kit.chips, project, 0)
    def between(head):
        if head == 0:
            next(spread_down)

    attend_back(q, k, v, datt, att, lse, length[0], acc_q, acc_k, acc_v, between)
    wait_all(later)
    turn_back(acc_q, cosine, sine, dqkv, 0)
    turn_back(acc_k, cosine, sine, dqkv, own)

    def place(at):
        dqkv[at + (pl.ds(2 * own, own),)] = acc_v[at].astype(BF16)

    each(acc_v, place)
    rows_tiles(n1, dqkv, g_qkv, 256)
    parts = g_qkv.shape[0] // (n * reps)
    t_qkv = kit.scatter_rep(
        column_blocks(g_qkv.reshape(n, reps, parts, 3 * own)), land_in(rest[: 2 * bits]), put_half(s_qkv)
    )
    next(t_qkv)

    def first(d):
        times_tiles(dqkv, pl.ds(d * 2 * rows, 2 * rows), cols, dn1, True, 256)

    total = kit.scatter_line(dn1, total_out, rows, near, land, first)
    next(total)
    next(total)
    rows_tiles(att_low, dres, g_out, 128)
    t_out = kit.scatter_rep(
        column_blocks(g_out.reshape(reps, g_out.shape[0] // reps, g_out.shape[1])),
        land_in(rest[2 * bits : 4 * bits]),
        put_half(s_out),
    )
    next(t_out)
    next(total)
    next(t_qkv)
    next(t_out)
    units = o_in.shape[2] // 2
    spreads = []
    for g in range(2):
        next(moves_in[g])
        spread = kit.gather_rep(column_blocks(o_in.at[:, :, pl.ds(g * units, units)]))
        next(spread)
        spreads.append(spread)
    next(total)
    for _ in range(bits - 1):
        next(t_qkv)
    move_qkv = unshard(kit, s_qkv, o_qkv, 3)
    next(move_qkv)
    for _ in range(bits - 1):
        next(t_out)
    own_out = pltpu.make_async_copy(s_out, o_out.at[kit.rep], kit.sem())
    own_out.start()
    for _ in range(kit.chips - 3):
        next(total)
    other = kit.scatter_line(part_h, branch, rows, near_b, land_b, stage=stage)
    next(other)
    next(total)
    next(spreads[0])
    next(other)
    own_out.wait()
    next(move_qkv)
    spread_qkv = kit.gather_rep(column_blocks(o_qkv))
    next(spread_qkv)
    spread_out = kit.gather_rep(column_blocks(o_out))
    next(spread_out)
    next(spreads[1])
    for _ in range(kit.chips):
        next(other)
    finish_in_turn(
        [spread_qkv, spread_out, other, total, spread_down]
        + spreads + moves_in + [move_qkv, t_qkv, t_out]
    )


def end(sizes, length, dres, w_out, qkv, att, att_low, lse, cosine, sine, cols, n1, part, s_in, s_down):
    n, reps = sizes
    slot, width = dres.shape
    rows, own = slot // n, w_out.shape[0]
    g_qkv = (n, reps, width // (n * reps), 3 * own)
    g_out = (reps, own // reps, width)
    big = lambda *shape: VMEM(shape, BF16)
    wide = lambda *shape: VMEM(shape, F32)
    any_of = [(a, ANY) for a in (dres, w_out, qkv, att, att_low, lse, cosine, sine, cols, n1, part)]
    total, branch, o_in, o_down, o_qkv, o_out = call(
        functools.partial(end_kernel, sizes),
        [(length, pltpu.SMEM)] + any_of + [(s_in, VMEM), (s_down, VMEM)],
        [
            ((rows, width), F32, VMEM),
            ((rows, width), F32, VMEM),
            ((reps, s_in.shape[1], n * s_in.shape[2]), BF16, ANY),
            ((reps,) + s_down.shape, BF16, ANY),
            ((reps, g_qkv[2], n * g_qkv[3]), BF16, ANY),
            (g_out, BF16, ANY),
        ],
        [big(slot, width), big(own, width), big(slot, own), big(slot, own), big(slot, own)]
        + [wide(slot, own), big(slot, own), wide(slot, 128), wide(slot, 128), wide(slot, 128)]
        + [big(width, 3 * own), big(slot, width), big(slot, own)]
        + [wide(slot, own)] * 3
        + [big(slot, 3 * own), big(width, 3 * own), big(own, width), big(slot, width)]
        + line_lands(n, rows, width) * 2
        + [big(rows, width), big(n, g_qkv[2], 3 * own), big(*g_out[1:])]
        + lands_of(g_qkv, reps)
        + lands_of(g_out, reps),
        32 * n, 4, "end",
    )
    return [total, branch] + [o.reshape(-1, o.shape[-1]).astype(F32) for o in (o_in, o_down, o_qkv, o_out)]


def on_device(tokens, lengths, cotangent, w_qkv, w_out, w_in, w_down):
    rows = tokens.shape[1]
    width = tokens.shape[2]
    n = lax.axis_size("fsdp")
    slot_len = rows * n
    head_dim = HEAD_DIM
    length = lengths[0]
    own_positions = lax.axis_index("fsdp") * rows + jnp.arange(rows, dtype=jnp.int32)
    valid = (own_positions < length).astype(F32)[:, None]
    positions = jnp.arange(slot_len, dtype=jnp.int32)
    cosine, sine = rotary_tables(positions, head_dim)

    sizes = (n, lax.axis_size("rep"))
    dy_rows = valid * cotangent[0].astype(F32)
    dy_low = dy_rows.astype(BF16)
    turn_cos = jnp.concatenate([cosine, cosine], axis=1)
    turn_sin = jnp.concatenate([sine, -sine], axis=1)
    hidden_in, qkv_low, attended, att_low, level, n1_full, n2_full, qkv_cols, in_cols = front(
        sizes, lengths, tokens[0], w_qkv, w_in, w_out, turn_cos, turn_sin
    )
    d_resid, branch_partial, _, dres_full, sum_in, sum_down = back(
        sizes, n2_full, in_cols, w_down, hidden_in, dy_low
    )
    d_norm1, branch, all_in, all_down, all_qkv, all_out = end(
        sizes,
        lengths,
        dres_full,
        w_out,
        qkv_low,
        attended,
        att_low,
        level,
        turn_cos,
        turn_sin,
        qkv_cols,
        n1_full,
        branch_partial,
        sum_in,
        sum_down,
    )
    output = (valid * (hidden_in + branch)).astype(BF16)
    normed1, inv1 = normalize(tokens[0].astype(F32))
    grad_tokens = (d_resid + norm_back(normed1, inv1, d_norm1)).astype(BF16)
    return (output[None], grad_tokens[None], all_qkv, all_out, all_in, all_down)


def solution(mesh):
    in_specs = (
        P("rep", "fsdp", None),
        P("rep"),
        P("rep", "fsdp", None),
        P("fsdp", None),
        P("fsdp", None),
        P("fsdp", None),
        P("fsdp", None),
    )
    out_specs = (
        P("rep", "fsdp", None),
        P("rep", "fsdp", None),
        P("fsdp", None),
        P("fsdp", None),
        P("fsdp", None),
        P("fsdp", None),
    )
    return jax.shard_map(
        on_device, mesh=mesh, in_specs=in_specs, out_specs=out_specs, check_vma=False
    )
```

```python
import functools

import jax
import jax.numpy as jnp
from jax import lax
from jax.experimental import pallas as pl
from jax.experimental.pallas import tpu as pltpu
from jax.sharding import PartitionSpec as P

HEAD_DIM = 128

eps = 1e-05
neg_big = -1e30
F32 = jnp.float32
BF16 = jnp.bfloat16


def normalize(rows):
    centred = rows - jnp.mean(rows, axis=-1, keepdims=True)
    inv_std = lax.rsqrt(jnp.mean(centred * centred, axis=-1, keepdims=True) + eps)
    return (centred * inv_std, inv_std)


def norm_back(normed, inv_std, grad):
    return inv_std * (
        grad
        - jnp.mean(grad, axis=-1, keepdims=True)
        - normed * jnp.mean(grad * normed, axis=-1, keepdims=True)
    )


def rotary_tables(positions, head_dim):
    half = head_dim // 2
    freqs = 10000.0 ** (-jnp.arange(half, dtype=F32) * 2.0 / head_dim)
    angles = positions.astype(F32)[:, None] * freqs[None, :]
    return (jnp.cos(angles), jnp.sin(angles))


def times_transpose(left, weight):
    return lax.dot_general(
        left, weight, (((1,), (1,)), ((), ())), preferred_element_type=F32
    )


def over_rows(left, right):
    return lax.dot_general(
        left, right, (((0,), (0,)), ((), ())), preferred_element_type=F32
    )


def dot(left, right):
    return jnp.dot(left, right, preferred_element_type=F32)


MESH = pl.DeviceIdType.MESH
LIMIT = 67043328


class Kit:
    def __init__(self, sems, sizes):
        self.sems = sems
        self.used = 0
        self.n, self.reps = sizes
        self.chips = self.n // 2
        self.me = lax.axis_index("fsdp")
        self.rep = lax.axis_index("rep")
        self.chip = self.me // 2
        self.core = self.me % 2
        self.bits = self.reps.bit_length() - 1

    def sem(self):
        self.used += 1
        assert self.used <= self.sems.shape[0], "semaphores"
        return self.sems.at[self.used - 1]

    def barrier(self, fsdp=True, rep=True):
        wall = pltpu.get_barrier_semaphore()
        count = 0
        if fsdp:
            for k in range(1, self.n):
                pl.semaphore_signal(wall, inc=1, device_id={"fsdp": self.me ^ k}, device_id_type=MESH)
                count += 1
        if rep:
            for b in range(self.bits):
                pl.semaphore_signal(wall, inc=1, device_id={"rep": self.rep ^ (1 << b)}, device_id_type=MESH)
                count += 1
        pl.semaphore_wait(wall, count)

    def copy(self, src, dst, sems, fsdp=None, rep=None):
        where = {"fsdp": fsdp} if rep is None else {"rep": rep}
        return pltpu.make_async_remote_copy(
            src_ref=src, dst_ref=dst, send_sem=sems[0], recv_sem=sems[1],
            device_id=where, device_id_type=MESH,
        )

    def pair(self):
        return (self.sem(), self.sem())

    def bit(self, index):
        return (self.rep >> index) & 1

    def gather_line(self, src, dst, rows):
        C, z, c = self.chips, self.chip, self.core

        def blk(chip, core):
            return dst.at[pl.ds(pl.multiple_of((2 * chip + core) * rows, rows), rows)]

        local = pltpu.make_async_copy(src, blk(z, c), self.sem())
        local.start()
        partner = self.me ^ 1
        own_sems = self.pair()
        own_pair = self.copy(src, blk(z, c), own_sems, fsdp=partner)
        other_own = blk(z, 1 - c)
        ways = []
        for sign in (1, -1):
            sends = [self.pair() for _ in range(C - 1)]
            forwards = [self.pair() for _ in range(C - 1)]
            ways.append((sign, sends, forwards))

        def inside(chip):
            return (chip >= 0) & (chip < C)

        def hop(sign, sends, k):
            shard = z - sign * k
            ref = src if k == 0 else blk(shard, c)
            return self.copy(ref, blk(shard, c), sends[k], fsdp=2 * (z + sign) + c)

        def across(sign, forwards, k):
            shard = z - sign * k
            return self.copy(blk(shard, c), blk(shard, c), forwards[k - 1], fsdp=partner)

        for sign, sends, forwards in ways:
            @pl.when(inside(z + sign))
            def _():
                hop(sign, sends, 0).start()
        own_pair.start()
        for k in range(1, C):
            yield
            for sign, sends, forwards in ways:
                @pl.when(inside(z - sign * k))
                def _():
                    shard = z - sign * k
                    self.copy(blk(shard, c), blk(shard, c), sends[k - 1], fsdp=partner).wait_recv()
                    if k < C - 1:
                        @pl.when(inside(z + sign))
                        def _():
                            hop(sign, sends, k).start()
                    across(sign, forwards, k).start()
        yield
        local.wait()
        own_pair.wait_send()
        self.copy(src, other_own, own_sems, fsdp=partner).wait_recv()
        for k in range(0, C - 1):
            for sign, sends, forwards in ways:
                @pl.when(inside(z + sign) & inside(z - sign * k))
                def _():
                    hop(sign, sends, k).wait_send()
        for k in range(1, C):
            for sign, sends, forwards in ways:
                @pl.when(inside(z - sign * k))
                def _():
                    across(sign, forwards, k).wait_send()
                    shard = z - sign * k
                    self.copy(blk(shard, c), blk(shard, 1 - c), forwards[k - 1], fsdp=partner).wait_recv()

    def scatter_line(self, partial, total, rows, near, land, compute=None, stage=None):
        C, z, c = self.chips, self.chip, self.core
        partner = self.me ^ 1

        def blk(chip, core):
            return partial.at[pl.ds(pl.multiple_of((2 * chip + core) * rows, rows), rows)]

        order = []
        for j in range(C):
            for d in (C - 1 - j, j):
                if d not in order:
                    order.append(d)
        near_sems = [self.pair() for _ in range(C)]
        right_sems = [self.pair() for _ in range(C)]
        left_sems = [self.pair() for _ in range(C)]

        def swap(d):
            return self.copy(blk(d, 1 - c), near.at[d], near_sems[d], fsdp=partner)

        def to_right(d):
            return self.copy(near.at[d], land.at[d], right_sems[d], fsdp=2 * (z + 1) + c)

        def to_left(d):
            place = jnp.where(z - 1 == d, C, d)
            return self.copy(near.at[d], land.at[place], left_sems[d], fsdp=2 * (z - 1) + c)

        def arrived_left(d, last):
            return self.copy(near.at[d], land.at[C if last else d], left_sems[d], fsdp=partner)

        def settle(d):
            own = blk(d, c)
            if stage is not None:
                load = pltpu.make_async_copy(own, stage, self.sem())
                load.start()
                load.wait()
                own = stage
            swap(d).wait_recv()
            add_into(near.at[d], near.at[d], own)
            if d > 0:
                @pl.when(z == 0)
                def _():
                    to_right(d).start()
            if d < C - 1:
                @pl.when(z == C - 1)
                def _():
                    to_left(d).start()

        for i, d in enumerate(order):
            if compute is not None:
                compute(d)
            swap(d).start()
            if i > 0 and compute is not None:
                settle(order[i - 1])
        yield
        for d in order if compute is None else order[-1:]:
            settle(d)
        for j in range(C - 1):
            yield
            d = C - 1 - j
            if d > 1:
                @pl.when((z > 0) & (z < d))
                def _():
                    to_right(d).wait_recv()
                    add_into(near.at[d], near.at[d], land.at[d])
                    to_right(d).start()
            e = j
            if e < C - 2:
                @pl.when((z < C - 1) & (z > e))
                def _():
                    arrived_left(e, False).wait_recv()
                    add_into(near.at[e], near.at[e], land.at[e])
                    to_left(e).start()
        yield
        keep(total, near.at[z])
        for d in range(C):
            if d > 0:
                @pl.when(z == d)
                def _():
                    to_right(d).wait_recv()
                    accumulate(total, land.at[d])
            if d < C - 1:
                @pl.when(z == d)
                def _():
                    arrived_left(d, True).wait_recv()
                    accumulate(total, land.at[C])
        yield
        for d in range(C):
            swap(d).wait_send()
            @pl.when(z < d)
            def _():
                to_right(d).wait_send()
            @pl.when(z > d)
            def _():
                to_left(d).wait_send()

    def exchange(self, pieces, arrivals):
        sems = {}
        for k in range(1, self.n):
            for i, (src, dst) in enumerate(pieces(self.me ^ k)):
                sems[k, i] = self.pair()
                self.copy(src, dst, sems[k, i], fsdp=self.me ^ k).start()
        yield
        for k in range(1, self.n):
            for i, (src, dst) in enumerate(arrivals(self.me ^ k)):
                self.copy(src, dst, sems[k, i], fsdp=self.me ^ k).wait_recv()
        yield
        for k in range(1, self.n):
            for i, (src, dst) in enumerate(pieces(self.me ^ k)):
                self.copy(src, dst, sems[k, i], fsdp=self.me ^ k).wait_send()

    def gather_rep(self, blk):
        sent = []
        waits = {0: [], 1: []}
        for i in range(self.bits):
            for half in (0, 1):
                b = i if half == 0 else self.bits - 1 - i
                before = [j if half == 0 else self.bits - 1 - j for j in range(i)]
                for cp in waits[half]:
                    cp.wait_recv()
                waits[half] = []
                peer = self.rep ^ (1 << b)
                for mask in range(1 << i):
                    flip = sum(((mask >> j) & 1) << before[j] for j in range(i))
                    r = self.rep ^ flip
                    sems = self.pair()
                    cp = self.copy(blk(half, r), blk(half, r), sems, rep=peer)
                    cp.start()
                    sent.append(cp)
                    waits[half].append(self.copy(blk(half, r), blk(half, r ^ (1 << b)), sems, rep=peer))
            yield
        for half in (0, 1):
            for cp in waits[half]:
                cp.wait_recv()
        yield
        for cp in sent:
            cp.wait_send()

    def scatter_rep(self, blk, land, done, stage=None):
        sent = []
        waits = {0: [], 1: []}
        nb = self.bits

        def start(half, i):
            order = list(range(nb)) if half == 0 else list(range(nb))[::-1]
            peer = self.rep ^ (1 << order[i])
            rest = order[i + 1:]
            todo = []
            for combo in range(1 << len(rest)):
                def source(own, combo=combo):
                    value = self.bit(order[i]) if own else 1 - self.bit(order[i])
                    if i == 0:
                        r = value << order[0]
                        r = r + sum(((combo >> j) & 1) << rest[j] for j in range(len(rest)))
                        return blk(half, r)
                    return land(half, i - 1, value + 2 * combo)
                sems = self.pair()
                cp = self.copy(source(False), land(half, i, combo), sems, rep=peer)
                cp.start()
                sent.append(cp)
                todo.append((cp, land(half, i, combo), source(True)))
            return todo

        for i in range(nb):
            for half in (0, 1):
                if i == 0:
                    waits[half] = start(half, 0)
            if i == 0:
                yield
            for half in (0, 1):
                for cp, ref, own in waits[half]:
                    if stage is not None and i == 0:
                        load = pltpu.make_async_copy(own, stage[half], self.sem())
                        load.start()
                        load.wait()
                        own = stage[half]
                    cp.wait_recv()
                    if i < nb - 1:
                        add_into(ref, ref, own)
                    else:
                        done(half, ref, own)
                if i < nb - 1:
                    waits[half] = start(half, i + 1)
            yield
        for cp in sent:
            cp.wait_send()


def each(ref, body):
    lead = ref.shape[:-2]
    height = 16
    while height * ref.shape[-1] < 16 * 2048 and ref.shape[-2] % (2 * height) == 0:
        height *= 2
    count = ref.shape[-2] // height
    total = count
    for size in lead:
        total *= size

    def step(t, carry):
        rows = pl.ds(pl.multiple_of((t % count) * height, height), height)
        rest = t // count
        index = []
        for size in reversed(lead):
            index.append(rest % size)
            rest = rest // size
        body(tuple(reversed(index)) + (rows,))
        return carry

    lax.fori_loop(0, total, step, 0)


def add_into(dst, a, b):
    def body(at):
        dst[at] = (a[at].astype(F32) + b[at].astype(F32)).astype(dst.dtype)

    each(dst, body)


def keep(dst, a):
    def body(at):
        dst[at] = a[at].astype(dst.dtype)

    each(dst, body)


def accumulate(dst, a):
    def body(at):
        dst[at] = dst[at] + a[at].astype(F32)

    each(dst, body)


def finish(*tasks):
    for task in tasks:
        for _ in task:
            pass


def turns(order):
    for task in order:
        next(task, None)


def cut(width):
    low = width // 256 * 128
    return ((0, low), (low, width - low))


def column_blocks(ref):
    parts = cut(ref.shape[-1])
    lead = len(ref.shape) - 3

    def blk(half, r):
        start, size = parts[half]
        return ref.at[(slice(None),) * lead + (r, slice(None), pl.ds(start, size))]

    return blk


def own_piece(kit, src_of, dst_of, stage, groups, width):
    first, second = kit.sem(), kit.sem()
    loads = [
        pltpu.make_async_copy(src_of(g), stage.at[:, pl.ds(g * width, width)], kit.sem())
        for g in range(groups)
    ]
    for cp in loads:
        cp.start()
    yield
    for cp in loads:
        cp.wait()
    store = pltpu.make_async_copy(stage, dst_of, first)
    store.start()
    yield
    store.wait()


def column_slice(start, size):
    return pl.ds(pl.multiple_of(start, 128), size)


def reshard(kit, weight, cols, stage, groups):
    n, reps, part, total = cols.shape
    width = total // groups
    rows = pl.ds(pl.multiple_of(kit.rep * part, part), part)

    def source(g, d):
        return weight.at[rows, column_slice(g * (width * n) + d * width, width)]

    def pieces(d):
        return [
            (source(g, d), cols.at[kit.me, kit.rep, :, pl.ds(g * width, width)])
            for g in range(groups)
        ]

    def arrivals(d):
        return [
            (source(g, d), cols.at[d, kit.rep, :, pl.ds(g * width, width)])
            for g in range(groups)
        ]

    own = own_piece(
        kit, lambda g: source(g, kit.me), cols.at[kit.me, kit.rep], stage, groups, width
    )
    move = kit.exchange(pieces, arrivals)
    next(move)
    next(own)
    yield
    next(own)
    next(own, None)
    next(move)
    yield
    finish(move)


def unshard(kit, sums, out, groups, only=None):
    n, part, total = sums.shape
    width = total // groups
    chosen = range(groups) if only is None else (only,)

    def target(g, d):
        return out.at[kit.rep, :, column_slice(g * (width * n) + d * width, width)]

    def pieces(d):
        return [(sums.at[d, :, pl.ds(g * width, width)], target(g, kit.me)) for g in chosen]

    def arrivals(d):
        return [(sums.at[d, :, pl.ds(g * width, width)], target(g, d)) for g in chosen]

    own = [
        pltpu.make_async_copy(src, dst, kit.sem()) for src, dst in pieces(kit.me)
    ]
    for cp in own:
        cp.start()
    move = kit.exchange(pieces, arrivals)
    next(move)
    yield
    for cp in own:
        cp.wait()
    next(move)
    yield
    finish(move)


def call(body, ins, outs, scratch, count, ident, name):
    def spec(space):
        return pl.BlockSpec(memory_space=space)

    return pl.pallas_call(
        body,
        out_shape=[jax.ShapeDtypeStruct(s, d) for s, d, _ in outs],
        in_specs=[spec(space) for _, space in ins],
        out_specs=[spec(space) for _, _, space in outs],
        scratch_shapes=list(scratch) + [pltpu.SemaphoreType.DMA((count,))],
        compiler_params=pltpu.CompilerParams(
            collective_id=ident, has_side_effects=True, vmem_limit_bytes=LIMIT
        ),
        name=name,
    )(*[a for a, _ in ins])


ANY = pl.ANY
VMEM = pltpu.VMEM


def finish_in_turn(tasks):
    tasks = list(tasks)
    done = object()
    while tasks:
        tasks = [t for t in tasks if next(t, done) is not done]


def norm_rows(dst, src):
    def body(at):
        h = src[at]
        centred = h - jnp.mean(h, axis=-1, keepdims=True)
        inv = lax.rsqrt(jnp.mean(centred * centred, axis=-1, keepdims=True) + eps)
        dst[at] = (centred * inv).astype(BF16)

    each(dst, body)


def line_lands(n, rows, width):
    return [VMEM((n // 2, rows, width), BF16), VMEM((n // 2 + 1, rows, width), BF16)]


def lands_of(shape, reps):
    lead, (part, width) = shape[:-3], shape[-2:]
    bits = reps.bit_length() - 1
    places = []
    for start, size in cut(width):
        for i in range(bits):
            places.append(VMEM((1 << (bits - 1 - i),) + lead + (part, size), BF16))
    return places


def land_in(places):
    bits = len(places) // 2

    def land(half, i, j):
        return places[half * bits + i].at[j]

    return land


def put_half(out):
    parts = cut(out.shape[-1])

    def done(half, a, b):
        start, size = parts[half]
        add_into(out.at[(slice(None),) * (len(out.shape) - 1) + (pl.ds(start, size),)], a, b)

    return done


def times_tiles(left, at_rows, right, out, transposed, tile):
    count = out.shape[1] // tile

    def step(t, carry):
        cols = pl.ds(pl.multiple_of(t * tile, tile), tile)
        if transposed:
            value = times_transpose(left[at_rows, :], right[cols, :])
        else:
            value = dot(left[at_rows, :], right[:, cols])
        out[at_rows, cols] = value.astype(BF16)
        return carry

    lax.fori_loop(0, count, step, 0)


def load_all(kit, pairs):
    copies = [pltpu.make_async_copy(src, dst, kit.sem()) for src, dst in pairs]
    for cp in copies:
        cp.start()
    return copies


def wait_all(copies):
    for cp in copies:
        cp.wait()


def project_qkv(n1, cols, cosine, sine, qkv):
    slot, total = qkv.shape
    own = total // 3
    size = 256

    def step(i, carry):
        at = pl.ds(pl.multiple_of(i * size, size), size)
        value = dot(n1[at, :], cols[...])
        for low in range(0, 2 * own, HEAD_DIM):
            part = value[:, low : low + HEAD_DIM]
            turned = part * cosine[at, :] - pltpu.roll(part, HEAD_DIM // 2, 1) * sine[at, :]
            qkv[at, low : low + HEAD_DIM] = turned.astype(BF16)
        qkv[at, 2 * own :] = value[:, 2 * own :].astype(BF16)
        return carry

    lax.fori_loop(0, slot // size, step, 0)


def attend(qkv, length, att, att_low, lse):
    slot, own = att.shape
    heads = own // HEAD_DIM
    size = min(256, slot)
    scale = HEAD_DIM ** (-0.5)
    for i in range(slot // size):
        at = slice(i * size, (i + 1) * size)
        width = (i + 1) * size
        rows = i * size + lax.broadcasted_iota(jnp.int32, (size, width), 0)
        keys = lax.broadcasted_iota(jnp.int32, (size, width), 1)
        allowed = (keys <= rows) & (keys < length)
        for head in range(heads):
            low = head * HEAD_DIM
            q = qkv[at, low : low + HEAD_DIM]
            k = qkv[:width, own + low : own + low + HEAD_DIM]
            v = qkv[:width, 2 * own + low : 2 * own + low + HEAD_DIM]
            scores = jnp.where(allowed, times_transpose(q, k) * scale, neg_big)
            top = jnp.max(scores, axis=-1, keepdims=True)
            level = top + jnp.log(jnp.sum(jnp.exp(scores - top), axis=-1, keepdims=True))
            probs = jnp.exp(scores - level).astype(BF16)
            value = dot(probs, v)
            att[at, low : low + HEAD_DIM] = value
            att_low[at, low : low + HEAD_DIM] = value.astype(BF16)
            lse[at, head:] = jnp.broadcast_to(level, (size, 128 - head))


def front_kernel(sizes, *refs):
    (length, x, w_qkv, w_in, w_out_h, cos_h, sin_h) = refs[:7]
    (hidden, qkv, att, att_low, lse, n1_full, n2_full, qkv_cols, in_cols) = refs[7:16]
    (n_low, n1, cols, w_out, cosine, sine, partial, near, land, stage, stage_in, sems) = refs[16:]
    kit = Kit(sems, sizes)
    rows = x.shape[0]
    loads = load_all(kit, [(w_out_h, w_out), (cos_h, cosine), (sin_h, sine)])

    def widen(at):
        hidden[at] = x[at].astype(F32)

    each(hidden, widen)
    norm_rows(n_low.at[0], hidden)
    kit.barrier()
    move = reshard(kit, w_qkv, qkv_cols, stage, 3)
    next(move)
    line = kit.gather_line(n_low.at[0], n1_full, rows)
    next(line)
    next(move)
    spread = kit.gather_rep(column_blocks(qkv_cols))
    next(spread)
    finish_in_turn([line, spread, move])
    move_in = reshard(kit, w_in, in_cols, stage_in, 2)
    next(move_in)
    n, reps, part, own = qkv_cols.shape
    more = [(n1_full, n1)] + [
        (qkv_cols.at[d, r], cols.at[pl.ds((d * reps + r) * part, part)]) for d in range(n) for r in range(reps)
    ]
    wait_all(loads + load_all(kit, more))
    project_qkv(n1, cols, cosine, sine, qkv)
    attend(qkv, length[0], att, att_low, lse)

    def first(d):
        times_tiles(att_low, pl.ds(d * 2 * rows, 2 * rows), w_out, partial, False, 256)

    total = kit.scatter_line(partial, hidden, rows, near, land, first)
    next(total)
    next(total)
    next(move_in)
    spread_in = kit.gather_rep(column_blocks(in_cols))
    next(spread_in)
    for _ in range(kit.chips - 2):
        next(total)
    next(spread_in)
    next(total)
    next(total)

    def body(at):
        hidden[at] = hidden[at] + x[at].astype(F32)

    each(hidden, body)
    norm_rows(n_low.at[1], hidden)
    gather = kit.gather_line(n_low.at[1], n2_full, rows)
    next(gather)
    for _ in range(kit.chips - 1):
        next(gather)
    finish_in_turn([gather, spread_in, move_in, total])


def front(sizes, length, x, w_qkv, w_in, w_out, cosine, sine):
    n, reps = sizes
    rows, width = x.shape
    slot = n * rows
    depth = w_qkv.shape[0]
    part, own_qkv, own_in = depth // reps, w_qkv.shape[1] // n, w_in.shape[1] // n
    own = w_out.shape[0]
    big = lambda *shape: VMEM(shape, BF16)
    wide = lambda *shape: VMEM(shape, F32)
    outs = call(
        functools.partial(front_kernel, sizes),
        [(length, pltpu.SMEM), (x, VMEM)]
        + [(a, ANY) for a in (w_qkv, w_in, w_out, cosine, sine)],
        [
            ((rows, width), F32, VMEM),
            ((slot, 3 * own), BF16, VMEM),
            ((slot, own), F32, VMEM),
            ((slot, own), BF16, VMEM),
            ((slot, 128), F32, VMEM),
            ((slot, width), BF16, ANY),
            ((slot, width), BF16, ANY),
            ((n, reps, part, own_qkv), BF16, ANY),
            ((n, reps, part, own_in), BF16, ANY),
        ],
        [big(2, rows, width), big(slot, width), big(n * depth, own_qkv), big(own, width)]
        + [wide(slot, 128), wide(slot, 128), big(slot, width)]
        + line_lands(n, rows, width)
        + [big(part, own_qkv), big(part, own_in)],
        64 * n, 1, "front",
    )
    return list(outs[:7]) + [o.reshape(n * depth, -1) for o in outs[7:]]


def gated(n2, cols, at, act, slopes):
    units = act.shape[1]
    tile = 256

    def step(t, carry):
        low = pl.ds(pl.multiple_of(t * tile, tile), tile)
        high = pl.ds(pl.multiple_of(units + t * tile, tile), tile)
        gate = dot(n2[at, :], cols[:, low])
        upper = dot(n2[at, :], cols[:, high])
        sigma = 1.0 / (1.0 + jnp.exp(-gate))
        silu_gate = gate * sigma
        act[at, low] = (silu_gate * upper).astype(BF16)
        slopes[at, low] = (upper * sigma * (1.0 + gate * (1.0 - sigma))).astype(BF16)
        slopes[at, high] = silu_gate.astype(BF16)
        return carry

    lax.fori_loop(0, units // tile, step, 0)


def gated_back(dy, down, at, dgu):
    units = down.shape[0]
    tile = 256

    def step(t, carry):
        low = pl.ds(pl.multiple_of(t * tile, tile), tile)
        high = pl.ds(pl.multiple_of(units + t * tile, tile), tile)
        value = times_transpose(dy[at, :], down[low, :])
        dgu[at, low] = (value * dgu[at, low].astype(F32)).astype(BF16)
        dgu[at, high] = (value * dgu[at, high].astype(F32)).astype(BF16)
        return carry

    lax.fori_loop(0, units // tile, step, 0)


def back_kernel(sizes, *refs):
    (n2_h, cols_h, down_h, hidden, dy) = refs[:5]
    (resid, branch_h, dy_full, full, s_in, s_down) = refs[5:11]
    (n2, cols, down, dy_rows, act, dgu, g_in, g_down, near, land, low) = refs[11:22]
    rest = refs[22:]
    n, reps = sizes
    rows = dy.shape[0]
    bits = reps.bit_length() - 1
    kit = Kit(rest[-1], sizes)
    loads = load_all(kit, [(n2_h, n2), (cols_h, cols)])
    later = load_all(kit, [(down_h, down)])

    def chunk(d):
        return pl.ds(d * 2 * rows, 2 * rows)

    kit.barrier()
    line_dy = kit.gather_line(dy, dy_full, rows)
    next(line_dy)
    wait_all(loads)
    for d in range(kit.chips):
        gated(n2, cols, chunk(d), act, dgu)
        if d > 0:
            next(line_dy)
    finish(line_dy)
    wait_all(later + load_all(kit, [(dy_full, dy_rows)]))
    rows_tiles(act, dy_rows, g_down, 256)
    t_down = kit.scatter_rep(
        column_blocks(g_down.reshape(reps, g_down.shape[0] // reps, g_down.shape[1])),
        land_in(rest[4 * bits : 6 * bits]),
        put_half(s_down),
    )
    next(t_down)

    def first(d):
        gated_back(dy_rows, down, chunk(d), dgu)
        times_tiles(dgu, chunk(d), cols, dy_rows, True, 256)

    total = kit.scatter_line(dy_rows, resid, rows, near, land, first)
    next(total)
    next(total)
    units = act.shape[1]
    blocks = g_in.reshape(n, reps, g_in.shape[0] // (n * reps), 2 * units)
    parts_in = []
    for g in range(2):
        window = pl.ds(g * units, units)
        if g == 0:
            next(t_down)
        rows_tiles(n2, dgu, g_in, 256, window)
        part = kit.scatter_rep(
            column_blocks(blocks.at[:, :, :, window]),
            land_in(rest[2 * g * bits : 2 * (g + 1) * bits]),
            put_half(s_in.at[:, :, window]),
        )
        next(part)
        parts_in.append(part)
        if g == 0:
            next(total)
    next(total)
    for d in range(kit.chips):
        times_tiles(act, chunk(d), down, n2, False, 256)
    for _ in range(kit.chips - 3):
        next(total)
    store = pltpu.make_async_copy(n2, branch_h, kit.sem())
    store.start()
    next(total)

    def body(at):
        h = hidden[at]
        centred = h - jnp.mean(h, axis=-1, keepdims=True)
        inv = lax.rsqrt(jnp.mean(centred * centred, axis=-1, keepdims=True) + eps)
        d = dy[at].astype(F32) + norm_back(centred * inv, inv, resid[at])
        resid[at] = d
        low[at] = d.astype(BF16)

    each(resid, body)
    line = kit.gather_line(low, full, rows)
    next(line)
    next(parts_in[0])
    next(line)
    next(line)
    next(parts_in[1])
    for _ in range(kit.chips - 3):
        next(line)
    finish_in_turn([parts_in[0], t_down, line, parts_in[1], total])
    store.wait()


def back(sizes, n2_full, in_cols, w_down, hidden, dy):
    n, reps = sizes
    rows, width = dy.shape
    units = w_down.shape[0]
    g_in = (n, reps, width // (n * reps), 2 * units)
    g_down = (reps, units // reps, width)
    big = lambda *shape: VMEM(shape, BF16)
    return call(
        functools.partial(back_kernel, sizes),
        [(n2_full, ANY), (in_cols, ANY), (w_down, ANY), (hidden, VMEM), (dy, VMEM)],
        [
            ((rows, width), F32, VMEM),
            ((n * rows, width), BF16, ANY),
            ((n * rows, width), BF16, ANY),
            ((n * rows, width), BF16, ANY),
            ((n,) + g_in[2:], BF16, VMEM),
            (g_down[1:], BF16, VMEM),
        ],
        [big(n * rows, width), big(width, 2 * units), big(units, width), big(n * rows, width)]
        + [big(n * rows, units), big(n * rows, 2 * units), big(width, 2 * units), big(units, width)]
        + line_lands(n, rows, width)
        + [big(rows, width)]
        + lands_of(g_in[:3] + (units,), reps) * 2
        + lands_of(g_down, reps),
        28 * n, 3, "back",
    )


def attend_back(q, k, v, datt, att, lse, length, acc_q, acc_k, acc_v, between):
    slot, own = q.shape
    heads = own // HEAD_DIM
    size = min(256, slot)
    scale = HEAD_DIM ** (-0.5)

    def zero(at):
        for acc in (acc_q, acc_k, acc_v):
            acc[at] = jnp.zeros_like(acc[at])

    each(acc_q, zero)
    for head in range(heads):
        cols = slice(head * HEAD_DIM, (head + 1) * HEAD_DIM)

        def query_block(i, carry):
            at = pl.ds(pl.multiple_of(i * size, size), size)
            qb, db = q[at, cols], datt[at, cols]
            delta = jnp.sum(db.astype(F32) * att[at, cols], axis=-1, keepdims=True)
            level = lse[at, head : head + 1]
            rows = i * size + lax.broadcasted_iota(jnp.int32, (size, size), 0)

            def key_block(j, carry):
                there = pl.ds(pl.multiple_of(j * size, size), size)
                kb, vb = k[there, cols], v[there, cols]
                keys = j * size + lax.broadcasted_iota(jnp.int32, (size, size), 1)
                scores = times_transpose(qb, kb) * scale
                scores = jnp.where((keys <= rows) & (keys < length), scores, neg_big)
                probs = jnp.exp(scores - level)
                grads = (probs * (times_transpose(db, vb) - delta)).astype(BF16)
                acc_v[there, cols] = acc_v[there, cols] + over_rows(probs.astype(BF16), db)
                acc_k[there, cols] = acc_k[there, cols] + over_rows(grads, qb)
                acc_q[at, cols] = acc_q[at, cols] + dot(grads, kb)
                return carry

            return lax.fori_loop(0, i + 1, key_block, carry)

        lax.fori_loop(0, slot // size, query_block, 0)
        between(head)


def turn_back(acc, cosine, sine, out, start):
    slot, own = acc.shape
    scale = HEAD_DIM ** (-0.5)
    size = 128

    def step(i, carry):
        at = pl.ds(pl.multiple_of(i * size, size), size)
        for head in range(own // HEAD_DIM):
            low = head * HEAD_DIM
            value = acc[at, low : low + HEAD_DIM] * scale
            turned = value * cosine[at, :] + pltpu.roll(value, HEAD_DIM // 2, 1) * sine[at, :]
            out[at, start + low : start + low + HEAD_DIM] = turned.astype(BF16)
        return carry

    lax.fori_loop(0, slot // size, step, 0)


def rows_tiles(left, right, out, tile, window=slice(None)):
    def step(t, carry):
        cols = pl.ds(pl.multiple_of(t * tile, tile), tile)
        out[cols, window] = over_rows(left[:, cols], right[:, window]).astype(BF16)
        return carry

    lax.fori_loop(0, left.shape[1] // tile, step, 0)


def end_kernel(sizes, *refs):
    n, reps = sizes
    bits = reps.bit_length() - 1
    (length, dres_h, w_out_h, q_h, att_h, low_h, lse_h, cos_h, sin_h, cols_h, n1_h, part_h, s_in, s_down) = refs[:14]
    total_out, branch, o_in, o_down, o_qkv, o_out = refs[14:20]
    (dres, w_out, q, k, v, att, att_low, lse, cosine, sine, cols, n1, datt, acc_q, acc_k, acc_v, dqkv, g_qkv, g_out, dn1, near, land, near_b, land_b, stage, s_qkv, s_out) = refs[20:47]
    rest = refs[47:]
    rows = total_out.shape[0]
    own = q.shape[1]
    kit = Kit(rest[-1], sizes)
    loads = load_all(
        kit,
        [(dres_h, dres), (w_out_h, w_out)]
        + [(q_h.at[:, pl.ds(i * own, own)], ref) for i, ref in enumerate((q, k, v))]
        + [(att_h, att), (lse_h, lse)],
    )
    later = load_all(
        kit, [(low_h, att_low), (cos_h, cosine), (sin_h, sine), (cols_h, cols), (n1_h, n1)]
    )
    own_down = pltpu.make_async_copy(s_down, o_down.at[kit.rep], kit.sem())
    own_down.start()
    kit.barrier()
    moves_in = [unshard(kit, s_in, o_in, 2, g) for g in range(2)]
    for move in moves_in:
        next(move)
    own_down.wait()
    spread_down = kit.gather_rep(column_blocks(o_down))
    next(spread_down)
    wait_all(loads)

    def project(i, carry):
        at = pl.ds(pl.multiple_of(i * 2 * rows, 2 * rows), 2 * rows)
        datt[at, :] = times_transpose(dres[at, :], w_out[...]).astype(BF16)
        return carry

    lax.fori_loop(0, kit.chips, project, 0)
    def between(head):
        if head == 0:
            next(spread_down)

    attend_back(q, k, v, datt, att, lse, length[0], acc_q, acc_k, acc_v, between)
    wait_all(later)
    turn_back(acc_q, cosine, sine, dqkv, 0)
    turn_back(acc_k, cosine, sine, dqkv, own)

    def place(at):
        dqkv[at + (pl.ds(2 * own, own),)] = acc_v[at].astype(BF16)

    each(acc_v, place)
    rows_tiles(n1, dqkv, g_qkv, 256)
    parts = g_qkv.shape[0] // (n * reps)
    t_qkv = kit.scatter_rep(
        column_blocks(g_qkv.reshape(n, reps, parts, 3 * own)), land_in(rest[: 2 * bits]), put_half(s_qkv)
    )
    next(t_qkv)

    def first(d):
        times_tiles(dqkv, pl.ds(d * 2 * rows, 2 * rows), cols, dn1, True, 256)

    total = kit.scatter_line(dn1, total_out, rows, near, land, first)
    next(total)
    next(total)
    rows_tiles(att_low, dres, g_out, 128)
    t_out = kit.scatter_rep(
        column_blocks(g_out.reshape(reps, g_out.shape[0] // reps, g_out.shape[1])),
        land_in(rest[2 * bits : 4 * bits]),
        put_half(s_out),
    )
    next(t_out)
    next(total)
    next(t_qkv)
    next(t_out)
    units = o_in.shape[2] // 2
    spreads = []
    for g in range(2):
        next(moves_in[g])
        spread = kit.gather_rep(column_blocks(o_in.at[:, :, pl.ds(g * units, units)]))
        next(spread)
        spreads.append(spread)
    next(total)
    for _ in range(bits - 1):
        next(t_qkv)
    move_qkv = unshard(kit, s_qkv, o_qkv, 3)
    next(move_qkv)
    for _ in range(bits - 1):
        next(t_out)
    own_out = pltpu.make_async_copy(s_out, o_out.at[kit.rep], kit.sem())
    own_out.start()
    for _ in range(kit.chips - 3):
        next(total)
    other = kit.scatter_line(part_h, branch, rows, near_b, land_b, stage=stage)
    next(other)
    next(total)
    next(spreads[0])
    next(other)
    own_out.wait()
    next(move_qkv)
    spread_qkv = kit.gather_rep(column_blocks(o_qkv))
    next(spread_qkv)
    spread_out = kit.gather_rep(column_blocks(o_out))
    next(spread_out)
    next(spreads[1])
    for _ in range(kit.chips):
        next(other)
    finish_in_turn(
        [spread_qkv, spread_out, other, total, spread_down]
        + spreads + moves_in + [move_qkv, t_qkv, t_out]
    )


def end(sizes, length, dres, w_out, qkv, att, att_low, lse, cosine, sine, cols, n1, part, s_in, s_down):
    n, reps = sizes
    slot, width = dres.shape
    rows, own = slot // n, w_out.shape[0]
    g_qkv = (n, reps, width // (n * reps), 3 * own)
    g_out = (reps, own // reps, width)
    big = lambda *shape: VMEM(shape, BF16)
    wide = lambda *shape: VMEM(shape, F32)
    any_of = [(a, ANY) for a in (dres, w_out, qkv, att, att_low, lse, cosine, sine, cols, n1, part)]
    total, branch, o_in, o_down, o_qkv, o_out = call(
        functools.partial(end_kernel, sizes),
        [(length, pltpu.SMEM)] + any_of + [(s_in, VMEM), (s_down, VMEM)],
        [
            ((rows, width), F32, VMEM),
            ((rows, width), F32, VMEM),
            ((reps, s_in.shape[1], n * s_in.shape[2]), BF16, ANY),
            ((reps,) + s_down.shape, BF16, ANY),
            ((reps, g_qkv[2], n * g_qkv[3]), BF16, ANY),
            (g_out, BF16, ANY),
        ],
        [big(slot, width), big(own, width), big(slot, own), big(slot, own), big(slot, own)]
        + [wide(slot, own), big(slot, own), wide(slot, 128), wide(slot, 128), wide(slot, 128)]
        + [big(width, 3 * own), big(slot, width), big(slot, own)]
        + [wide(slot, own)] * 3
        + [big(slot, 3 * own), big(width, 3 * own), big(own, width), big(slot, width)]
        + line_lands(n, rows, width) * 2
        + [big(rows, width), big(n, g_qkv[2], 3 * own), big(*g_out[1:])]
        + lands_of(g_qkv, reps)
        + lands_of(g_out, reps),
        32 * n, 4, "end",
    )
    return [total, branch] + [o.reshape(-1, o.shape[-1]).astype(F32) for o in (o_in, o_down, o_qkv, o_out)]


def on_device(tokens, lengths, cotangent, w_qkv, w_out, w_in, w_down):
    rows = tokens.shape[1]
    width = tokens.shape[2]
    n = lax.axis_size("fsdp")
    slot_len = rows * n
    head_dim = HEAD_DIM
    length = lengths[0]
    own_positions = lax.axis_index("fsdp") * rows + jnp.arange(rows, dtype=jnp.int32)
    valid = (own_positions < length).astype(F32)[:, None]
    positions = jnp.arange(slot_len, dtype=jnp.int32)
    cosine, sine = rotary_tables(positions, head_dim)

    sizes = (n, lax.axis_size("rep"))
    dy_rows = valid * cotangent[0].astype(F32)
    dy_low = dy_rows.astype(BF16)
    turn_cos = jnp.concatenate([cosine, cosine], axis=1)
    turn_sin = jnp.concatenate([sine, -sine], axis=1)
    hidden_in, qkv_low, attended, att_low, level, n1_full, n2_full, qkv_cols, in_cols = front(
        sizes, lengths, tokens[0], w_qkv, w_in, w_out, turn_cos, turn_sin
    )
    d_resid, branch_partial, _, dres_full, sum_in, sum_down = back(
        sizes, n2_full, in_cols, w_down, hidden_in, dy_low
    )
    d_norm1, branch, all_in, all_down, all_qkv, all_out = end(
        sizes,
        lengths,
        dres_full,
        w_out,
        qkv_low,
        attended,
        att_low,
        level,
        turn_cos,
        turn_sin,
        qkv_cols,
        n1_full,
        branch_partial,
        sum_in,
        sum_down,
    )
    output = (valid * (hidden_in + branch)).astype(BF16)
    normed1, inv1 = normalize(tokens[0].astype(F32))
    grad_tokens = (d_resid + norm_back(normed1, inv1, d_norm1)).astype(BF16)
    return (output[None], grad_tokens[None], all_qkv, all_out, all_in, all_down)


def solution(mesh):
    in_specs = (
        P("rep", "fsdp", None),
        P("rep"),
        P("rep", "fsdp", None),
        P("fsdp", None),
        P("fsdp", None),
        P("fsdp", None),
        P("fsdp", None),
    )
    out_specs = (
        P("rep", "fsdp", None),
        P("rep", "fsdp", None),
        P("fsdp", None),
        P("fsdp", None),
        P("fsdp", None),
        P("fsdp", None),
    )
    return jax.shard_map(
        on_device, mesh=mesh, in_specs=in_specs, out_specs=out_specs, check_vma=False
    )
```

```python
import functools

import jax
import jax.numpy as jnp
from jax import lax
from jax.experimental import pallas as pl
from jax.experimental.pallas import tpu as pltpu
from jax.sharding import PartitionSpec as P

HEAD_DIM = 128

eps = 1e-05
neg_big = -1e30
F32 = jnp.float32
BF16 = jnp.bfloat16


def normalize(rows):
    centred = rows - jnp.mean(rows, axis=-1, keepdims=True)
    inv_std = lax.rsqrt(jnp.mean(centred * centred, axis=-1, keepdims=True) + eps)
    return (centred * inv_std, inv_std)


def norm_back(normed, inv_std, grad):
    return inv_std * (
        grad
        - jnp.mean(grad, axis=-1, keepdims=True)
        - normed * jnp.mean(grad * normed, axis=-1, keepdims=True)
    )


def rotary_tables(positions, head_dim):
    half = head_dim // 2
    freqs = 10000.0 ** (-jnp.arange(half, dtype=F32) * 2.0 / head_dim)
    angles = positions.astype(F32)[:, None] * freqs[None, :]
    return (jnp.cos(angles), jnp.sin(angles))


def times_transpose(left, weight):
    return lax.dot_general(
        left, weight, (((1,), (1,)), ((), ())), preferred_element_type=F32
    )


def over_rows(left, right):
    return lax.dot_general(
        left, right, (((0,), (0,)), ((), ())), preferred_element_type=F32
    )


def dot(left, right):
    return jnp.dot(left, right, preferred_element_type=F32)


MESH = pl.DeviceIdType.MESH
LIMIT = 67043328


class Kit:
    def __init__(self, sems, sizes):
        self.sems = sems
        self.used = 0
        self.n, self.reps = sizes
        self.chips = self.n // 2
        self.me = lax.axis_index("fsdp")
        self.rep = lax.axis_index("rep")
        self.chip = self.me // 2
        self.core = self.me % 2
        self.bits = self.reps.bit_length() - 1

    def sem(self):
        self.used += 1
        assert self.used <= self.sems.shape[0], "semaphores"
        return self.sems.at[self.used - 1]

    def barrier(self, fsdp=True, rep=True):
        wall = pltpu.get_barrier_semaphore()
        count = 0
        if fsdp:
            for k in range(1, self.n):
                pl.semaphore_signal(wall, inc=1, device_id={"fsdp": self.me ^ k}, device_id_type=MESH)
                count += 1
        if rep:
            for b in range(self.bits):
                pl.semaphore_signal(wall, inc=1, device_id={"rep": self.rep ^ (1 << b)}, device_id_type=MESH)
                count += 1
        pl.semaphore_wait(wall, count)

    def copy(self, src, dst, sems, fsdp=None, rep=None):
        where = {"fsdp": fsdp} if rep is None else {"rep": rep}
        return pltpu.make_async_remote_copy(
            src_ref=src, dst_ref=dst, send_sem=sems[0], recv_sem=sems[1],
            device_id=where, device_id_type=MESH,
        )

    def pair(self):
        return (self.sem(), self.sem())

    def bit(self, index):
        return (self.rep >> index) & 1

    def gather_line(self, src, dst, rows):
        C, z, c = self.chips, self.chip, self.core

        def blk(chip, core):
            return dst.at[pl.ds(pl.multiple_of((2 * chip + core) * rows, rows), rows)]

        local = pltpu.make_async_copy(src, blk(z, c), self.sem())
        local.start()
        partner = self.me ^ 1
        own_sems = self.pair()
        own_pair = self.copy(src, blk(z, c), own_sems, fsdp=partner)
        other_own = blk(z, 1 - c)
        ways = []
        for sign in (1, -1):
            sends = [self.pair() for _ in range(C - 1)]
            forwards = [self.pair() for _ in range(C - 1)]
            ways.append((sign, sends, forwards))

        def inside(chip):
            return (chip >= 0) & (chip < C)

        def hop(sign, sends, k):
            shard = z - sign * k
            ref = src if k == 0 else blk(shard, c)
            return self.copy(ref, blk(shard, c), sends[k], fsdp=2 * (z + sign) + c)

        def across(sign, forwards, k):
            shard = z - sign * k
            return self.copy(blk(shard, c), blk(shard, c), forwards[k - 1], fsdp=partner)

        for sign, sends, forwards in ways:
            @pl.when(inside(z + sign))
            def _():
                hop(sign, sends, 0).start()
        own_pair.start()
        for k in range(1, C):
            yield
            for sign, sends, forwards in ways:
                @pl.when(inside(z - sign * k))
                def _():
                    shard = z - sign * k
                    self.copy(blk(shard, c), blk(shard, c), sends[k - 1], fsdp=partner).wait_recv()
                    if k < C - 1:
                        @pl.when(inside(z + sign))
                        def _():
                            hop(sign, sends, k).start()
                    across(sign, forwards, k).start()
        yield
        local.wait()
        own_pair.wait_send()
        self.copy(src, other_own, own_sems, fsdp=partner).wait_recv()
        for k in range(0, C - 1):
            for sign, sends, forwards in ways:
                @pl.when(inside(z + sign) & inside(z - sign * k))
                def _():
                    hop(sign, sends, k).wait_send()
        for k in range(1, C):
            for sign, sends, forwards in ways:
                @pl.when(inside(z - sign * k))
                def _():
                    across(sign, forwards, k).wait_send()
                    shard = z - sign * k
                    self.copy(blk(shard, c), blk(shard, 1 - c), forwards[k - 1], fsdp=partner).wait_recv()

    def scatter_line(self, partial, total, rows, near, land, compute=None, stage=None):
        C, z, c = self.chips, self.chip, self.core
        partner = self.me ^ 1

        def blk(chip, core):
            return partial.at[pl.ds(pl.multiple_of((2 * chip + core) * rows, rows), rows)]

        order = []
        for j in range(C):
            for d in (C - 1 - j, j):
                if d not in order:
                    order.append(d)
        near_sems = [self.pair() for _ in range(C)]
        right_sems = [self.pair() for _ in range(C)]
        left_sems = [self.pair() for _ in range(C)]

        def swap(d):
            return self.copy(blk(d, 1 - c), near.at[d], near_sems[d], fsdp=partner)

        def to_right(d):
            return self.copy(near.at[d], land.at[d], right_sems[d], fsdp=2 * (z + 1) + c)

        def to_left(d):
            place = jnp.where(z - 1 == d, C, d)
            return self.copy(near.at[d], land.at[place], left_sems[d], fsdp=2 * (z - 1) + c)

        def arrived_left(d, last):
            return self.copy(near.at[d], land.at[C if last else d], left_sems[d], fsdp=partner)

        def settle(d):
            own = blk(d, c)
            if stage is not None:
                load = pltpu.make_async_copy(own, stage, self.sem())
                load.start()
                load.wait()
                own = stage
            swap(d).wait_recv()
            add_into(near.at[d], near.at[d], own)
            if d > 0:
                @pl.when(z == 0)
                def _():
                    to_right(d).start()
            if d < C - 1:
                @pl.when(z == C - 1)
                def _():
                    to_left(d).start()

        for i, d in enumerate(order):
            if compute is not None:
                compute(d)
            swap(d).start()
            if i > 0 and compute is not None:
                settle(order[i - 1])
        yield
        for d in order if compute is None else order[-1:]:
            settle(d)
        for j in range(C - 1):
            yield
            d = C - 1 - j
            if d > 1:
                @pl.when((z > 0) & (z < d))
                def _():
                    to_right(d).wait_recv()
                    add_into(near.at[d], near.at[d], land.at[d])
                    to_right(d).start()
            e = j
            if e < C - 2:
                @pl.when((z < C - 1) & (z > e))
                def _():
                    arrived_left(e, False).wait_recv()
                    add_into(near.at[e], near.at[e], land.at[e])
                    to_left(e).start()
        yield
        keep(total, near.at[z])
        for d in range(C):
            if d > 0:
                @pl.when(z == d)
                def _():
                    to_right(d).wait_recv()
                    accumulate(total, land.at[d])
            if d < C - 1:
                @pl.when(z == d)
                def _():
                    arrived_left(d, True).wait_recv()
                    accumulate(total, land.at[C])
        yield
        for d in range(C):
            swap(d).wait_send()
            @pl.when(z < d)
            def _():
                to_right(d).wait_send()
            @pl.when(z > d)
            def _():
                to_left(d).wait_send()

    def exchange(self, pieces, arrivals):
        sems = {}
        for k in range(1, self.n):
            for i, (src, dst) in enumerate(pieces(self.me ^ k)):
                sems[k, i] = self.pair()
                self.copy(src, dst, sems[k, i], fsdp=self.me ^ k).start()
        yield
        for k in range(1, self.n):
            for i, (src, dst) in enumerate(arrivals(self.me ^ k)):
                self.copy(src, dst, sems[k, i], fsdp=self.me ^ k).wait_recv()
        yield
        for k in range(1, self.n):
            for i, (src, dst) in enumerate(pieces(self.me ^ k)):
                self.copy(src, dst, sems[k, i], fsdp=self.me ^ k).wait_send()

    def gather_rep(self, blk):
        sent = []
        waits = {0: [], 1: []}
        for i in range(self.bits):
            for half in (0, 1):
                b = i if half == 0 else self.bits - 1 - i
                before = [j if half == 0 else self.bits - 1 - j for j in range(i)]
                for cp in waits[half]:
                    cp.wait_recv()
                waits[half] = []
                peer = self.rep ^ (1 << b)
                for mask in range(1 << i):
                    flip = sum(((mask >> j) & 1) << before[j] for j in range(i))
                    r = self.rep ^ flip
                    sems = self.pair()
                    cp = self.copy(blk(half, r), blk(half, r), sems, rep=peer)
                    cp.start()
                    sent.append(cp)
                    waits[half].append(self.copy(blk(half, r), blk(half, r ^ (1 << b)), sems, rep=peer))
            yield
        for half in (0, 1):
            for cp in waits[half]:
                cp.wait_recv()
        yield
        for cp in sent:
            cp.wait_send()

    def scatter_rep(self, blk, land, done, stage=None):
        sent = []
        waits = {0: [], 1: []}
        nb = self.bits

        def start(half, i):
            order = list(range(nb)) if half == 0 else list(range(nb))[::-1]
            peer = self.rep ^ (1 << order[i])
            rest = order[i + 1:]
            todo = []
            for combo in range(1 << len(rest)):
                def source(own, combo=combo):
                    value = self.bit(order[i]) if own else 1 - self.bit(order[i])
                    if i == 0:
                        r = value << order[0]
                        r = r + sum(((combo >> j) & 1) << rest[j] for j in range(len(rest)))
                        return blk(half, r)
                    return land(half, i - 1, value + 2 * combo)
                sems = self.pair()
                cp = self.copy(source(False), land(half, i, combo), sems, rep=peer)
                cp.start()
                sent.append(cp)
                todo.append((cp, land(half, i, combo), source(True)))
            return todo

        for i in range(nb):
            for half in (0, 1):
                if i == 0:
                    waits[half] = start(half, 0)
            if i == 0:
                yield
            for half in (0, 1):
                for cp, ref, own in waits[half]:
                    if stage is not None and i == 0:
                        load = pltpu.make_async_copy(own, stage[half], self.sem())
                        load.start()
                        load.wait()
                        own = stage[half]
                    cp.wait_recv()
                    if i < nb - 1:
                        add_into(ref, ref, own)
                    else:
                        done(half, ref, own)
                if i < nb - 1:
                    waits[half] = start(half, i + 1)
            yield
        for cp in sent:
            cp.wait_send()


def each(ref, body):
    lead = ref.shape[:-2]
    height = 16
    while height * ref.shape[-1] < 16 * 2048 and ref.shape[-2] % (2 * height) == 0:
        height *= 2
    count = ref.shape[-2] // height
    total = count
    for size in lead:
        total *= size

    def step(t, carry):
        rows = pl.ds(pl.multiple_of((t % count) * height, height), height)
        rest = t // count
        index = []
        for size in reversed(lead):
            index.append(rest % size)
            rest = rest // size
        body(tuple(reversed(index)) + (rows,))
        return carry

    lax.fori_loop(0, total, step, 0)


def add_into(dst, a, b):
    def body(at):
        dst[at] = (a[at].astype(F32) + b[at].astype(F32)).astype(dst.dtype)

    each(dst, body)


def keep(dst, a):
    def body(at):
        dst[at] = a[at].astype(dst.dtype)

    each(dst, body)


def accumulate(dst, a):
    def body(at):
        dst[at] = dst[at] + a[at].astype(F32)

    each(dst, body)


def finish(*tasks):
    for task in tasks:
        for _ in task:
            pass


def turns(order):
    for task in order:
        next(task, None)


def cut(width):
    low = width // 256 * 128
    return ((0, low), (low, width - low))


def column_blocks(ref):
    parts = cut(ref.shape[-1])
    lead = len(ref.shape) - 3

    def blk(half, r):
        start, size = parts[half]
        return ref.at[(slice(None),) * lead + (r, slice(None), pl.ds(start, size))]

    return blk


def own_piece(kit, src_of, dst_of, stage, groups, width):
    first, second = kit.sem(), kit.sem()
    loads = [
        pltpu.make_async_copy(src_of(g), stage.at[:, pl.ds(g * width, width)], kit.sem())
        for g in range(groups)
    ]
    for cp in loads:
        cp.start()
    yield
    for cp in loads:
        cp.wait()
    store = pltpu.make_async_copy(stage, dst_of, first)
    store.start()
    yield
    store.wait()


def column_slice(start, size):
    return pl.ds(pl.multiple_of(start, 128), size)


def reshard(kit, weight, cols, stage, groups):
    n, reps, part, total = cols.shape
    width = total // groups
    rows = pl.ds(pl.multiple_of(kit.rep * part, part), part)

    def source(g, d):
        return weight.at[rows, column_slice(g * (width * n) + d * width, width)]

    def pieces(d):
        return [
            (source(g, d), cols.at[kit.me, kit.rep, :, pl.ds(g * width, width)])
            for g in range(groups)
        ]

    def arrivals(d):
        return [
            (source(g, d), cols.at[d, kit.rep, :, pl.ds(g * width, width)])
            for g in range(groups)
        ]

    own = own_piece(
        kit, lambda g: source(g, kit.me), cols.at[kit.me, kit.rep], stage, groups, width
    )
    move = kit.exchange(pieces, arrivals)
    next(move)
    next(own)
    yield
    next(own)
    next(own, None)
    next(move)
    yield
    finish(move)


def unshard(kit, sums, out, groups, only=None):
    n, part, total = sums.shape
    width = total // groups
    chosen = range(groups) if only is None else (only,)

    def target(g, d):
        return out.at[kit.rep, :, column_slice(g * (width * n) + d * width, width)]

    def pieces(d):
        return [(sums.at[d, :, pl.ds(g * width, width)], target(g, kit.me)) for g in chosen]

    def arrivals(d):
        return [(sums.at[d, :, pl.ds(g * width, width)], target(g, d)) for g in chosen]

    own = [
        pltpu.make_async_copy(src, dst, kit.sem()) for src, dst in pieces(kit.me)
    ]
    for cp in own:
        cp.start()
    move = kit.exchange(pieces, arrivals)
    next(move)
    yield
    for cp in own:
        cp.wait()
    next(move)
    yield
    finish(move)


def call(body, ins, outs, scratch, count, ident, name):
    def spec(space):
        return pl.BlockSpec(memory_space=space)

    return pl.pallas_call(
        body,
        out_shape=[jax.ShapeDtypeStruct(s, d) for s, d, _ in outs],
        in_specs=[spec(space) for _, space in ins],
        out_specs=[spec(space) for _, _, space in outs],
        scratch_shapes=list(scratch) + [pltpu.SemaphoreType.DMA((count,))],
        compiler_params=pltpu.CompilerParams(
            collective_id=ident, has_side_effects=True, vmem_limit_bytes=LIMIT
        ),
        name=name,
    )(*[a for a, _ in ins])


ANY = pl.ANY
VMEM = pltpu.VMEM


def finish_in_turn(tasks):
    tasks = list(tasks)
    done = object()
    while tasks:
        tasks = [t for t in tasks if next(t, done) is not done]


def norm_rows(dst, src):
    def body(at):
        h = src[at]
        centred = h - jnp.mean(h, axis=-1, keepdims=True)
        inv = lax.rsqrt(jnp.mean(centred * centred, axis=-1, keepdims=True) + eps)
        dst[at] = (centred * inv).astype(BF16)

    each(dst, body)


def line_lands(n, rows, width):
    return [VMEM((n // 2, rows, width), BF16), VMEM((n // 2 + 1, rows, width), BF16)]


def lands_of(shape, reps):
    lead, (part, width) = shape[:-3], shape[-2:]
    bits = reps.bit_length() - 1
    places = []
    for start, size in cut(width):
        for i in range(bits):
            places.append(VMEM((1 << (bits - 1 - i),) + lead + (part, size), BF16))
    return places


def land_in(places):
    bits = len(places) // 2

    def land(half, i, j):
        return places[half * bits + i].at[j]

    return land


def put_half(out):
    parts = cut(out.shape[-1])

    def done(half, a, b):
        start, size = parts[half]
        add_into(out.at[(slice(None),) * (len(out.shape) - 1) + (pl.ds(start, size),)], a, b)

    return done


def times_tiles(left, at_rows, right, out, transposed, tile):
    count = out.shape[1] // tile

    def step(t, carry):
        cols = pl.ds(pl.multiple_of(t * tile, tile), tile)
        if transposed:
            value = times_transpose(left[at_rows, :], right[cols, :])
        else:
            value = dot(left[at_rows, :], right[:, cols])
        out[at_rows, cols] = value.astype(BF16)
        return carry

    lax.fori_loop(0, count, step, 0)


def load_all(kit, pairs):
    copies = [pltpu.make_async_copy(src, dst, kit.sem()) for src, dst in pairs]
    for cp in copies:
        cp.start()
    return copies


def wait_all(copies):
    for cp in copies:
        cp.wait()


def project_qkv(n1, cols, cosine, sine, qkv):
    slot, total = qkv.shape
    own = total // 3
    size = 256

    def step(i, carry):
        at = pl.ds(pl.multiple_of(i * size, size), size)
        value = dot(n1[at, :], cols[...])
        for low in range(0, 2 * own, HEAD_DIM):
            part = value[:, low : low + HEAD_DIM]
            turned = part * cosine[at, :] - pltpu.roll(part, HEAD_DIM // 2, 1) * sine[at, :]
            qkv[at, low : low + HEAD_DIM] = turned.astype(BF16)
        qkv[at, 2 * own :] = value[:, 2 * own :].astype(BF16)
        return carry

    lax.fori_loop(0, slot // size, step, 0)


def attend(qkv, length, att, att_low, lse):
    slot, own = att.shape
    heads = own // HEAD_DIM
    size = min(256, slot)
    scale = HEAD_DIM ** (-0.5)
    for i in range(slot // size):
        at = slice(i * size, (i + 1) * size)
        width = (i + 1) * size
        rows = i * size + lax.broadcasted_iota(jnp.int32, (size, width), 0)
        keys = lax.broadcasted_iota(jnp.int32, (size, width), 1)
        allowed = (keys <= rows) & (keys < length)
        for head in range(heads):
            low = head * HEAD_DIM
            q = qkv[at, low : low + HEAD_DIM]
            k = qkv[:width, own + low : own + low + HEAD_DIM]
            v = qkv[:width, 2 * own + low : 2 * own + low + HEAD_DIM]
            scores = jnp.where(allowed, times_transpose(q, k) * scale, neg_big)
            top = jnp.max(scores, axis=-1, keepdims=True)
            level = top + jnp.log(jnp.sum(jnp.exp(scores - top), axis=-1, keepdims=True))
            probs = jnp.exp(scores - level).astype(BF16)
            value = dot(probs, v)
            att[at, low : low + HEAD_DIM] = value
            att_low[at, low : low + HEAD_DIM] = value.astype(BF16)
            lse[at, head:] = jnp.broadcast_to(level, (size, 128 - head))


def front_kernel(sizes, *refs):
    (length, x, cot, w_qkv, w_in, w_out_h, cos_h, sin_h) = refs[:8]
    (hidden, qkv, att, att_low, lse, dy, n1_full, n2_full, qkv_cols, in_cols) = refs[8:18]
    (n_low, n1, cols, w_out, cosine, sine, partial, near, land, stage, stage_in, sems) = refs[18:]
    kit = Kit(sems, sizes)
    rows = x.shape[0]
    loads = load_all(kit, [(w_out_h, w_out), (cos_h, cosine), (sin_h, sine)])

    def widen(at):
        hidden[at] = x[at].astype(F32)

    each(hidden, widen)
    norm_rows(n_low.at[0], hidden)
    kit.barrier()
    move = reshard(kit, w_qkv, qkv_cols, stage, 3)
    next(move)
    line = kit.gather_line(n_low.at[0], n1_full, rows)
    next(line)
    next(move)
    spread = kit.gather_rep(column_blocks(qkv_cols))
    next(spread)

    def mask(at):
        start, size = at[0].start, at[0].size
        place = kit.me * rows + start + lax.broadcasted_iota(jnp.int32, (size, cot.shape[1]), 0)
        dy[at] = jnp.where(place < length[0], cot[at].astype(F32), 0.0).astype(BF16)

    each(dy, mask)
    finish_in_turn([line, spread, move])
    move_in = reshard(kit, w_in, in_cols, stage_in, 2)
    next(move_in)
    n, reps, part, own = qkv_cols.shape
    more = [(n1_full, n1)] + [
        (qkv_cols.at[d, r], cols.at[pl.ds((d * reps + r) * part, part)]) for d in range(n) for r in range(reps)
    ]
    wait_all(loads + load_all(kit, more))
    project_qkv(n1, cols, cosine, sine, qkv)
    attend(qkv, length[0], att, att_low, lse)

    def first(d):
        times_tiles(att_low, pl.ds(d * 2 * rows, 2 * rows), w_out, partial, False, 256)

    total = kit.scatter_line(partial, hidden, rows, near, land, first)
    next(total)
    next(total)
    next(move_in)
    spread_in = kit.gather_rep(column_blocks(in_cols))
    next(spread_in)
    for _ in range(kit.chips - 2):
        next(total)
    next(spread_in)
    next(total)
    next(total)

    def body(at):
        hidden[at] = hidden[at] + x[at].astype(F32)

    each(hidden, body)
    norm_rows(n_low.at[1], hidden)
    gather = kit.gather_line(n_low.at[1], n2_full, rows)
    next(gather)
    for _ in range(kit.chips - 1):
        next(gather)
    finish_in_turn([gather, spread_in, move_in, total])


def front(sizes, length, x, cot, w_qkv, w_in, w_out, cosine, sine):
    n, reps = sizes
    rows, width = x.shape
    slot = n * rows
    depth = w_qkv.shape[0]
    part, own_qkv, own_in = depth // reps, w_qkv.shape[1] // n, w_in.shape[1] // n
    own = w_out.shape[0]
    big = lambda *shape: VMEM(shape, BF16)
    wide = lambda *shape: VMEM(shape, F32)
    outs = call(
        functools.partial(front_kernel, sizes),
        [(length, pltpu.SMEM), (x, VMEM), (cot, VMEM)]
        + [(a, ANY) for a in (w_qkv, w_in, w_out, cosine, sine)],
        [
            ((rows, width), F32, VMEM),
            ((slot, 3 * own), BF16, VMEM),
            ((slot, own), F32, VMEM),
            ((slot, own), BF16, VMEM),
            ((slot, 128), F32, VMEM),
            ((rows, width), BF16, VMEM),
            ((slot, width), BF16, ANY),
            ((slot, width), BF16, ANY),
            ((n, reps, part, own_qkv), BF16, ANY),
            ((n, reps, part, own_in), BF16, ANY),
        ],
        [big(2, rows, width), big(slot, width), big(n * depth, own_qkv), big(own, width)]
        + [wide(slot, 128), wide(slot, 128), big(slot, width)]
        + line_lands(n, rows, width)
        + [big(part, own_qkv), big(part, own_in)],
        64 * n, 1, "front",
    )
    return list(outs[:8]) + [o.reshape(n * depth, -1) for o in outs[8:]]


def gated(n2, cols, at, act, slopes):
    units = act.shape[1]
    tile = 256

    def step(t, carry):
        low = pl.ds(pl.multiple_of(t * tile, tile), tile)
        high = pl.ds(pl.multiple_of(units + t * tile, tile), tile)
        gate = dot(n2[at, :], cols[:, low])
        upper = dot(n2[at, :], cols[:, high])
        sigma = 1.0 / (1.0 + jnp.exp(-gate))
        silu_gate = gate * sigma
        act[at, low] = (silu_gate * upper).astype(BF16)
        slopes[at, low] = (upper * sigma * (1.0 + gate * (1.0 - sigma))).astype(BF16)
        slopes[at, high] = silu_gate.astype(BF16)
        return carry

    lax.fori_loop(0, units // tile, step, 0)


def gated_back(dy, down, at, dgu):
    units = down.shape[0]
    tile = 256

    def step(t, carry):
        low = pl.ds(pl.multiple_of(t * tile, tile), tile)
        high = pl.ds(pl.multiple_of(units + t * tile, tile), tile)
        value = times_transpose(dy[at, :], down[low, :])
        dgu[at, low] = (value * dgu[at, low].astype(F32)).astype(BF16)
        dgu[at, high] = (value * dgu[at, high].astype(F32)).astype(BF16)
        return carry

    lax.fori_loop(0, units // tile, step, 0)


def back_kernel(sizes, *refs):
    (n2_h, cols_h, down_h, hidden, dy) = refs[:5]
    (resid, branch_h, dy_full, full, s_in, s_down) = refs[5:11]
    (n2, cols, down, dy_rows, act, dgu, g_in, g_down, near, land, low) = refs[11:22]
    rest = refs[22:]
    n, reps = sizes
    rows = dy.shape[0]
    bits = reps.bit_length() - 1
    kit = Kit(rest[-1], sizes)
    loads = load_all(kit, [(n2_h, n2), (cols_h, cols)])
    later = load_all(kit, [(down_h, down)])

    def chunk(d):
        return pl.ds(d * 2 * rows, 2 * rows)

    kit.barrier()
    line_dy = kit.gather_line(dy, dy_full, rows)
    next(line_dy)
    wait_all(loads)
    for d in range(kit.chips):
        gated(n2, cols, chunk(d), act, dgu)
        if d > 0:
            next(line_dy)
    finish(line_dy)
    wait_all(later + load_all(kit, [(dy_full, dy_rows)]))
    rows_tiles(act, dy_rows, g_down, 256)
    t_down = kit.scatter_rep(
        column_blocks(g_down.reshape(reps, g_down.shape[0] // reps, g_down.shape[1])),
        land_in(rest[4 * bits : 6 * bits]),
        put_half(s_down),
    )
    next(t_down)

    def first(d):
        gated_back(dy_rows, down, chunk(d), dgu)
        times_tiles(dgu, chunk(d), cols, dy_rows, True, 256)

    total = kit.scatter_line(dy_rows, resid, rows, near, land, first)
    next(total)
    next(total)
    units = act.shape[1]
    blocks = g_in.reshape(n, reps, g_in.shape[0] // (n * reps), 2 * units)
    parts_in = []
    for g in range(2):
        window = pl.ds(g * units, units)
        if g == 0:
            next(t_down)
        rows_tiles(n2, dgu, g_in, 256, window)
        part = kit.scatter_rep(
            column_blocks(blocks.at[:, :, :, window]),
            land_in(rest[2 * g * bits : 2 * (g + 1) * bits]),
            put_half(s_in.at[:, :, window]),
        )
        next(part)
        parts_in.append(part)
        if g == 0:
            next(total)
    next(total)
    for d in range(kit.chips):
        times_tiles(act, chunk(d), down, n2, False, 256)
    for _ in range(kit.chips - 3):
        next(total)
    store = pltpu.make_async_copy(n2, branch_h, kit.sem())
    store.start()
    next(total)

    def body(at):
        h = hidden[at]
        centred = h - jnp.mean(h, axis=-1, keepdims=True)
        inv = lax.rsqrt(jnp.mean(centred * centred, axis=-1, keepdims=True) + eps)
        d = dy[at].astype(F32) + norm_back(centred * inv, inv, resid[at])
        resid[at] = d
        low[at] = d.astype(BF16)

    each(resid, body)
    line = kit.gather_line(low, full, rows)
    next(line)
    next(parts_in[0])
    next(line)
    next(line)
    next(parts_in[1])
    for _ in range(kit.chips - 3):
        next(line)
    finish_in_turn([parts_in[0], t_down, line, parts_in[1], total])
    store.wait()


def back(sizes, n2_full, in_cols, w_down, hidden, dy):
    n, reps = sizes
    rows, width = dy.shape
    units = w_down.shape[0]
    g_in = (n, reps, width // (n * reps), 2 * units)
    g_down = (reps, units // reps, width)
    big = lambda *shape: VMEM(shape, BF16)
    return call(
        functools.partial(back_kernel, sizes),
        [(n2_full, ANY), (in_cols, ANY), (w_down, ANY), (hidden, VMEM), (dy, VMEM)],
        [
            ((rows, width), F32, VMEM),
            ((n * rows, width), BF16, ANY),
            ((n * rows, width), BF16, ANY),
            ((n * rows, width), BF16, ANY),
            ((n,) + g_in[2:], BF16, VMEM),
            (g_down[1:], BF16, VMEM),
        ],
        [big(n * rows, width), big(width, 2 * units), big(units, width), big(n * rows, width)]
        + [big(n * rows, units), big(n * rows, 2 * units), big(width, 2 * units), big(units, width)]
        + line_lands(n, rows, width)
        + [big(rows, width)]
        + lands_of(g_in[:3] + (units,), reps) * 2
        + lands_of(g_down, reps),
        28 * n, 3, "back",
    )


def attend_back(q, k, v, datt, att, lse, length, acc_q, acc_k, acc_v, between):
    slot, own = q.shape
    heads = own // HEAD_DIM
    size = min(256, slot)
    scale = HEAD_DIM ** (-0.5)

    def zero(at):
        for acc in (acc_q, acc_k, acc_v):
            acc[at] = jnp.zeros_like(acc[at])

    each(acc_q, zero)
    for head in range(heads):
        cols = slice(head * HEAD_DIM, (head + 1) * HEAD_DIM)

        def query_block(i, carry):
            at = pl.ds(pl.multiple_of(i * size, size), size)
            qb, db = q[at, cols], datt[at, cols]
            delta = jnp.sum(db.astype(F32) * att[at, cols], axis=-1, keepdims=True)
            level = lse[at, head : head + 1]
            rows = i * size + lax.broadcasted_iota(jnp.int32, (size, size), 0)

            def key_block(j, carry):
                there = pl.ds(pl.multiple_of(j * size, size), size)
                kb, vb = k[there, cols], v[there, cols]
                keys = j * size + lax.broadcasted_iota(jnp.int32, (size, size), 1)
                scores = times_transpose(qb, kb) * scale
                scores = jnp.where((keys <= rows) & (keys < length), scores, neg_big)
                probs = jnp.exp(scores - level)
                grads = (probs * (times_transpose(db, vb) - delta)).astype(BF16)
                acc_v[there, cols] = acc_v[there, cols] + over_rows(probs.astype(BF16), db)
                acc_k[there, cols] = acc_k[there, cols] + over_rows(grads, qb)
                acc_q[at, cols] = acc_q[at, cols] + dot(grads, kb)
                return carry

            return lax.fori_loop(0, i + 1, key_block, carry)

        lax.fori_loop(0, slot // size, query_block, 0)
        between(head)


def turn_back(acc, cosine, sine, out, start):
    slot, own = acc.shape
    scale = HEAD_DIM ** (-0.5)
    size = 128

    def step(i, carry):
        at = pl.ds(pl.multiple_of(i * size, size), size)
        for head in range(own // HEAD_DIM):
            low = head * HEAD_DIM
            value = acc[at, low : low + HEAD_DIM] * scale
            turned = value * cosine[at, :] + pltpu.roll(value, HEAD_DIM // 2, 1) * sine[at, :]
            out[at, start + low : start + low + HEAD_DIM] = turned.astype(BF16)
        return carry

    lax.fori_loop(0, slot // size, step, 0)


def rows_tiles(left, right, out, tile, window=slice(None)):
    def step(t, carry):
        cols = pl.ds(pl.multiple_of(t * tile, tile), tile)
        out[cols, window] = over_rows(left[:, cols], right[:, window]).astype(BF16)
        return carry

    lax.fori_loop(0, left.shape[1] // tile, step, 0)


def end_kernel(sizes, *refs):
    n, reps = sizes
    bits = reps.bit_length() - 1
    (length, dres_h, w_out_h, q_h, att_h, low_h, lse_h, cos_h, sin_h, cols_h, n1_h, part_h, s_in, s_down) = refs[:14]
    total_out, branch, o_in, o_down, o_qkv, o_out = refs[14:20]
    (dres, w_out, q, k, v, att, att_low, lse, cosine, sine, cols, n1, datt, acc_q, acc_k, acc_v, dqkv, g_qkv, g_out, dn1, near, land, near_b, land_b, stage, s_qkv, s_out) = refs[20:47]
    rest = refs[47:]
    rows = total_out.shape[0]
    own = q.shape[1]
    kit = Kit(rest[-1], sizes)
    loads = load_all(
        kit,
        [(dres_h, dres), (w_out_h, w_out)]
        + [(q_h.at[:, pl.ds(i * own, own)], ref) for i, ref in enumerate((q, k, v))]
        + [(att_h, att), (lse_h, lse)],
    )
    later = load_all(
        kit, [(low_h, att_low), (cos_h, cosine), (sin_h, sine), (cols_h, cols), (n1_h, n1)]
    )
    own_down = pltpu.make_async_copy(s_down, o_down.at[kit.rep], kit.sem())
    own_down.start()
    kit.barrier()
    moves_in = [unshard(kit, s_in, o_in, 2, g) for g in range(2)]
    for move in moves_in:
        next(move)
    own_down.wait()
    spread_down = kit.gather_rep(column_blocks(o_down))
    next(spread_down)
    wait_all(loads)

    def project(i, carry):
        at = pl.ds(pl.multiple_of(i * 2 * rows, 2 * rows), 2 * rows)
        datt[at, :] = times_transpose(dres[at, :], w_out[...]).astype(BF16)
        return carry

    lax.fori_loop(0, kit.chips, project, 0)
    def between(head):
        if head == 0:
            next(spread_down)

    attend_back(q, k, v, datt, att, lse, length[0], acc_q, acc_k, acc_v, between)
    wait_all(later)
    turn_back(acc_q, cosine, sine, dqkv, 0)
    turn_back(acc_k, cosine, sine, dqkv, own)

    def place(at):
        dqkv[at + (pl.ds(2 * own, own),)] = acc_v[at].astype(BF16)

    each(acc_v, place)
    rows_tiles(n1, dqkv, g_qkv, 256)
    parts = g_qkv.shape[0] // (n * reps)
    t_qkv = kit.scatter_rep(
        column_blocks(g_qkv.reshape(n, reps, parts, 3 * own)), land_in(rest[: 2 * bits]), put_half(s_qkv)
    )
    next(t_qkv)

    def first(d):
        times_tiles(dqkv, pl.ds(d * 2 * rows, 2 * rows), cols, dn1, True, 256)

    total = kit.scatter_line(dn1, total_out, rows, near, land, first)
    next(total)
    next(total)
    rows_tiles(att_low, dres, g_out, 128)
    t_out = kit.scatter_rep(
        column_blocks(g_out.reshape(reps, g_out.shape[0] // reps, g_out.shape[1])),
        land_in(rest[2 * bits : 4 * bits]),
        put_half(s_out),
    )
    next(t_out)
    next(total)
    next(t_qkv)
    next(t_out)
    units = o_in.shape[2] // 2
    spreads = []
    for g in range(2):
        next(moves_in[g])
        spread = kit.gather_rep(column_blocks(o_in.at[:, :, pl.ds(g * units, units)]))
        next(spread)
        spreads.append(spread)
    next(total)
    for _ in range(bits - 1):
        next(t_qkv)
    move_qkv = unshard(kit, s_qkv, o_qkv, 3)
    next(move_qkv)
    for _ in range(bits - 1):
        next(t_out)
    own_out = pltpu.make_async_copy(s_out, o_out.at[kit.rep], kit.sem())
    own_out.start()
    for _ in range(kit.chips - 3):
        next(total)
    other = kit.scatter_line(part_h, branch, rows, near_b, land_b, stage=stage)
    next(other)
    next(total)
    next(spreads[0])
    next(other)
    own_out.wait()
    next(move_qkv)
    spread_qkv = kit.gather_rep(column_blocks(o_qkv))
    next(spread_qkv)
    spread_out = kit.gather_rep(column_blocks(o_out))
    next(spread_out)
    next(spreads[1])
    for _ in range(kit.chips):
        next(other)
    finish_in_turn(
        [spread_qkv, spread_out, other, total, spread_down]
        + spreads + moves_in + [move_qkv, t_qkv, t_out]
    )


def end(sizes, length, dres, w_out, qkv, att, att_low, lse, cosine, sine, cols, n1, part, s_in, s_down):
    n, reps = sizes
    slot, width = dres.shape
    rows, own = slot // n, w_out.shape[0]
    g_qkv = (n, reps, width // (n * reps), 3 * own)
    g_out = (reps, own // reps, width)
    big = lambda *shape: VMEM(shape, BF16)
    wide = lambda *shape: VMEM(shape, F32)
    any_of = [(a, ANY) for a in (dres, w_out, qkv, att, att_low, lse, cosine, sine, cols, n1, part)]
    total, branch, o_in, o_down, o_qkv, o_out = call(
        functools.partial(end_kernel, sizes),
        [(length, pltpu.SMEM)] + any_of + [(s_in, VMEM), (s_down, VMEM)],
        [
            ((rows, width), F32, VMEM),
            ((rows, width), F32, VMEM),
            ((reps, s_in.shape[1], n * s_in.shape[2]), BF16, ANY),
            ((reps,) + s_down.shape, BF16, ANY),
            ((reps, g_qkv[2], n * g_qkv[3]), BF16, ANY),
            (g_out, BF16, ANY),
        ],
        [big(slot, width), big(own, width), big(slot, own), big(slot, own), big(slot, own)]
        + [wide(slot, own), big(slot, own), wide(slot, 128), wide(slot, 128), wide(slot, 128)]
        + [big(width, 3 * own), big(slot, width), big(slot, own)]
        + [wide(slot, own)] * 3
        + [big(slot, 3 * own), big(width, 3 * own), big(own, width), big(slot, width)]
        + line_lands(n, rows, width) * 2
        + [big(rows, width), big(n, g_qkv[2], 3 * own), big(*g_out[1:])]
        + lands_of(g_qkv, reps)
        + lands_of(g_out, reps),
        32 * n, 4, "end",
    )
    return [total, branch] + [o.reshape(-1, o.shape[-1]).astype(F32) for o in (o_in, o_down, o_qkv, o_out)]


def on_device(tokens, lengths, cotangent, w_qkv, w_out, w_in, w_down):
    rows = tokens.shape[1]
    width = tokens.shape[2]
    n = lax.axis_size("fsdp")
    slot_len = rows * n
    head_dim = HEAD_DIM
    length = lengths[0]
    own_positions = lax.axis_index("fsdp") * rows + jnp.arange(rows, dtype=jnp.int32)
    valid = (own_positions < length).astype(F32)[:, None]
    positions = jnp.arange(slot_len, dtype=jnp.int32)
    cosine, sine = rotary_tables(positions, head_dim)

    sizes = (n, lax.axis_size("rep"))
    turn_cos = jnp.concatenate([cosine, cosine], axis=1)
    turn_sin = jnp.concatenate([sine, -sine], axis=1)
    hidden_in, qkv_low, attended, att_low, level, dy_low, n1_full, n2_full, qkv_cols, in_cols = front(
        sizes, lengths, tokens[0], cotangent[0], w_qkv, w_in, w_out, turn_cos, turn_sin
    )
    d_resid, branch_partial, _, dres_full, sum_in, sum_down = back(
        sizes, n2_full, in_cols, w_down, hidden_in, dy_low
    )
    d_norm1, branch, all_in, all_down, all_qkv, all_out = end(
        sizes,
        lengths,
        dres_full,
        w_out,
        qkv_low,
        attended,
        att_low,
        level,
        turn_cos,
        turn_sin,
        qkv_cols,
        n1_full,
        branch_partial,
        sum_in,
        sum_down,
    )
    output = (valid * (hidden_in + branch)).astype(BF16)
    normed1, inv1 = normalize(tokens[0].astype(F32))
    grad_tokens = (d_resid + norm_back(normed1, inv1, d_norm1)).astype(BF16)
    return (output[None], grad_tokens[None], all_qkv, all_out, all_in, all_down)


def solution(mesh):
    in_specs = (
        P("rep", "fsdp", None),
        P("rep"),
        P("rep", "fsdp", None),
        P("fsdp", None),
        P("fsdp", None),
        P("fsdp", None),
        P("fsdp", None),
    )
    out_specs = (
        P("rep", "fsdp", None),
        P("rep", "fsdp", None),
        P("fsdp", None),
        P("fsdp", None),
        P("fsdp", None),
        P("fsdp", None),
    )
    return jax.shard_map(
        on_device, mesh=mesh, in_specs=in_specs, out_specs=out_specs, check_vma=False
    )
```
